32 devices in a mesh: dp: 8 (over z, x), seq: 4 (over y, core).
Axes of the slice: x: 2, y: 2, z: 4, core: 2. Of those that a mesh axis runs over, the one named last changes fastest.
Arguments:
- hidden_in: bfloat16 [16384, 512], P(('dp', 'seq')), may hold values from -6 to 6
- memory: bfloat16 [8192, 512], P(('dp', 'seq')), may hold values from -6 to 6
- lengths: int32 [8], P('dp'), may hold values from 512 to 2048, as said below
- memory_lengths: int32 [8], P('dp'), may hold values from 256 to 1024, as said below
- self_in: bfloat16 [512, 1536], P('dp'), may hold values from -0.25 to 0.25
- self_out: bfloat16 [512, 512], P('dp'), may hold values from -1.5 to 1.5
- cross_query: bfloat16 [512, 512], P('dp'), may hold values from -0.25 to 0.25
- cross_memory: bfloat16 [512, 1024], P('dp'), may hold values from -0.25 to 0.25
- cross_out: bfloat16 [512, 512], P('dp'), may hold values from -1 to 1
- ffn_in: bfloat16 [512, 2048], P('dp'), may hold values from -0.25 to 0.25
- ffn_bias: bfloat16 [2048], P('dp'), may hold values from -3 to 3
- ffn_out: bfloat16 [2048, 512], P('dp'), may hold values from -0.125 to 0.125
- out_bias: bfloat16 [512], P('dp'), may hold values from -2 to 2
- gain_self: bfloat16 [512], P('dp'), may hold values from 0.099609375 to 1.8984375
- shift_self: bfloat16 [512], P('dp'), may hold values from -2 to 2
- gain_cross: bfloat16 [512], P('dp'), may hold values from 0.099609375 to 1.8984375
- shift_cross: bfloat16 [512], P('dp'), may hold values from -2 to 2
- gain_ffn: bfloat16 [512], P('dp'), may hold values from 0.099609375 to 1.8984375
- shift_ffn: bfloat16 [512], P('dp'), may hold values from -2 to 2
- exit_weight: bfloat16 [512], P('dp'), may hold values from -0.25 to 0.25
- grad_result: bfloat16 [16384, 512], P(('dp', 'seq')), may hold values from -6 to 6
- grad_halting: float32 [16384], P(('dp', 'seq')), may hold values from -6 to 6
Outputs:
- result: bfloat16 [16384, 512], P(('dp', 'seq'))
- halting: float32 [16384], P(('dp', 'seq'))
- grad_hidden: float32 [16384, 512], P(('dp', 'seq'))
- grad_memory: float32 [8192, 512], P(('dp', 'seq'))
- grad_self_in: float32 [512, 1536], P('dp')
- grad_self_out: float32 [512, 512], P('dp')
- grad_cross_query: float32 [512, 512], P('dp')
- grad_cross_memory: float32 [512, 1024], P('dp')
- grad_cross_out: float32 [512, 512], P('dp')
- grad_ffn_in: float32 [512, 2048], P('dp')
- grad_ffn_bias: float32 [2048], P('dp')
- grad_ffn_out: float32 [2048, 512], P('dp')
- grad_out_bias: float32 [512], P('dp')
- grad_gain_self: float32 [512], P('dp')
- grad_shift_self: float32 [512], P('dp')
- grad_gain_cross: float32 [512], P('dp')
- grad_shift_cross: float32 [512], P('dp')
- grad_gain_ffn: float32 [512], P('dp')
- grad_shift_ffn: float32 [512], P('dp')
- grad_exit_weight: float32 [512], P('dp')
The draws below stay inside these ranges and needn't reach their ends.
Inputs may be any that keep to these rules, and one draw needn't show every extreme that they name: Positions from lengths[s] to 2047 of sequence s are padding; some sequence has exactly 2048 valid positions in every draw. Memory positions from memory_lengths[s] on are padding; some sequence has exactly 1024 in every draw.
All inputs are finite; a program needn't handle non-finite values.
Results may differ from the reference program's by a relative error of at most 0.02.
The reference program's roundings to bfloat16 on the way count: a program that leaves them out, or rounds other values in their place, can miss the bound.
Values may be sent and summed in bfloat16 or wider, within the bound.
A program may use at most 128 MiB of HBM per device.

```python
import jax
import jax.numpy as jnp
from jax import lax

D = 512
H = 8
HD = 64
FF = 2048
MEM = 1024
SEQ_LEN = 2048
SEQS = 8
TOKENS = 16384
MEMORY_ROWS = 8192


def ragged_counts(key, number, largest):
    head_key, tail_key = jax.random.split(key)
    values = jax.random.randint(head_key, (number,), largest // 4, largest + 1)
    chosen = jax.random.randint(tail_key, (), 0, number)
    return jnp.where(jnp.arange(number) == chosen, largest, values).astype(jnp.int32)


def draw_lengths(key, part):
    return ragged_counts(jax.random.fold_in(key, 11), SEQS, SEQ_LEN)


def draw_memory_lengths(key, part):
    return ragged_counts(jax.random.fold_in(key, 23), SEQS, MEM)


def strengthened(values, key, source, target, parts, factor):
    owner, partner = [(jnp.arange(values.shape[position]) // (values.shape[position] // parts)).reshape([-1 if axis == position else 1 for axis in range(values.ndim)]) for position in (source, target)]
    chosen = jax.random.permutation(key, parts)[partner]
    strong = (owner == chosen) | (owner == (partner + parts // 2) % parts)
    return jnp.where(strong, factor * values, values)


def shard_levels(stream_key, extent, cuts, least, high):
    level = 1.0
    for dim, blocks in cuts:
        heights = jax.random.uniform(jax.random.fold_in(jax.random.fold_in(stream_key, 6), dim), (blocks,), jnp.float32, least / len(cuts), high / len(cuts))
        level = level * jnp.repeat(jnp.exp(heights), extent[dim] // blocks).reshape((-1,) + (1,) * (len(extent) - 1 - dim))
    return level


def bell_draw(key, shape, spread, bound, pieces=(), kind=jnp.bfloat16):
    level = shard_levels(key, shape, pieces, -0.22, 0.18) if pieces else 1.0
    values = jax.random.normal(key, shape, jnp.float32) * spread * level
    return jnp.minimum(jnp.maximum(values, -bound), bound).astype(kind)


def heavy_noise(key, extent, width, most, cuts, heavy, held_as=jnp.bfloat16):
    array = width * jax.random.normal(key, extent, jnp.float32)
    if cuts:
        array = array * shard_levels(key, extent, cuts, -0.22, 0.18)
    return jnp.clip(strengthened(array, jax.random.fold_in(key, 3), *heavy), -most, most).astype(held_as)


def setup_inputs(seed: int = 0) -> dict:
    splits = jax.random.split(jax.random.key(seed), 23)
    return {
        "hidden_in": bell_draw(splits[0], (TOKENS, D), 1.0, 6.0, ((0, 32),)),
        "memory": bell_draw(splits[1], (MEMORY_ROWS, D), 1.0, 6.0, ((0, 32),)),
        "lengths": draw_lengths(jax.random.fold_in(splits[22], 71), 0),
        "memory_lengths": draw_memory_lengths(jax.random.fold_in(splits[22], 71), 0),
        "self_in": bell_draw(splits[4], (D, 3 * D), D ** -0.5, 0.25, ((0, 8),)),
        "self_out": bell_draw(splits[5], (D, D), (max(1, D * 64 // SEQ_LEN)) ** -0.5, 1.5, ((0, 8),)),
        "cross_query": bell_draw(splits[6], (D, D), D ** -0.5, 0.25, ((0, 8),)),
        "cross_memory": bell_draw(splits[7], (D, 2 * D), D ** -0.5, 0.25, ((0, 8),)),
        "cross_out": bell_draw(splits[8], (D, D), (max(1, D * 64 // MEM)) ** -0.5, 1.0, ((0, 8),)),
        "ffn_in": bell_draw(splits[9], (D, FF), D ** -0.5, 0.25, ((0, 8),)),
        "ffn_bias": bell_draw(splits[10], (FF,), 0.5, 3.0, ((0, 8),)),
        "ffn_out": bell_draw(splits[11], (FF, D), FF ** -0.5, 0.125, ((0, 8),)),
        "out_bias": bell_draw(splits[12], (D,), 0.3, 2.0, ((0, 8),)),
        "gain_self": jnp.clip(1.0 + 0.18 * jax.random.normal(splits[13], (D,), jnp.float32), 0.099609375, 1.8984375).astype(jnp.bfloat16),
        "shift_self": bell_draw(splits[14], (D,), 0.3, 2.0, ((0, 8),)),
        "gain_cross": jnp.clip(1.0 + 0.18 * jax.random.normal(splits[15], (D,), jnp.float32), 0.099609375, 1.8984375).astype(jnp.bfloat16),
        "shift_cross": bell_draw(splits[16], (D,), 0.3, 2.0, ((0, 8),)),
        "gain_ffn": jnp.clip(1.0 + 0.18 * jax.random.normal(splits[17], (D,), jnp.float32), 0.099609375, 1.8984375).astype(jnp.bfloat16),
        "shift_ffn": bell_draw(splits[18], (D,), 0.3, 2.0, ((0, 8),)),
        "exit_weight": bell_draw(splits[19], (D,), D ** -0.5, 0.25, ((0, 8),)),
        "grad_result": heavy_noise(splits[20], (TOKENS, D), 1.0, 6.0, ((0, 32),), (0, 1, 32, 2.75)),
        "grad_halting": bell_draw(splits[21], (TOKENS,), 1.0, 6.0, ((0, 32),), jnp.float32),
    }


@jax.custom_vjp
def low(v):
    return lax.optimization_barrier(v.astype(jnp.bfloat16)).astype(jnp.float32)

@jax.custom_vjp
def low_back(v):
    return v

def low_keep(v):
    return (low(v), None)

def low_pass(kept, grad):
    return (grad,)

def back_keep(v):
    return (v, None)

def back_low(kept, grad):
    return (low(grad),)
low.defvjp(low_keep, low_pass)
low_back.defvjp(back_keep, back_low)
epsilon = 1e-05
masked_score = -1e+30
gelu_scale = 0.7978845608028654
gelu_cubic = 0.044715

def product(left, right):
    return jnp.dot(left, right, precision=lax.Precision.HIGHEST)

def smooth_gate(value):
    return 0.5 * value * (1.0 + jnp.tanh(gelu_scale * (value + gelu_cubic * value * value * value)))

def layer_norm(value, gain, shift):
    average = lax.optimization_barrier(jnp.mean(value, axis=-1, keepdims=True))
    centred = value - average
    variance = lax.optimization_barrier(jnp.mean(centred * centred, axis=-1, keepdims=True))
    return centred * lax.rsqrt(variance + epsilon) * gain + shift

def attend(queries, keys_in, values_in, key_limit, causal):
    query_rows = queries.shape[0]
    key_rows = keys_in.shape[0]
    block_rows = min(512, query_rows)
    blocks = query_rows // block_rows
    score_scale = HD ** (-0.5)
    key_heads = keys_in.reshape(key_rows, H, HD)
    value_heads = values_in.reshape(key_rows, H, HD)
    key_place = jnp.arange(key_rows, dtype=jnp.int32)
    limit_value = jnp.asarray(key_limit).astype(jnp.int32)
    query_blocks = queries.reshape(blocks, block_rows, H, HD)
    first_rows = (jnp.arange(blocks, dtype=jnp.int32) * block_rows).astype(jnp.int32)

    def one_block(block_pair):
        query_block, first_row = block_pair
        scores = low_back(jnp.einsum('qhd,khd->hqk', query_block, key_heads, precision=lax.Precision.HIGHEST) * score_scale)
        allowed = key_place[None, :] < limit_value
        if causal:
            row_place = (first_row.astype(jnp.int32) + jnp.arange(block_rows, dtype=jnp.int32)).astype(jnp.int32)
            allowed = allowed & (key_place[None, :] <= row_place[:, None])
        scores = jnp.where(allowed[None], scores, jnp.asarray(masked_score, dtype=jnp.float32))
        largest = lax.optimization_barrier(jnp.max(scores, axis=-1, keepdims=True))
        powers = jnp.exp(scores - largest)
        weights = low(powers / lax.optimization_barrier(jnp.sum(powers, axis=-1, keepdims=True)))
        attended = jnp.einsum('hqk,khd->qhd', weights, value_heads, precision=lax.Precision.HIGHEST)
        return attended.reshape(block_rows, H * HD)
    return lax.map(jax.checkpoint(one_block), (query_blocks, first_rows)).reshape(query_rows, H * HD)

def layer(params, hidden, memory_rows, length, memory_length):
    self_in, self_out, cross_query, cross_memory, cross_out, ffn_in, ffn_bias, ffn_out, out_bias, gain_self, shift_self, gain_cross, shift_cross, gain_ffn, shift_ffn, exit_weight = params
    normed = low(layer_norm(hidden, gain_self, shift_self))
    packed = low(low_back(product(normed, self_in)))
    memory_pair = low(low_back(product(memory_rows, cross_memory)))
    attended = low(low_back(attend(packed[:, :D], packed[:, D:2 * D], packed[:, 2 * D:], length, True)))
    after_self = hidden + low_back(product(attended, self_out))
    normed_cross = low(layer_norm(after_self, gain_cross, shift_cross))
    cross_queries = low(low_back(product(normed_cross, cross_query)))
    cross_mixed = low(low_back(attend(cross_queries, memory_pair[:, :D], memory_pair[:, D:], memory_length, False)))
    after_cross = after_self + low_back(product(cross_mixed, cross_out))
    normed_ffn = low(layer_norm(after_cross, gain_ffn, shift_ffn))
    inner_pre = low_back(product(normed_ffn, ffn_in) + ffn_bias)
    active = low(smooth_gate(inner_pre))
    output = after_cross + low_back(product(active, ffn_out) + out_bias)
    halting = jax.nn.sigmoid(product(output, exit_weight))
    return (output, halting)

def reference(hidden_in, memory, lengths, memory_lengths, self_in, self_out, cross_query, cross_memory, cross_out, ffn_in, ffn_bias, ffn_out, out_bias, gain_self, shift_self, gain_cross, shift_cross, gain_ffn, shift_ffn, exit_weight, grad_result, grad_halting):
    params = tuple((weight_arg.astype(jnp.float32) for weight_arg in (self_in, self_out, cross_query, cross_memory, cross_out, ffn_in, ffn_bias, ffn_out, out_bias, gain_self, shift_self, gain_cross, shift_cross, gain_ffn, shift_ffn, exit_weight)))
    hidden_seqs = hidden_in.astype(jnp.float32).reshape(SEQS, SEQ_LEN, D)
    memory_seqs = memory.astype(jnp.float32).reshape(SEQS, MEM, D)
    result_seqs = grad_result.astype(jnp.float32).reshape(SEQS, SEQ_LEN, D)
    halting_seqs = grad_halting.astype(jnp.float32).reshape(SEQS, SEQ_LEN)
    length_items = lengths.astype(jnp.int32)
    memory_items = memory_lengths.astype(jnp.int32)
    running = tuple((jnp.zeros(weight_arg.shape, jnp.float32) for weight_arg in params))

    def one_sequence(running, seq_items):
        hidden_seq, memory_seq, length, memory_length, grad_out, grad_halt = seq_items
        live_rows = (jnp.arange(SEQ_LEN, dtype=jnp.int32) < length.astype(jnp.int32)).astype(jnp.float32)

        def forward(weights, hidden, memory_rows):
            return layer(weights, hidden, memory_rows, length, memory_length)
        (output, halting), pullback = jax.vjp(forward, params, hidden_seq, memory_seq)
        grad_weights, grad_hidden, grad_memory = pullback(((grad_out * live_rows[:, None]).astype(output.dtype), (grad_halt * live_rows).astype(halting.dtype)))
        running = jax.tree.map(lambda total, term: total + term.astype(jnp.float32), running, grad_weights)
        return (running, (output.astype(jnp.bfloat16), halting.astype(jnp.float32), grad_hidden.astype(jnp.float32), grad_memory.astype(jnp.float32)))
    running, (outputs, haltings, grads_hidden, grads_memory) = lax.scan(one_sequence, running, (hidden_seqs, memory_seqs, length_items, memory_items, result_seqs, halting_seqs))
    return (outputs.reshape(TOKENS, D), haltings.reshape(TOKENS), grads_hidden.reshape(TOKENS, D), grads_memory.reshape(MEMORY_ROWS, D), running[0], running[1], running[2], running[3], running[4], running[5], running[6], running[7], running[8], running[9], running[10], running[11], running[12], running[13], running[14], running[15])
```

```python
import functools
import jax
import jax.numpy as jnp
from jax import lax
from jax.experimental import pallas as pl
from jax.experimental.pallas import tpu as pltpu
from jax.sharding import PartitionSpec as P

bf16 = jnp.bfloat16
f32 = jnp.float32
i32 = jnp.int32
MESH = pl.DeviceIdType.MESH
HD = 64
LANES = 128
epsilon = 1e-05
masked_score = -1e30
gelu_scale = 0.7978845608028654
gelu_cubic = 0.044715
log2_e = 1.4426950408889634


def nn(left, right):
    return jnp.dot(left, right, preferred_element_type=f32)


def nt(left, right, precision=None):
    return lax.dot_general(
        left, right, (((1,), (1,)), ((), ())), preferred_element_type=f32, precision=precision
    )


def tn(left, right):
    return lax.dot_general(
        left, right, (((0,), (0,)), ((), ())), preferred_element_type=f32
    )


def many(count, step):
    if count <= 8:
        for index in range(count):
            step(index)
    else:
        lax.fori_loop(0, count, lambda index, carry: (step(index), carry)[1], 0)


def tiles(rows, size, step):
    lax.fori_loop(0, rows // size, lambda index, carry: (step(pl.ds(pl.multiple_of(index * size, size), size)), carry)[1], 0)


def unit_rows(value):
    average = jnp.mean(value, axis=-1, keepdims=True)
    centred = value - average
    variance = jnp.mean(centred * centred, axis=-1, keepdims=True)
    inverse = lax.rsqrt(variance + epsilon)
    return centred * inverse, inverse


def head_mask(head):
    lane = lax.broadcasted_iota(i32, (1, LANES), 1)
    return (lane < HD) == (head == 0)


def pick(value, mask):
    return jnp.where(mask, value, jnp.zeros_like(value))


def forward_kernel(sizes, *refs):
    dp, sq, rows, mem_rows, width, inner = sizes
    high = dp // 2
    strip = width // dp
    seq_rows = rows * sq
    all_mem = mem_rows * sq
    (len_ref, mlen_ref, hidden_ref, memory_ref, vec_ref, self_in_ref, cross_memory_ref, self_out_ref,
     cross_query_ref, cross_out_ref, ffn_in_ref, ffn_out_ref,
     w_cm, w_so, w_cq, w_co, w_fi, w_fo, vec_full, bias_full, after_self, after_cross, normed_two, cross_q,
     mixed, mem_pair, cross_lse, att_tok, q_all, k_all, v_all, self_lse,
     w_in, hid_all, mem_all, vec_all, normed_all, o_heads,
     loc_sem, hid_s, hid_r, mem_s, mem_r, vec_s, vec_r, in_s, in_r, z_s, z_r, x_s, x_r, c_s, c_r, a_s, a_r) = refs
    me_dp = lax.axis_index("dp")
    me_sq = lax.axis_index("seq")
    me_hi = me_dp // 2
    me_lo = me_dp % 2
    half = me_sq % 2
    pair = me_sq + 1 - 2 * half
    far = (me_sq + 2) % sq
    cross = (pair + 2) % sq
    shards = (cross_memory_ref, self_out_ref, cross_query_ref, cross_out_ref, ffn_in_ref, ffn_out_ref)
    wholes = (w_cm, w_so, w_cq, w_co, w_fi, w_fo)

    def remote(src, dst, send, recv, device):
        return pltpu.make_async_remote_copy(src_ref=src, dst_ref=dst, send_sem=send, recv_sem=recv, device_id=device, device_id_type=MESH)

    def other_dp(step):
        return (me_dp + 1 + step) % dp

    barrier = pltpu.get_barrier_semaphore()
    many(dp - 1, lambda k: pl.semaphore_signal(barrier, inc=1, device_id=(other_dp(k), me_sq), device_id_type=MESH))
    for peer in (pair, far, cross):
        pl.semaphore_signal(barrier, inc=1, device_id=(me_dp, peer), device_id_type=MESH)
    pl.semaphore_wait(barrier, dp - 1 + 3)

    def slab_copy(src, dst_all, slab, send, recv, peer):
        return remote(src, dst_all.at[slab], send, recv.at[slab], (me_dp, peer))

    own_hidden = pltpu.make_async_copy(hidden_ref, hid_all.at[me_sq], loc_sem.at[0])
    own_memory = pltpu.make_async_copy(memory_ref, mem_all.at[me_sq], loc_sem.at[1])
    hid_far = slab_copy(hidden_ref, hid_all, me_sq, hid_s.at[1], hid_r, far)
    hid_pair = slab_copy(hidden_ref, hid_all, me_sq, hid_s.at[0], hid_r, pair)
    mem_far = slab_copy(memory_ref, mem_all, me_sq, mem_s.at[1], mem_r, far)
    mem_pair_copy = slab_copy(memory_ref, mem_all, me_sq, mem_s.at[0], mem_r, pair)
    hid_next = slab_copy(hid_all.at[far], hid_all, far, hid_s.at[2], hid_r, pair)
    mem_next = slab_copy(mem_all.at[far], mem_all, far, mem_s.at[2], mem_r, pair)

    def vec_copy(peer, slot):
        return remote(vec_ref, vec_all.at[slot], vec_s.at[peer], vec_r.at[slot], (peer, me_sq))

    def in_copy(part, peer, slot):
        return remote(
            self_in_ref.at[:, pl.ds(pl.multiple_of(part * width + me_sq * LANES, LANES), LANES)],
            w_in.at[pl.ds(pl.multiple_of(slot * strip, strip), strip), pl.ds(part * LANES, LANES)],
            in_s.at[part, peer], in_r.at[part, slot], (peer, me_sq))

    own_vec = pltpu.make_async_copy(vec_ref, vec_all.at[me_dp], loc_sem.at[2])
    own_in = [pltpu.make_async_copy(
        self_in_ref.at[:, pl.ds(pl.multiple_of(part * width + me_sq * LANES, LANES), LANES)],
        w_in.at[pl.ds(pl.multiple_of(me_dp * strip, strip), strip), pl.ds(part * LANES, LANES)],
        loc_sem.at[3 + part]) for part in range(3)]

    hid_far.start()
    hid_pair.start()
    many(dp - 1, lambda k: vec_copy(other_dp(k), me_dp).start())
    many(dp - 1, lambda k: [in_copy(part, other_dp(k), me_dp).start() for part in range(3)])
    own_hidden.start()
    own_memory.start()
    own_vec.start()
    for copy in own_in:
        copy.start()
    mem_far.start()
    mem_pair_copy.start()

    def columns(index):
        size = shards[index].shape[1] // 2
        return pl.ds(pl.multiple_of(half * size, LANES), size)

    def block_rows(index, slot):
        size = shards[index].shape[0]
        return pl.ds(pl.multiple_of(slot * size, size), size)

    def z_copy(index, peer, slot):
        return remote(shards[index].at[:, columns(index)], wholes[index].at[block_rows(index, slot * 2 + me_lo), columns(index)],
                      z_s.at[index, peer], z_r.at[index, slot], (peer * 2 + me_lo, me_sq))

    def x_copy(index, slot, low, own):
        there = wholes[index].at[block_rows(index, slot * 2 + low), columns(index)]
        src = shards[index].at[:, columns(index)] if own else there
        return remote(src, there, x_s.at[index, slot], x_r.at[index, slot], (me_hi * 2 + 1 - me_lo, me_sq))

    def c_copy(index):
        there = wholes[index].at[:, columns(index)]
        return remote(there, there, c_s.at[index], c_r.at[index], (me_dp, pair))

    def c_wait(index):
        size = shards[index].shape[1] // 2
        there = wholes[index].at[:, pl.ds(pl.multiple_of((1 - half) * size, LANES), size)]
        remote(there, there, c_s.at[index], c_r.at[index], (me_dp, pair)).wait_recv()

    def own_copy(index):
        return pltpu.make_async_copy(shards[index].at[:, columns(index)], wholes[index].at[block_rows(index, me_dp), columns(index)], loc_sem.at[6 + index])

    def other_hi(step):
        return (me_hi + 1 + step) % high

    def first_stage(index):
        many(high - 1, lambda k: z_copy(index, other_hi(k), me_hi).start())
        x_copy(index, me_hi, me_lo, True).start()
        own_copy(index).start()

    def second_stage(index):
        def forward(k):
            z_copy(index, other_hi(k), other_hi(k)).wait_recv()
            x_copy(index, other_hi(k), me_lo, False).start()
        many(high - 1, forward)

    def third_stage(index):
        many(high, lambda k: x_copy(index, k, 1 - me_lo, False).wait_recv())
        own_copy(index).wait()
        c_copy(index).start()

    def finish_weight(index):
        many(high - 1, lambda k: z_copy(index, other_hi(k), me_hi).wait_send())
        many(high, lambda k: x_copy(index, k, me_lo, False).wait_send())
        c_copy(index).wait_send()

    for index in range(6):
        first_stage(index)

    own_vec.wait()
    many(dp - 1, lambda k: vec_copy(other_dp(k), other_dp(k)).wait_recv())
    vec_full[...] = jnp.zeros_like(vec_full)
    bias_full[...] = jnp.zeros_like(bias_full)
    lane_k = lax.broadcasted_iota(i32, (LANES, width), 0)
    lane_j = lax.broadcasted_iota(i32, (LANES, width), 1)
    big = inner // dp
    piece = min(big, LANES)
    big_k = lax.broadcasted_iota(i32, (LANES, inner), 0)
    big_j = lax.broadcasted_iota(i32, (LANES, inner), 1)

    def place(slot):
        hot = ((lane_j - slot * strip == lane_k) & (lane_k < strip)).astype(f32).astype(bf16)
        vec_full[...] = vec_full[...] + nn(vec_all[slot], hot)[:8]
        for part in range(big // piece):
            wide = ((big_j - slot * big - part * piece == big_k) & (big_k < piece)).astype(f32).astype(bf16)
            bias_full[...] = bias_full[...] + nn(vec_all[slot], wide)[8 + part:9 + part]
    lax.fori_loop(0, dp, lambda slot, carry: (place(slot), carry)[1], 0)
    gain_one, shift_one = vec_full[0:1], vec_full[1:2]
    gain_two, shift_two = vec_full[2:3], vec_full[3:4]

    def norm_slab(slab):
        def step(place_rows):
            unit, _ = unit_rows(hid_all[slab, place_rows].astype(f32))
            start = pl.multiple_of(slab * rows + place_rows.start, place_rows.size)
            normed_all[pl.ds(start, place_rows.size)] = (unit * gain_one + shift_one).astype(bf16)
        tiles(rows, 256, step)

    def project_slab(slab):
        def step(place_rows):
            here = pl.ds(pl.multiple_of(slab * rows + place_rows.start, place_rows.size), place_rows.size)
            packed = nn(normed_all[here], w_in[...]).astype(bf16)
            q_all[here] = packed[:, :LANES]
            k_all[here] = packed[:, LANES:2 * LANES]
            v_all[here] = packed[:, 2 * LANES:]
        tiles(rows, 256, step)

    own_hidden.wait()
    norm_slab(me_sq)
    hid_pair_in = slab_copy(hid_all.at[pair], hid_all, pair, hid_s.at[0], hid_r, pair)
    hid_pair_in.wait_recv()
    norm_slab(pair)
    for copy in own_in:
        copy.wait()
    many(dp - 1, lambda k: [in_copy(part, other_dp(k), other_dp(k)).wait_recv() for part in range(3)])
    project_slab(me_sq)
    project_slab(pair)
    slab_copy(hid_all.at[far], hid_all, far, hid_s.at[1], hid_r, far).wait_recv()
    hid_next.start()
    second_stage(0)
    norm_slab(far)
    project_slab(far)
    slab_copy(hid_all.at[cross], hid_all, cross, hid_s.at[2], hid_r, pair).wait_recv()
    norm_slab(cross)
    project_slab(cross)
    slab_copy(mem_all.at[far], mem_all, far, mem_s.at[1], mem_r, far).wait_recv()
    mem_next.start()
    second_stage(1)
    second_stage(2)
    third_stage(0)

    limit = len_ref[0]
    mem_limit = mlen_ref[0]
    scale = HD ** (-0.5) * log2_e

    def softmax_block(scores, values):
        largest = jnp.max(scores, axis=1, keepdims=True)
        powers = jnp.exp2(scores - largest)
        total = jnp.sum(powers, axis=1, keepdims=True)
        return nn(powers.astype(bf16), values) / total, largest + jnp.log2(total)

    def att_copy(block, owner):
        return remote(o_heads.at[pl.ds(pl.multiple_of(block * rows, rows), rows)],
                      att_tok.at[:, pl.ds(pl.multiple_of(owner * LANES, LANES), LANES)],
                      a_s.at[block], a_r.at[owner], (me_dp, block))

    def self_block(block):
        keys = (block + 1) * rows
        here = pl.ds(block * rows, rows)
        query = q_all[here]
        bias = jnp.where(lax.broadcasted_iota(i32, (1, keys), 1) < limit, 0.0, masked_score)
        outs, spreads = [], []
        for head in range(2):
            scores = nt(pick(query, head_mask(head)), k_all[pl.ds(0, keys)]) * scale + bias
            row = lax.broadcasted_iota(i32, (rows, rows), 0)
            column = lax.broadcasted_iota(i32, (rows, rows), 1)
            last = jnp.where(column <= row, scores[:, keys - rows:], masked_score)
            scores = jnp.concatenate([scores[:, :keys - rows], last], axis=1) if block else last
            out, spread = softmax_block(scores, v_all[pl.ds(0, keys)])
            outs.append(out)
            spreads.append(spread)
        o_heads[here] = jnp.where(head_mask(0), outs[0], outs[1]).astype(bf16)
        turned = jnp.transpose(jnp.where(head_mask(0), spreads[0], spreads[1]))
        self_lse[0:1, here] = turned[0:1]
        self_lse[1:2, here] = turned[HD:HD + 1]

        @pl.when(me_sq != block)
        def _():
            att_copy(block, me_sq).start()

    comm_steps = {3: lambda: (third_stage(1), second_stage(3)), 2: lambda: (third_stage(2), second_stage(4)),
                  1: lambda: (third_stage(3), second_stage(5)), 0: lambda: third_stage(4)}
    for block in range(sq - 1, -1, -1):
        self_block(block)
        comm_steps[block]()
    att_tok[:, pl.ds(pl.multiple_of(me_sq * LANES, LANES), LANES)] = o_heads[pl.ds(pl.multiple_of(me_sq * rows, rows), rows)]

    own_memory.wait()
    slab_copy(mem_all.at[pair], mem_all, pair, mem_s.at[0], mem_r, pair).wait_recv()
    slab_copy(mem_all.at[cross], mem_all, cross, mem_s.at[2], mem_r, pair).wait_recv()
    c_wait(0)

    def project_memory(slab, carry):
        mem_pair[pl.ds(pl.multiple_of(slab * mem_rows, mem_rows), mem_rows)] = nn(mem_all[slab], w_cm[...]).astype(bf16)
        return carry
    lax.fori_loop(0, sq, project_memory, 0)

    for peer in (pair, far, cross):
        att_copy(peer, peer).wait_recv()
    c_wait(1)
    c_wait(2)

    def step_two(here):
        value = hidden_ref[here].astype(f32) + nn(att_tok[here], w_so[...])
        after_self[here] = value
        unit, _ = unit_rows(value)
        normed = (unit * gain_two + shift_two).astype(bf16)
        normed_two[here] = normed
        cross_q[here] = nn(normed, w_cq[...]).astype(bf16)
    tiles(rows, 256, step_two)

    mem_bias = jnp.where(lax.broadcasted_iota(i32, (1, all_mem), 1) < mem_limit, 0.0, masked_score)

    def cross_pair(number):
        lanes = pl.ds(number * LANES, LANES)
        query = cross_q[:, lanes]
        outs, spreads = [], []
        for head in range(2):
            scores = nt(pick(query, head_mask(head)), mem_pair[:, lanes]) * scale + mem_bias
            out, spread = softmax_block(scores, mem_pair[:, pl.ds(width + number * LANES, LANES)])
            outs.append(out)
            spreads.append(spread)
        mixed[:, lanes] = jnp.where(head_mask(0), outs[0], outs[1]).astype(bf16)
        turned = jnp.transpose(jnp.where(head_mask(0), spreads[0], spreads[1]))
        cross_lse[2 * number:2 * number + 1] = turned[0:1]
        cross_lse[2 * number + 1:2 * number + 2] = turned[HD:HD + 1]

    for number in range(width // LANES):
        cross_pair(number)
        if number == 1:
            third_stage(5)
    c_wait(3)

    def step_three(here):
        after_cross[here] = after_self[here] + nn(mixed[here], w_co[...])
    tiles(rows, 256, step_three)

    c_wait(4)
    c_wait(5)
    for copy in (hid_far, hid_pair, hid_next, mem_far, mem_pair_copy, mem_next):
        copy.wait_send()
    many(dp - 1, lambda k: vec_copy(other_dp(k), me_dp).wait_send())
    many(dp - 1, lambda k: [in_copy(part, other_dp(k), me_dp).wait_send() for part in range(3)])
    for index in range(6):
        finish_weight(index)
    for peer in (pair, far, cross):
        att_copy(peer, me_sq).wait_send()


def whole_specs(names):
    return [pl.BlockSpec(memory_space=name) for name in names]


def run_forward(sizes, args):
    dp, sq, rows, mem_rows, width, inner = sizes
    seq_rows, all_mem = rows * sq, mem_rows * sq
    high = dp // 2
    V, A, S = pltpu.VMEM, pl.ANY, pltpu.SMEM
    dma = pltpu.SemaphoreType.DMA
    outs = [((width, 2 * width), bf16), ((width, width), bf16), ((width, width), bf16), ((width, width), bf16),
            ((width, inner), bf16), ((inner, width), bf16), ((8, width), f32), ((1, inner), f32),
            ((rows, width), f32), ((rows, width), f32), ((rows, width), bf16), ((rows, width), bf16),
            ((rows, width), bf16), ((all_mem, 2 * width), bf16), ((8, rows), f32), ((rows, width), bf16),
            ((seq_rows, LANES), bf16), ((seq_rows, LANES), bf16), ((seq_rows, LANES), bf16), ((8, seq_rows), f32)]
    scratch = [pltpu.VMEM((width, 3 * LANES), bf16), pltpu.VMEM((sq, rows, width), bf16), pltpu.VMEM((sq, mem_rows, width), bf16),
               pltpu.VMEM((dp, 16, LANES), bf16), pltpu.VMEM((seq_rows, width), bf16), pltpu.VMEM((seq_rows, LANES), bf16),
               dma((12,)), dma((3,)), dma((sq,)), dma((3,)), dma((sq,)), dma((dp,)), dma((dp,)), dma((3, dp)), dma((3, dp)),
               dma((6, high)), dma((6, high)), dma((6, high)), dma((6, high)), dma((6,)), dma((6,)), dma((sq,)), dma((sq,))]
    return pl.pallas_call(
        functools.partial(forward_kernel, sizes),
        out_shape=[jax.ShapeDtypeStruct(*out) for out in outs],
        in_specs=whole_specs([S, S, V, V, V, A, A, A, A, A, A, A]),
        out_specs=whole_specs([V] * len(outs)),
        scratch_shapes=scratch,
        compiler_params=pltpu.CompilerParams(collective_id=0, has_side_effects=True, vmem_limit_bytes=60 << 20),
        name="forward",
    )(*args)


def shards(hidden_in, memory, lengths, memory_lengths, self_in, self_out, cross_query, cross_memory, cross_out,
           ffn_in, ffn_bias, ffn_out, out_bias, gain_self, shift_self, gain_cross, shift_cross, gain_ffn, shift_ffn,
           exit_weight, grad_result, grad_halting):
    dp = lax.axis_size("dp")
    sq = lax.axis_size("seq")
    rows, width = hidden_in.shape
    mem_rows = memory.shape[0]
    inner = ffn_in.shape[1]
    sizes = (dp, sq, rows, mem_rows, width, inner)
    strip = width // dp
    big = inner // dp
    piece = min(big, LANES)
    vectors = jnp.stack([gain_self, shift_self, gain_cross, shift_cross, gain_ffn, shift_ffn, out_bias, exit_weight])
    packed_vec = jnp.concatenate([
        jnp.pad(vectors, ((0, 0), (0, LANES - strip))),
        jnp.pad(ffn_bias.reshape(big // piece, piece), ((0, 8 - big // piece), (0, LANES - piece)))])
    (w_cm, w_so, w_cq, w_co, w_fi, w_fo, vec_full, bias_full, after_self, after_cross, normed_two, cross_q,
     mixed, mem_pair, cross_lse, att_tok, q_all, k_all, v_all, self_lse) = run_forward(
        sizes, (lengths, memory_lengths, hidden_in, memory, packed_vec, self_in, cross_memory, self_out, cross_query, cross_out, ffn_in, ffn_out))
    return finish(locals())


def old_norm(value, gain, shift):
    average = jnp.mean(value, axis=-1, keepdims=True)
    centred = value - average
    variance = jnp.mean(centred * centred, axis=-1, keepdims=True)
    inverse = lax.rsqrt(variance + epsilon)
    unit = centred * inverse
    return (unit * gain + shift, unit, inverse)


def old_norm_back(grad_out, unit, inverse, gain):
    scaled = grad_out * gain
    first_mean = jnp.mean(scaled, axis=-1, keepdims=True)
    second_mean = jnp.mean(scaled * unit, axis=-1, keepdims=True)
    grad_in = inverse * (scaled - first_mean - unit * second_mean)
    return (grad_in, jnp.sum(grad_out * unit, axis=0), jnp.sum(grad_out, axis=0))


def old_attend_back(queries, keys_in, values_in, spread, grad_mixed, key_limit, causal):
    query_rows, model_width = queries.shape
    heads = model_width // HD
    block_rows = min(512, query_rows)
    key_rows = keys_in.shape[0]
    key_heads = keys_in.reshape(key_rows, heads, HD)
    value_heads = values_in.reshape(key_rows, heads, HD)
    scale = HD ** (-0.5)

    def one_block(running, items):
        grad_keys, grad_values = running
        index, block_spread = items
        first = index * block_rows
        query = lax.dynamic_slice_in_dim(queries, first, block_rows, 0).reshape(block_rows, heads, HD)
        grad = lax.dynamic_slice_in_dim(grad_mixed, first, block_rows, 0).reshape(block_rows, heads, HD)
        scores = jnp.einsum("qhd,khd->hqk", query, key_heads, preferred_element_type=f32) * scale
        place = jnp.arange(key_rows)
        allowed = place[None, :] < key_limit
        if causal:
            allowed = allowed & (place[None, :] <= first + jnp.arange(block_rows)[:, None])
        scores = jnp.where(allowed[None], scores, masked_score)
        recalled = jnp.exp(scores - block_spread[:, :, None])
        grad_probs = jnp.einsum("qhd,khd->hqk", grad, value_heads, preferred_element_type=f32)
        weighted = jnp.sum(recalled * grad_probs, axis=-1, keepdims=True)
        grad_scores = (recalled * (grad_probs - weighted)).astype(bf16)
        grad_query = jnp.einsum("hqk,khd->qhd", grad_scores, key_heads, preferred_element_type=f32) * scale
        grad_keys = grad_keys + jnp.einsum("hqk,qhd->khd", grad_scores, query, preferred_element_type=f32) * scale
        grad_values = grad_values + jnp.einsum("hqk,qhd->khd", recalled.astype(bf16), grad, preferred_element_type=f32)
        return (grad_keys, grad_values), grad_query.reshape(block_rows, model_width).astype(bf16)

    zero = jnp.zeros((key_rows, heads, HD), f32)
    (grad_keys, grad_values), grad_queries = lax.scan(one_block, (zero, zero), (jnp.arange(query_rows // block_rows), spread))
    return grad_queries.reshape(query_rows, model_width), grad_keys.reshape(key_rows, model_width), grad_values.reshape(key_rows, model_width)


def finish(env):
    class E: pass
    e = E(); e.__dict__.update(env)
    dp, sq, rows, width, mem_rows = e.dp, e.sq, e.rows, e.width, e.mem_rows
    joint = lax.all_gather(e.self_in, "dp", axis=0, tiled=True)
    gain_one, shift_one, gain_two, shift_two, gain_three, shift_three, outer_bias, exit_col = [e.vec_full[i] for i in range(8)]
    positions = lax.axis_index("seq") * rows + jnp.arange(rows)
    live = (positions < e.lengths[0]).astype(f32)
    hidden = e.hidden_in.astype(f32)
    n1, unit_one, inv_one = old_norm(hidden, gain_one, shift_one)
    n1 = n1.astype(bf16)
    _, unit_two, inv_two = old_norm(e.after_self, gain_two, shift_two)
    n3, unit_three, inv_three = old_norm(e.after_cross, gain_three, shift_three)
    n3 = n3.astype(bf16)
    inner_pre = nn(n3, e.w_fi) + e.bias_full[0]
    bent = jnp.tanh(gelu_scale * (inner_pre + gelu_cubic * inner_pre ** 3))
    active = (0.5 * inner_pre * (1.0 + bent)).astype(bf16)
    slope = 0.5 * (1.0 + bent) + 0.5 * inner_pre * (1.0 - bent * bent) * gelu_scale * (1.0 + 3.0 * gelu_cubic * inner_pre * inner_pre)
    output = e.after_cross + nn(active, e.w_fo) + outer_bias
    halting = jax.nn.sigmoid(jnp.dot(output, exit_col, precision=lax.Precision.HIGHEST))
    grad_logit = e.grad_halting * live * halting * (1.0 - halting)
    grad_exit = jnp.dot(grad_logit, output, precision=lax.Precision.HIGHEST)
    grad_output = e.grad_result.astype(f32) * live[:, None] + grad_logit[:, None] * exit_col[None, :]
    gb = grad_output.astype(bf16)
    g_ob = jnp.sum(gb.astype(f32), axis=0)
    g_fo = tn(active, gb)
    g_inner = (nt(gb, e.w_fo) * slope).astype(bf16)
    g_fb = jnp.sum(g_inner.astype(f32), axis=0)
    g_fi = tn(n3, g_inner)
    gn3, gg3, gs3 = old_norm_back(nt(g_inner, e.w_fi), unit_three, inv_three, gain_three)
    gcr = grad_output + gn3
    gcb = gcr.astype(bf16)
    g_co = tn(e.mixed, gcb)
    gmix = nt(gcb, e.w_co).astype(bf16)
    spread_cross = (e.cross_lse * (1 / log2_e))[None]
    gcq, gmk, gmv = old_attend_back(e.cross_q, e.mem_pair[:, :width], e.mem_pair[:, width:], spread_cross, gmix, e.memory_lengths[0], False)
    gmp = lax.psum_scatter(jnp.concatenate([gmk, gmv], axis=1), "seq", scatter_dimension=0, tiled=True).astype(bf16)
    g_cq = tn(e.normed_two, gcq)
    g_cm = tn(e.memory, gmp)
    grad_memory = nt(gmp, e.w_cm)
    gn2, gg2, gs2 = old_norm_back(nt(gcq, e.w_cq), unit_two, inv_two, gain_two)
    gsr = gcr + gn2
    gsb = gsr.astype(bf16)
    g_so = tn(e.att_tok, gsb)
    gatt = nt(gsb, e.w_so).astype(bf16)
    gatt_heads = lax.all_to_all(gatt, "seq", split_axis=1, concat_axis=0, tiled=True)
    spread_self = (e.self_lse[:2] * (1 / log2_e)).reshape(2, sq, rows).transpose(1, 0, 2)
    gq, gk, gv = old_attend_back(e.q_all, e.k_all, e.v_all, spread_self, gatt_heads, e.lengths[0], True)
    gp = lax.all_to_all(jnp.stack([gq, gk.astype(bf16), gv.astype(bf16)], axis=1), "seq", split_axis=0, concat_axis=2, tiled=True).reshape(rows, 3 * width)
    g_si = tn(n1, gp)
    gn1, gg1, gs1 = old_norm_back(nt(gp, joint), unit_one, inv_one, gain_one)
    grad_hidden = gsr + gn1
    grads = (g_si, g_so, g_cq, g_cm, g_co, g_fi, g_fb, g_fo, g_ob, gg1, gs1, gg2, gs2, gg3, gs3, grad_exit)
    pieces = [None] * len(grads)
    for i, g in enumerate(grads):
        if g.ndim == 2:
            part = lax.psum_scatter(g.astype(bf16), "dp", scatter_dimension=0, tiled=True)
            pieces[i] = lax.psum(part.astype(f32), "seq")
    small = [i for i, g in enumerate(grads) if g.ndim == 1]
    flat = jnp.concatenate([grads[i].reshape(dp, -1) for i in small], axis=1)
    flat = lax.dynamic_slice_in_dim(lax.psum(flat, ("dp", "seq")), lax.axis_index("dp"), 1, 0)[0]
    offset = 0
    for i in small:
        n = grads[i].size // dp
        pieces[i] = flat[offset:offset + n]
        offset += n
    return (output.astype(bf16), halting, grad_hidden, grad_memory) + tuple(pieces)


def solution(mesh):
    both = P(("dp", "seq"), None)
    matrix = P("dp", None)
    vector = P("dp")
    return jax.shard_map(
        shards,
        mesh=mesh,
        in_specs=(both, both, vector, vector, matrix, matrix, matrix, matrix, matrix, matrix, vector, matrix)
        + (vector,) * 8 + (both, P(("dp", "seq"))),
        out_specs=(both, P(("dp", "seq")), both, both) + (matrix,) * 6 + (vector, matrix) + (vector,) * 8,
        check_vma=False,
    )
```

```python
import functools
import jax
import jax.numpy as jnp
from jax import lax
from jax.experimental import pallas as pl
from jax.experimental.pallas import tpu as pltpu
from jax.sharding import PartitionSpec as P

bf16 = jnp.bfloat16
f32 = jnp.float32
i32 = jnp.int32
MESH = pl.DeviceIdType.MESH
HD = 64
LANES = 128
epsilon = 1e-05
masked_score = -1e30
gelu_scale = 0.7978845608028654
gelu_cubic = 0.044715
log2_e = 1.4426950408889634


def nn(left, right):
    return jnp.dot(left, right, preferred_element_type=f32)


def nt(left, right, precision=None):
    return lax.dot_general(
        left, right, (((1,), (1,)), ((), ())), preferred_element_type=f32, precision=precision
    )


def tn(left, right):
    return lax.dot_general(
        left, right, (((0,), (0,)), ((), ())), preferred_element_type=f32
    )


def many(count, step):
    if count <= 8:
        for index in range(count):
            step(index)
    else:
        lax.fori_loop(0, count, lambda index, carry: (step(index), carry)[1], 0)


def tiles(rows, size, step):
    lax.fori_loop(0, rows // size, lambda index, carry: (step(pl.ds(pl.multiple_of(index * size, size), size)), carry)[1], 0)


def unit_rows(value):
    average = jnp.mean(value, axis=-1, keepdims=True)
    centred = value - average
    variance = jnp.mean(centred * centred, axis=-1, keepdims=True)
    inverse = lax.rsqrt(variance + epsilon)
    return centred * inverse, inverse


def head_mask(head):
    lane = lax.broadcasted_iota(i32, (1, LANES), 1)
    return (lane < HD) == (head == 0)


def pick(value, mask):
    return jnp.where(mask, value, jnp.zeros_like(value))


def layer_kernel(sizes, *refs):
    dp, sq, rows, mem_rows, width, inner = sizes
    high = dp // 2
    strip = width // dp
    seq_rows = rows * sq
    all_mem = mem_rows * sq
    (len_ref, mlen_ref, hidden_ref, memory_ref, vec_ref, grad_ref, halt_grad_ref, self_in_ref, cross_memory_ref, self_out_ref,
     cross_query_ref, cross_out_ref, ffn_in_ref, ffn_out_ref,
     result_ref, halting_ref, grad_hidden_ref, grad_memory_ref, out_si, out_cm, out_so, out_cq, out_co, out_fi, out_fo, out_vec,
     w_cm, w_so, w_cq, w_co, w_fi, w_fo, vec_full, bias_full, after_self, after_cross, normed_two, cross_q,
     mixed, mem_pair, cross_lse, att_tok, q_all, k_all, v_all, self_lse,
     w_in, hid_all, mem_all, vec_all, normed_all, o_heads,
     normed_three, active, grad_inner, slope, branch, cross_branch, grad_mixed, cross_delta,
     grad_heads, grad_in, grad_in_got, part_mem, part_mem_got,
     half_got, pair_got, far_got, sums, sums_seq, sums_dp, last_sums, last_seq, last_dp,
     g_cm, g_so, g_cq, g_co, g_fi, g_fo, p_cm, p_so, p_cq, p_co, p_fi, p_fo, x_cm, x_so, x_cq, x_co, x_fi, x_fo,
     h_cm, h_so, h_cq, h_co, h_fi, h_fo, f_cm, f_so, f_cq, f_co, f_fi, f_fo, y_cm, y_so, y_cq, y_co, y_fi, y_fo,
     loc_sem, hid_s, hid_r, mem_s, mem_r, vec_s, vec_r, in_s, in_r, z_s, z_r, x_s, x_r, c_s, c_r, a_s, a_r,
     gc_s, gc_r, gx_s, gx_r, gz_s, gz_r, gy_s, gy_r, gp_s, gp_r, gi_s, gi_r, go_s, go_r, gm_s, gm_r, da_s, da_r,
     yh_s, yh_r, yf_s, yf_r, yp_s, yp_r, s1_s, s1_r, s2_s, s2_r, s3_s, s3_r, s4_s, s4_r) = refs
    me_dp = lax.axis_index("dp")
    me_sq = lax.axis_index("seq")
    me_hi = me_dp // 2
    me_lo = me_dp % 2
    half = me_sq % 2
    pair = me_sq + 1 - 2 * half
    far = (me_sq + 2) % sq
    cross = (pair + 2) % sq
    shards = (cross_memory_ref, self_out_ref, cross_query_ref, cross_out_ref, ffn_in_ref, ffn_out_ref)
    wholes = (w_cm, w_so, w_cq, w_co, w_fi, w_fo)

    def remote(src, dst, send, recv, device):
        return pltpu.make_async_remote_copy(src_ref=src, dst_ref=dst, send_sem=send, recv_sem=recv, device_id=device, device_id_type=MESH)

    def other_dp(step):
        return (me_dp + 1 + step) % dp

    barrier = pltpu.get_barrier_semaphore()
    many(dp - 1, lambda k: pl.semaphore_signal(barrier, inc=1, device_id=(other_dp(k), me_sq), device_id_type=MESH))
    for peer in (pair, far, cross):
        pl.semaphore_signal(barrier, inc=1, device_id=(me_dp, peer), device_id_type=MESH)
    pl.semaphore_wait(barrier, dp - 1 + 3)

    def slab_copy(src, dst_all, slab, send, recv, peer):
        return remote(src, dst_all.at[slab], send, recv.at[slab], (me_dp, peer))

    def mem_slab(slab):
        return mem_all.at[pl.ds(pl.multiple_of(slab * mem_rows, mem_rows), mem_rows)]

    def mem_copy(src, slab, send, peer):
        return remote(src, mem_slab(slab), send, mem_r.at[slab], (me_dp, peer))

    own_hidden = pltpu.make_async_copy(hidden_ref, hid_all.at[me_sq], loc_sem.at[0])
    own_memory = pltpu.make_async_copy(memory_ref, mem_slab(me_sq), loc_sem.at[1])
    hid_far = slab_copy(hidden_ref, hid_all, me_sq, hid_s.at[1], hid_r, far)
    hid_pair = slab_copy(hidden_ref, hid_all, me_sq, hid_s.at[0], hid_r, pair)
    mem_far = mem_copy(memory_ref, me_sq, mem_s.at[1], far)
    mem_pair_copy = mem_copy(memory_ref, me_sq, mem_s.at[0], pair)
    hid_next = slab_copy(hid_all.at[far], hid_all, far, hid_s.at[2], hid_r, pair)
    mem_next = mem_copy(mem_slab(far), far, mem_s.at[2], pair)

    def vec_copy(peer, slot):
        return remote(vec_ref, vec_all.at[slot], vec_s.at[peer], vec_r.at[slot], (peer, me_sq))

    def in_copy(part, peer, slot):
        return remote(
            self_in_ref.at[:, pl.ds(pl.multiple_of(part * width + me_sq * LANES, LANES), LANES)],
            w_in.at[pl.ds(pl.multiple_of(slot * strip, strip), strip), pl.ds(part * LANES, LANES)],
            in_s.at[part, peer], in_r.at[part, slot], (peer, me_sq))

    own_vec = pltpu.make_async_copy(vec_ref, vec_all.at[me_dp], loc_sem.at[2])
    own_in = [pltpu.make_async_copy(
        self_in_ref.at[:, pl.ds(pl.multiple_of(part * width + me_sq * LANES, LANES), LANES)],
        w_in.at[pl.ds(pl.multiple_of(me_dp * strip, strip), strip), pl.ds(part * LANES, LANES)],
        loc_sem.at[3 + part]) for part in range(3)]

    hid_far.start()
    hid_pair.start()
    many(dp - 1, lambda k: vec_copy(other_dp(k), me_dp).start())
    many(dp - 1, lambda k: [in_copy(part, other_dp(k), me_dp).start() for part in range(3)])
    own_hidden.start()
    own_memory.start()
    own_vec.start()
    for copy in own_in:
        copy.start()
    mem_far.start()
    mem_pair_copy.start()

    def columns(index):
        size = shards[index].shape[1] // 2
        return pl.ds(pl.multiple_of(half * size, LANES), size)

    def block_rows(index, slot):
        size = shards[index].shape[0]
        return pl.ds(pl.multiple_of(slot * size, size), size)

    def z_copy(index, peer, slot):
        return remote(shards[index].at[:, columns(index)], wholes[index].at[block_rows(index, slot * 2 + me_lo), columns(index)],
                      z_s.at[index, peer], z_r.at[index, slot], (peer * 2 + me_lo, me_sq))

    def x_copy(index, slot, low, own):
        there = wholes[index].at[block_rows(index, slot * 2 + low), columns(index)]
        src = shards[index].at[:, columns(index)] if own else there
        return remote(src, there, x_s.at[index, slot], x_r.at[index, slot], (me_hi * 2 + 1 - me_lo, me_sq))

    def c_copy(index):
        there = wholes[index].at[:, columns(index)]
        return remote(there, there, c_s.at[index], c_r.at[index], (me_dp, pair))

    def c_wait(index):
        size = shards[index].shape[1] // 2
        there = wholes[index].at[:, pl.ds(pl.multiple_of((1 - half) * size, LANES), size)]
        remote(there, there, c_s.at[index], c_r.at[index], (me_dp, pair)).wait_recv()

    def own_copy(index):
        return pltpu.make_async_copy(shards[index].at[:, columns(index)], wholes[index].at[block_rows(index, me_dp), columns(index)], loc_sem.at[6 + index])

    def other_hi(step):
        return (me_hi + 1 + step) % high

    def first_stage(index):
        many(high - 1, lambda k: z_copy(index, other_hi(k), me_hi).start())
        x_copy(index, me_hi, me_lo, True).start()
        own_copy(index).start()

    def second_stage(index):
        def forward(k):
            z_copy(index, other_hi(k), other_hi(k)).wait_recv()
            x_copy(index, other_hi(k), me_lo, False).start()
        many(high - 1, forward)

    def third_stage(index):
        many(high, lambda k: x_copy(index, k, 1 - me_lo, False).wait_recv())
        own_copy(index).wait()
        c_copy(index).start()

    def finish_weight(index):
        many(high - 1, lambda k: z_copy(index, other_hi(k), me_hi).wait_send())
        many(high, lambda k: x_copy(index, k, me_lo, False).wait_send())
        c_copy(index).wait_send()

    for index in range(6):
        first_stage(index)

    own_vec.wait()
    many(dp - 1, lambda k: vec_copy(other_dp(k), other_dp(k)).wait_recv())
    vec_full[...] = jnp.zeros_like(vec_full)
    bias_full[...] = jnp.zeros_like(bias_full)
    lane_k = lax.broadcasted_iota(i32, (LANES, width), 0)
    lane_j = lax.broadcasted_iota(i32, (LANES, width), 1)
    big = inner // dp
    piece = min(big, LANES)
    big_k = lax.broadcasted_iota(i32, (LANES, inner), 0)
    big_j = lax.broadcasted_iota(i32, (LANES, inner), 1)

    def place(slot):
        hot = ((lane_j - slot * strip == lane_k) & (lane_k < strip)).astype(f32).astype(bf16)
        vec_full[...] = vec_full[...] + nn(vec_all[slot], hot)[:8]
        for part in range(big // piece):
            wide = ((big_j - slot * big - part * piece == big_k) & (big_k < piece)).astype(f32).astype(bf16)
            bias_full[...] = bias_full[...] + nn(vec_all[slot], wide)[8 + part:9 + part]
    lax.fori_loop(0, dp, lambda slot, carry: (place(slot), carry)[1], 0)
    gain_one, shift_one = vec_full[0:1], vec_full[1:2]
    gain_two, shift_two = vec_full[2:3], vec_full[3:4]

    def norm_slab(slab):
        def step(place_rows):
            unit, _ = unit_rows(hid_all[slab, place_rows].astype(f32))
            start = pl.multiple_of(slab * rows + place_rows.start, place_rows.size)
            normed_all[pl.ds(start, place_rows.size)] = (unit * gain_one + shift_one).astype(bf16)
        tiles(rows, 256, step)

    def project_slab(slab):
        def step(place_rows):
            here = pl.ds(pl.multiple_of(slab * rows + place_rows.start, place_rows.size), place_rows.size)
            packed = nn(normed_all[here], w_in[...]).astype(bf16)
            q_all[here] = packed[:, :LANES]
            k_all[here] = packed[:, LANES:2 * LANES]
            v_all[here] = packed[:, 2 * LANES:]
        tiles(rows, 256, step)

    own_hidden.wait()
    norm_slab(me_sq)
    hid_pair_in = slab_copy(hid_all.at[pair], hid_all, pair, hid_s.at[0], hid_r, pair)
    hid_pair_in.wait_recv()
    norm_slab(pair)
    for copy in own_in:
        copy.wait()
    many(dp - 1, lambda k: [in_copy(part, other_dp(k), other_dp(k)).wait_recv() for part in range(3)])
    project_slab(me_sq)
    project_slab(pair)
    slab_copy(hid_all.at[far], hid_all, far, hid_s.at[1], hid_r, far).wait_recv()
    hid_next.start()
    second_stage(0)
    norm_slab(far)
    project_slab(far)
    slab_copy(hid_all.at[cross], hid_all, cross, hid_s.at[2], hid_r, pair).wait_recv()
    norm_slab(cross)
    project_slab(cross)
    mem_copy(mem_slab(far), far, mem_s.at[1], far).wait_recv()
    mem_next.start()
    second_stage(1)
    second_stage(2)
    third_stage(0)

    limit = len_ref[0]
    mem_limit = mlen_ref[0]
    scale = HD ** (-0.5) * log2_e

    def softmax_block(scores, values):
        largest = jnp.max(scores, axis=1, keepdims=True)
        powers = jnp.exp2(scores - largest)
        total = jnp.sum(powers, axis=1, keepdims=True)
        return nn(powers.astype(bf16), values) / total, largest + jnp.log2(total)

    def att_copy(block, owner):
        return remote(o_heads.at[pl.ds(pl.multiple_of(block * rows, rows), rows)],
                      att_tok.at[:, pl.ds(pl.multiple_of(owner * LANES, LANES), LANES)],
                      a_s.at[block], a_r.at[owner], (me_dp, block))

    def self_block(block):
        here = pl.ds(block * rows, rows)
        query = q_all[here]
        outs, spreads = [], []
        for head in range(2):
            head_query = pick(query, head_mask(head))

            def key_part(index, carry, diagonal):
                largest, total, out = carry
                there = pl.ds(pl.multiple_of(index * rows, rows), rows)
                place = index * rows + lax.broadcasted_iota(i32, (1, rows), 1)
                scores = nt(head_query, k_all[there]) * scale + jnp.where(place < limit, 0.0, masked_score)
                if diagonal:
                    scores = jnp.where(lax.broadcasted_iota(i32, (rows, rows), 1) <= lax.broadcasted_iota(i32, (rows, rows), 0), scores, masked_score)
                higher = jnp.maximum(largest, jnp.max(scores, axis=1, keepdims=True))
                powers = jnp.exp2(scores - higher)
                shrink = jnp.exp2(largest - higher)
                total = total * shrink + jnp.sum(powers, axis=1, keepdims=True)
                return higher, total, out * shrink + nn(powers.astype(bf16), v_all[there])

            carry = (jnp.full((rows, 1), -3e38, f32), jnp.zeros((rows, 1), f32), jnp.zeros((rows, LANES), f32))
            if block:
                carry = lax.fori_loop(0, block, lambda index, held: key_part(index, held, False), carry)
            largest, total, out = key_part(block, carry, True)
            outs.append(out / total)
            spreads.append(largest + jnp.log2(total))
        o_heads[here] = jnp.where(head_mask(0), outs[0], outs[1]).astype(bf16)
        turned = jnp.transpose(jnp.where(head_mask(0), spreads[0], spreads[1]))
        self_lse[0:1, here] = turned[0:1]
        self_lse[1:2, here] = turned[HD:HD + 1]

        @pl.when(me_sq != block)
        def _():
            att_copy(block, me_sq).start()

    comm_steps = {3: lambda: (third_stage(1), second_stage(3)), 2: lambda: (third_stage(2), second_stage(4)),
                  1: lambda: (third_stage(3), second_stage(5)), 0: lambda: third_stage(4)}
    for block in range(sq - 1, -1, -1):
        self_block(block)
        comm_steps[block]()
    att_tok[:, pl.ds(pl.multiple_of(me_sq * LANES, LANES), LANES)] = o_heads[pl.ds(pl.multiple_of(me_sq * rows, rows), rows)]

    own_memory.wait()
    mem_copy(mem_slab(pair), pair, mem_s.at[0], pair).wait_recv()
    mem_copy(mem_slab(cross), cross, mem_s.at[2], pair).wait_recv()
    c_wait(0)

    def project_memory(slab, carry):
        place = pl.ds(pl.multiple_of(slab * mem_rows, mem_rows), mem_rows)
        mem_pair[place] = nn(mem_all[place], w_cm[...]).astype(bf16)
        return carry
    lax.fori_loop(0, sq, project_memory, 0)

    for peer in (pair, far, cross):
        att_copy(peer, peer).wait_recv()
    c_wait(1)
    c_wait(2)

    def step_two(here):
        value = hidden_ref[here].astype(f32) + nn(att_tok[here], w_so[...])
        after_self[here] = value
        unit, _ = unit_rows(value)
        normed = (unit * gain_two + shift_two).astype(bf16)
        normed_two[here] = normed
        cross_q[here] = nn(normed, w_cq[...]).astype(bf16)
    tiles(rows, 256, step_two)

    mem_bias = jnp.where(lax.broadcasted_iota(i32, (1, all_mem), 1) < mem_limit, 0.0, masked_score)

    def cross_pair(number, held):
        lanes = pl.ds(pl.multiple_of(number * LANES, LANES), LANES)
        value_lanes = pl.ds(pl.multiple_of(width + number * LANES, LANES), LANES)
        query = cross_q[:, lanes]
        outs, spreads = [], []
        for head in range(2):
            scores = nt(pick(query, head_mask(head)), mem_pair[:, lanes]) * scale + mem_bias
            out, spread = softmax_block(scores, mem_pair[:, value_lanes])
            outs.append(out)
            spreads.append(spread)
        mixed[:, lanes] = jnp.where(head_mask(0), outs[0], outs[1]).astype(bf16)
        turned = jnp.transpose(jnp.where(head_mask(0), spreads[0], spreads[1]))
        cross_lse[pl.ds(2 * number, 1)] = turned[0:1]
        cross_lse[pl.ds(2 * number + 1, 1)] = turned[HD:HD + 1]
        return held

    pairs = width // LANES
    lax.fori_loop(0, pairs // 2, cross_pair, 0)
    third_stage(5)
    lax.fori_loop(pairs // 2, pairs, cross_pair, 0)
    c_wait(3)

    def step_three(here):
        after_cross[here] = after_self[here] + nn(mixed[here], w_co[...])
    tiles(rows, 256, step_three)

    c_wait(4)
    c_wait(5)
    gain_three, shift_three, outer_bias, exit_row = vec_full[4:5], vec_full[5:6], vec_full[6:7], vec_full[7:8]
    parts = ((g_cm, p_cm, x_cm, h_cm, f_cm, y_cm, out_cm), (g_so, p_so, x_so, h_so, f_so, y_so, out_so),
             (g_cq, p_cq, x_cq, h_cq, f_cq, y_cq, out_cq), (g_co, p_co, x_co, h_co, f_co, y_co, out_co),
             (g_fi, p_fi, x_fi, h_fi, f_fi, y_fi, out_fi), (g_fo, p_fo, x_fo, h_fo, f_fo, y_fo, out_fo))
    chunk = 512

    def norm_back(grad, unit, inverse, gain):
        scaled = grad * gain
        first = jnp.mean(scaled, axis=-1, keepdims=True)
        second = jnp.mean(scaled * unit, axis=-1, keepdims=True)
        return inverse * (scaled - first - unit * second)

    def add_sum(index, value):
        sums[index:index + 1] = sums[index:index + 1] + jnp.sum(value, axis=0, keepdims=True)

    def gc_copy(index):
        size = shards[index].shape[1] // 2
        other = pl.ds(pl.multiple_of((1 - half) * size, LANES), size)
        return remote(parts[index][0].at[:, :, :, other], parts[index][1], gc_s.at[index], gc_r.at[index], (me_dp, pair))

    def gx_copy(index):
        return remote(parts[index][1].at[:, 1 - me_lo], parts[index][2], gx_s.at[index], gx_r.at[index], (me_hi * 2 + 1 - me_lo, me_sq))

    def gz_copy(index, peer, slot):
        return remote(parts[index][2].at[peer], parts[index][3].at[slot], gz_s.at[index, peer], gz_r.at[index, slot], (peer * 2 + me_lo, me_sq))

    def gy_copy(index):
        return remote(parts[index][4], parts[index][5], gy_s.at[index], gy_r.at[index], (me_dp, far))

    def gp_copy(index, side):
        size = shards[index].shape[1] // 2
        there = parts[index][6].at[:, pl.ds(pl.multiple_of(side * size, LANES), size)]
        return remote(there, there, gp_s.at[index], gp_r.at[index], (me_dp, pair))

    def reduce_pair(index):
        gc_copy(index).start()

    def reduce_low(index):
        gc_copy(index).wait_recv()
        whole_ref, part_ref = parts[index][0], parts[index][1]

        def add(place, carry):
            for low in range(2):
                part_ref[place, low] = (part_ref[place, low].astype(f32) + whole_ref[place, low, :, columns(index)].astype(f32)).astype(bf16)
            return carry
        lax.fori_loop(0, high, add, 0)
        gx_copy(index).start()

    def reduce_high(index):
        gx_copy(index).wait_recv()
        part_ref, low_ref = parts[index][1], parts[index][2]

        def add(place, carry):
            low_ref[place] = (low_ref[place].astype(f32) + part_ref[place, me_lo].astype(f32)).astype(bf16)
            return carry
        lax.fori_loop(0, high, add, 0)
        many(high - 1, lambda k: gz_copy(index, other_hi(k), me_hi).start())

    def reduce_far(index):
        low_ref, high_ref, far_ref = parts[index][2], parts[index][3], parts[index][4]
        high_ref[me_hi] = low_ref[me_hi]
        many(high - 1, lambda k: gz_copy(index, other_hi(k), other_hi(k)).wait_recv())
        far_ref[...] = high_ref[0].astype(f32)

        def add(place, carry):
            far_ref[...] = far_ref[...] + high_ref[place].astype(f32)
            return carry
        lax.fori_loop(1, high, add, 0)
        gy_copy(index).start()

    def reduce_last(index):
        far_ref, got_ref, out_ref = parts[index][4], parts[index][5], parts[index][6]
        gy_copy(index).wait_recv()
        out_ref[:, columns(index)] = far_ref[...] + got_ref[...]
        gp_copy(index, half).start()

    def reduce_end(index):
        gp_copy(index, 1 - half).wait_recv()

    def reduce_drain(index):
        gc_copy(index).wait_send()
        gx_copy(index).wait_send()
        many(high - 1, lambda k: gz_copy(index, other_hi(k), me_hi).wait_send())
        gy_copy(index).wait_send()
        gp_copy(index, half).wait_send()

    def weight_grad(index, left, rights):
        out_ref = parts[index][0]
        size = shards[index].shape[0]
        pieces = max(1, 256 // size)

        def step(tile, carry):
            features = left(tile)
            for number, right in enumerate(rights):
                value = tn(features, right())
                span = min(size, 256)
                cols = pl.ds(number * value.shape[1], value.shape[1])
                for piece in range(pieces):
                    place = tile * pieces + piece
                    out_ref[place // 2, place % 2, :, cols] = value[piece * span:(piece + 1) * span].astype(bf16)
            return carry
        lax.fori_loop(0, size * dp // 256, step, 0)

    def feature_tile(ref):
        return lambda tile: ref[:, pl.ds(pl.multiple_of(tile * 256, 256), 256)]

    hid_next.wait_send()
    for index in range(6):
        finish_weight(index)
    grad_res = grad_hidden_ref
    grad_packed, sum_in, turned_q = w_fo, after_cross, slope
    packed_cols = pl.ds(0, 3 * LANES)
    turned_rows = pl.ds(0, LANES)
    sums[...] = jnp.zeros_like(sums)
    halting_ref[...] = jnp.zeros_like(halting_ref)

    def ffn_step(here):
        size = here.size
        unit, inverse = unit_rows(after_cross[here])
        normed = (unit * gain_three + shift_three).astype(bf16)
        normed_three[here] = normed
        out = after_cross[here] + outer_bias
        for part in range(inner // chunk):
            cols = pl.ds(part * chunk, chunk)
            pre = nn(normed, w_fi[:, cols]) + bias_full[:, cols]
            square = pre * pre
            bent = jnp.tanh(gelu_scale * (pre + gelu_cubic * square * pre))
            act = (0.5 * pre * (1.0 + bent)).astype(bf16)
            active[part, here] = act
            slope[:, cols] = 0.5 * (1.0 + bent) + 0.5 * pre * (1.0 - bent * bent) * gelu_scale * (1.0 + 3.0 * gelu_cubic * square)
            out = out + nn(act, w_fo[cols])
        result_ref[here] = out.astype(bf16)
        halt = 1.0 / (1.0 + jnp.exp(-jnp.sum(out * exit_row, axis=-1, keepdims=True)))
        place = here.start + lax.broadcasted_iota(i32, (size, rows), 0)
        same = place == lax.broadcasted_iota(i32, (size, rows), 1)
        halting_ref[...] = halting_ref[...] + jnp.sum(jnp.where(same, halt, 0.0), axis=0, keepdims=True)
        halt_grad = jnp.sum(jnp.where(same, halt_grad_ref[...], 0.0), axis=1, keepdims=True)
        live = (me_sq * rows + here.start + lax.broadcasted_iota(i32, (size, 1), 0) < limit).astype(f32)
        grad_logit = halt_grad * live * halt * (1.0 - halt)
        add_sum(7, grad_logit * out)
        grad_out = grad_ref[here].astype(f32) * live + grad_logit * exit_row
        grad_branch = grad_out.astype(bf16)
        branch[here] = grad_branch
        add_sum(6, grad_branch.astype(f32))
        grad_normed = jnp.zeros((size, width), f32)
        for part in range(inner // chunk):
            cols = pl.ds(part * chunk, chunk)
            grad_part = (nt(grad_branch, w_fo[cols]) * slope[:, cols]).astype(bf16)
            grad_inner[part, here] = grad_part
            add_sum(8 + part, grad_part.astype(f32))
            grad_normed = grad_normed + nt(grad_part, w_fi[:, cols])
        add_sum(4, grad_normed * unit)
        add_sum(5, grad_normed)
        grad_cross = grad_out + norm_back(grad_normed, unit, inverse, gain_three)
        grad_res[here] = grad_cross
        grad_cross_branch = grad_cross.astype(bf16)
        cross_branch[here] = grad_cross_branch
        grad_mixed[here] = nt(grad_cross_branch, w_co[...]).astype(bf16)
    tiles(rows, 256, ffn_step)
    weight_grad(5, lambda tile: active[tile // 2, :, pl.ds(pl.multiple_of(tile % 2 * 256, 256), 256)], [lambda: branch[...]])
    reduce_pair(5)
    weight_grad(4, feature_tile(normed_three), [functools.partial(lambda part: grad_inner[part], part) for part in range(inner // chunk)])
    reduce_pair(4)
    weight_grad(3, feature_tile(mixed), [lambda: cross_branch[...]])
    reduce_pair(3)

    select = (lax.broadcasted_iota(i32, (8, width), 1) // HD == lax.broadcasted_iota(i32, (8, width), 0)).astype(f32)
    cross_delta[...] = nt(select, grad_mixed[...].astype(f32) * mixed[...].astype(f32), lax.Precision.HIGHEST)
    score_scale = HD ** (-0.5)

    def attend_back(keys, values, query, grad, spread_rows, delta_rows, bias, mask):
        grad_keys, grad_values, grad_query = None, None, None
        for head in range(2):
            only = head_mask(head)
            head_keys = pick(keys, only)
            scores = nt(head_keys, query) * scale + bias
            if mask is not None:
                scores = jnp.where(mask, scores, masked_score)
            powers = jnp.exp2(scores - spread_rows[head])
            grad_powers = nt(pick(values, only), grad)
            grad_scores = (powers * (grad_powers - delta_rows[head])).astype(bf16)
            value_part = nn(powers.astype(bf16), pick(grad, only))
            key_part = nn(grad_scores, pick(query, only))
            query_part = nn(jnp.transpose(head_keys), grad_scores)
            grad_values = value_part if head == 0 else grad_values + value_part
            grad_keys = key_part if head == 0 else grad_keys + key_part
            grad_query = query_part if head == 0 else grad_query + query_part
        return grad_keys, grad_values, grad_query

    key_block = 512
    key_blocks = all_mem // key_block
    grad_pair = active
    grad_cq = branch
    grad_att = normed_three
    part_hid = hid_all
    cross_comm = {0: lambda: (reduce_low(5), reduce_low(4)), 1: lambda: reduce_low(3), 2: lambda: None, 3: lambda: reduce_high(5)}
    def cross_back(number, held):
        lanes = pl.ds(pl.multiple_of(number * LANES, LANES), LANES)
        value_lanes = pl.ds(pl.multiple_of(width + number * LANES, LANES), LANES)

        def block_step(block, total):
            here = pl.ds(pl.multiple_of(block * key_block, key_block), key_block)
            key_place = block * key_block + lax.broadcasted_iota(i32, (key_block, 1), 0)
            grad_keys, grad_values, grad_query = attend_back(
                mem_pair[here, lanes], mem_pair[here, value_lanes], cross_q[:, lanes], grad_mixed[:, lanes],
                [cross_lse[pl.ds(2 * number + head, 1)] for head in range(2)],
                [cross_delta[pl.ds(2 * number + head, 1)] for head in range(2)],
                jnp.where(key_place < mem_limit, 0.0, masked_score), None)
            grad_pair[block, :, lanes] = (grad_keys * score_scale).astype(bf16)
            grad_pair[key_blocks + block, :, lanes] = grad_values.astype(bf16)
            return total + grad_query

        total = lax.fori_loop(0, key_blocks, block_step, jnp.zeros((LANES, rows), f32))
        grad_cq[:, lanes] = (jnp.transpose(total) * score_scale).astype(bf16)
        return held

    for number in range(pairs):
        lax.fori_loop(number, number + 1, cross_back, 0)
        cross_comm[number]()

    def step_two_back(here):
        grad_normed = nt(grad_cq[here], w_cq[...])
        unit, inverse = unit_rows(after_self[here])
        add_sum(2, grad_normed * unit)
        add_sum(3, grad_normed)
        grad_self = grad_res[here] + norm_back(grad_normed, unit, inverse, gain_two)
        grad_res[here] = grad_self
        grad_self_branch = grad_self.astype(bf16)
        cross_branch[here] = grad_self_branch
        grad_att[here] = nt(grad_self_branch, w_so[...]).astype(bf16)

    tiles(rows, 256, step_two_back)

    def da_copy(peer, owner):
        return remote(grad_att.at[:, pl.ds(pl.multiple_of(peer * LANES, LANES), LANES)],
                      grad_heads.at[pl.ds(pl.multiple_of(owner * rows, rows), rows)], da_s.at[peer], da_r.at[owner], (me_dp, peer))

    for peer in (far, cross, pair):
        da_copy(peer, me_sq).start()
    grad_heads[pl.ds(pl.multiple_of(me_sq * rows, rows), rows)] = grad_att[:, pl.ds(pl.multiple_of(me_sq * LANES, LANES), LANES)]

    def gm_copy(peer, owner):
        return remote(part_mem.at[peer], part_mem_got.at[owner], gm_s.at[peer], gm_r.at[owner], (me_dp, peer))

    def memory_part(slab, carry):
        per_block = key_block // mem_rows
        place = pl.ds(pl.multiple_of(slab % per_block * mem_rows, mem_rows), mem_rows)
        part_mem[slab] = (nt(grad_pair[slab // per_block, place], w_cm[:, :width])
                          + nt(grad_pair[key_blocks + slab // per_block, place], w_cm[:, width:])).astype(bf16)
        return carry

    weight_grad(0, feature_tile(mem_all), [functools.partial(lambda part: grad_pair[part * key_blocks:(part + 1) * key_blocks].reshape(all_mem, width), part) for part in range(2)])
    reduce_pair(0)
    weight_grad(1, feature_tile(att_tok), [lambda: cross_branch[...]])
    reduce_pair(1)
    weight_grad(2, feature_tile(normed_two), [lambda: grad_cq[...]])
    reduce_pair(2)
    reduce_high(4)
    lax.fori_loop(0, sq, memory_part, 0)

    def s1_copy(peer, owner):
        return remote(sums, sums_seq.at[owner], s1_s.at[peer], s1_r.at[owner], (me_dp, peer))

    for peer in (pair, far, cross):
        da_copy(peer, peer).wait_recv()
    for peer in (far, cross, pair):
        gm_copy(peer, me_sq).start()
    select_two = (lax.broadcasted_iota(i32, (8, LANES), 1) // HD == lax.broadcasted_iota(i32, (8, LANES), 0)).astype(f32)
    deltas = nt(select_two, grad_heads[...].astype(f32) * o_heads[...].astype(f32), lax.Precision.HIGHEST)
    self_lse[2:4] = deltas[0:2]
    turned_q[turned_rows] = jnp.zeros((LANES, rows * sq), f32)
    half_rows = rows // 2

    def yh_copy(block):
        there = half_got.at[block % 2]
        return remote(part_hid.at[block, pl.ds(pl.multiple_of((1 - half) * half_rows, half_rows), half_rows)], there,
                      yh_s.at[block], yh_r.at[block], (me_dp, pair))

    def yf_copy(block, side):
        return remote(part_hid.at[block, pl.ds(pl.multiple_of(half * half_rows, half_rows), half_rows)], far_got.at[pl.ds(pl.multiple_of(side * half_rows, half_rows), half_rows)],
                      yf_s.at[block], yf_r.at[side], (me_dp, block))

    def yp_copy(block):
        return remote(part_hid.at[block], pair_got, yp_s.at[0], yp_r.at[0], (me_dp, pair))

    def away(block):
        return me_sq // 2 != block // 2

    def send_part(block):
        @pl.when(away(block))
        def _():
            yh_copy(block).start()

        @pl.when(pair == block)
        def _():
            yp_copy(block).start()

    def forward_part(block):
        @pl.when(away(block))
        def _():
            yh_copy(block).wait_recv()
            place = pl.ds(pl.multiple_of(half * half_rows, half_rows), half_rows)
            part_hid[block, place] = (part_hid[block, place].astype(f32) + half_got[block % 2].astype(f32)).astype(bf16)
            yf_copy(block, half).start()

    def key_step(block):
        here = pl.ds(block * rows, rows)
        keys, values = k_all[here], v_all[here]
        bias = jnp.where(block * rows + lax.broadcasted_iota(i32, (rows, 1), 0) < limit, 0.0, masked_score)

        def query_step(index, carry, diagonal):
            there = pl.ds(pl.multiple_of(index * rows, rows), rows)
            mask = None
            if diagonal:
                mask = lax.broadcasted_iota(i32, (rows, rows), 0) <= lax.broadcasted_iota(i32, (rows, rows), 1)
            grad_keys, grad_values, grad_query = attend_back(
                keys, values, q_all[there], grad_heads[there],
                [self_lse[head:head + 1, there] for head in range(2)],
                [self_lse[2 + head:3 + head, there] for head in range(2)], bias, mask)
            turned_q[turned_rows, there] = turned_q[turned_rows, there] + grad_query
            return carry[0] + grad_keys, carry[1] + grad_values

        zero = jnp.zeros((rows, LANES), f32)
        carry = query_step(block, (zero, zero), True)
        if block + 1 < sq:
            carry = lax.fori_loop(block + 1, sq, lambda index, held: query_step(index, held, False), carry)
        grad_packed[here, pl.ds(LANES, LANES)] = (carry[0] * score_scale).astype(bf16)
        grad_packed[here, pl.ds(2 * LANES, LANES)] = carry[1].astype(bf16)
        grad_packed[here, pl.ds(0, LANES)] = (jnp.transpose(turned_q[turned_rows, here]) * score_scale).astype(bf16)

        def hidden_part(place):
            rows_here = pl.ds(pl.multiple_of(block * rows + place.start, place.size), place.size)
            part_hid[block, place] = nt(grad_packed[rows_here, packed_cols], w_in[...]).astype(bf16)
        tiles(rows, 256, hidden_part)
        send_part(block)

        def input_part(tile, held):
            cols = pl.ds(pl.multiple_of(tile * 256, 256), 256)
            value = tn(normed_all[here, cols], grad_packed[here, packed_cols])
            if block == 0:
                sum_in[cols, packed_cols] = value
            else:
                sum_in[cols, packed_cols] = sum_in[cols, packed_cols] + value
            return held
        lax.fori_loop(0, width // 256, input_part, 0)

    self_comm = {
        0: lambda: (reduce_low(0), reduce_low(1), reduce_low(2), reduce_high(3), reduce_far(5)),
        1: lambda: (forward_part(0), reduce_far(4), reduce_high(0), reduce_last(5)),
        2: lambda: (forward_part(1), reduce_high(1), reduce_high(2), reduce_far(3), reduce_last(4)),
        3: lambda: (forward_part(2), forward_part(3))}
    for block in range(sq):
        key_step(block)
        self_comm[block]()

    def gi_copy(peer, slot):
        return remote(grad_in.at[peer], grad_in_got.at[slot], gi_s.at[peer], gi_r.at[slot], (peer, me_sq))

    many_rows = [(place, place * strip) for place in range(dp)]
    for place, start in many_rows:
        grad_in[place] = sum_in[start:start + strip, packed_cols].astype(bf16)
    many(dp - 1, lambda k: gi_copy(other_dp(k), me_dp).start())
    grad_in_got[me_dp] = grad_in[me_dp]

    for peer in (pair, far, cross):
        gm_copy(peer, peer).wait_recv()
    part_mem_got[me_sq] = part_mem[me_sq]
    grad_memory_ref[...] = (part_mem_got[0].astype(f32) + part_mem_got[1].astype(f32)) + (part_mem_got[2].astype(f32) + part_mem_got[3].astype(f32))
    reduce_far(0)
    reduce_far(1)
    reduce_far(2)
    reduce_last(3)

    yp_copy(me_sq).wait_recv()
    yf_copy(me_sq, 0).wait_recv()
    yf_copy(me_sq, 1).wait_recv()

    def last_step(here):
        grad_normed = part_hid[me_sq, here].astype(f32) + pair_got[here].astype(f32) + far_got[here].astype(f32)
        unit, inverse = unit_rows(hidden_ref[here].astype(f32))
        add_sum(0, grad_normed * unit)
        add_sum(1, grad_normed)
        grad_hidden_ref[here] = grad_res[here] + norm_back(grad_normed, unit, inverse, gain_one)
    tiles(rows, 256, last_step)

    for peer in (far, cross, pair):
        s1_copy(peer, me_sq).start()
    many(dp - 1, lambda k: gi_copy(other_dp(k), other_dp(k)).wait_recv())
    total_in = grad_in_got[0].astype(f32)
    for place in range(1, dp):
        total_in = total_in + grad_in_got[place].astype(f32)

    def go_copy(part, owner, peer):
        there = out_si.at[:, pl.ds(pl.multiple_of(part * width + owner * LANES, LANES), LANES)]
        return remote(there, there, go_s.at[part, peer], go_r.at[part, owner], (me_dp, peer))
    for part in range(3):
        out_si[:, pl.ds(pl.multiple_of(part * width + me_sq * LANES, LANES), LANES)] = total_in[:, part * LANES:(part + 1) * LANES]
    for peer in (far, cross, pair):
        for part in range(3):
            go_copy(part, me_sq, peer).start()
    for peer in (far, cross, pair):
        s1_copy(peer, peer).wait_recv()
    sums_seq[me_sq] = sums[...]
    last_sums[...] = (sums_seq[0] + sums_seq[1]) + (sums_seq[2] + sums_seq[3])

    def v_copy(peer, slot):
        return remote(last_sums, sums_dp.at[slot], s2_s.at[peer], s2_r.at[slot], (peer, me_sq))
    many(dp - 1, lambda k: v_copy(other_dp(k), me_dp).start())
    sums_dp[me_dp] = last_sums[...]
    for index in (0, 1, 2):
        reduce_last(index)
    many(dp - 1, lambda k: v_copy(other_dp(k), other_dp(k)).wait_recv())
    out_vec[...] = sums_dp[0]

    def add_vec(place, carry):
        out_vec[...] = out_vec[...] + sums_dp[place]
        return carry
    lax.fori_loop(1, dp, add_vec, 0)
    for index in range(6):
        reduce_end(index)
    for peer in (far, cross, pair):
        for part in range(3):
            go_copy(part, peer, peer).wait_recv()
    for index in range(6):
        reduce_drain(index)
    for peer in (far, cross, pair):
        da_copy(peer, me_sq).wait_send()
        gm_copy(peer, me_sq).wait_send()
        s1_copy(peer, me_sq).wait_send()
        for part in range(3):
            go_copy(part, me_sq, peer).wait_send()
    many(dp - 1, lambda k: gi_copy(other_dp(k), me_dp).wait_send())
    many(dp - 1, lambda k: v_copy(other_dp(k), me_dp).wait_send())
    yp_copy(pair).wait_send()
    for block in range(sq):
        @pl.when(away(block))
        def _():
            yh_copy(block).wait_send()
            yf_copy(block, half).wait_send()
    for copy in (hid_far, hid_pair, mem_far, mem_pair_copy, mem_next):
        copy.wait_send()
    many(dp - 1, lambda k: vec_copy(other_dp(k), me_dp).wait_send())
    many(dp - 1, lambda k: [in_copy(part, other_dp(k), me_dp).wait_send() for part in range(3)])
    for peer in (pair, far, cross):
        att_copy(peer, me_sq).wait_send()


def whole_specs(names):
    return [pl.BlockSpec(memory_space=name) for name in names]


def run_layer(sizes, args):
    dp, sq, rows, mem_rows, width, inner = sizes
    seq_rows, all_mem = rows * sq, mem_rows * sq
    high, strip, big = dp // 2, width // dp, inner // dp
    V, A, S = pltpu.VMEM, pl.ANY, pltpu.SMEM
    dma = pltpu.SemaphoreType.DMA
    shard_shapes = [(strip, 2 * width), (strip, width), (strip, width), (strip, width), (strip, inner), (big, width)]
    outs = [((rows, width), bf16), ((1, rows), f32), ((rows, width), f32), ((mem_rows, width), f32),
            ((strip, 3 * width), f32)] + [(shape, f32) for shape in shard_shapes] + [((16, width), f32)]
    scratch = [((width, 2 * width), bf16), ((width, width), bf16), ((width, width), bf16), ((width, width), bf16),
               ((width, inner), bf16), ((inner, width), bf16), ((8, width), f32), ((1, inner), f32),
               ((rows, width), f32), ((rows, width), f32), ((rows, width), bf16), ((rows, width), bf16),
               ((rows, width), bf16), ((all_mem, 2 * width), bf16), ((8, rows), f32), ((rows, width), bf16),
               ((seq_rows, LANES), bf16), ((seq_rows, LANES), bf16), ((seq_rows, LANES), bf16), ((8, seq_rows), f32),
               ((width, 3 * LANES), bf16), ((sq, rows, width), bf16), ((all_mem, width), bf16),
               ((dp, 16, LANES), bf16), ((seq_rows, width), bf16), ((seq_rows, LANES), bf16),
               ((rows, width), bf16), ((inner // 512, rows, 512), bf16), ((inner // 512, rows, 512), bf16), ((256, inner), f32),
               ((rows, width), bf16), ((rows, width), bf16), ((rows, width), bf16), ((8, rows), f32),
               ((seq_rows, LANES), bf16),
               ((dp, strip, 3 * LANES), bf16), ((dp, strip, 3 * LANES), bf16),
               ((sq, mem_rows, width), bf16), ((sq, mem_rows, width), bf16),
               ((2, rows // 2, width), bf16), ((rows, width), bf16), ((rows, width), bf16),
               ((16, width), f32), ((sq, 16, width), f32), ((dp, 16, width), f32), ((16, width), f32), ((8, LANES), f32), ((8, LANES), f32)]
    scratch += [((high, 2, size, columns), bf16) for size, columns in shard_shapes]
    scratch += [((high, 2, size, columns // 2), bf16) for size, columns in shard_shapes]
    scratch += [((high, size, columns // 2), bf16) for size, columns in shard_shapes]
    scratch += [((high, size, columns // 2), bf16) for size, columns in shard_shapes]
    scratch += [((size, columns // 2), f32) for size, columns in shard_shapes]
    scratch += [((size, columns // 2), f32) for size, columns in shard_shapes]
    semaphores = [dma((12,)), dma((3,)), dma((sq,)), dma((3,)), dma((sq,)), dma((dp,)), dma((dp,)), dma((3, dp)), dma((3, dp)),
                  dma((6, high)), dma((6, high)), dma((6, high)), dma((6, high)), dma((6,)), dma((6,)), dma((sq,)), dma((sq,)),
                  dma((6,)), dma((6,)), dma((6,)), dma((6,)), dma((6, high)), dma((6, high)), dma((6,)), dma((6,)), dma((6,)), dma((6,)),
                  dma((dp,)), dma((dp,)), dma((3, sq)), dma((3, sq)), dma((sq,)), dma((sq,)), dma((sq,)), dma((sq,)),
                  dma((sq,)), dma((sq,)), dma((sq,)), dma((2,)), dma((1,)), dma((1,)),
                  dma((sq,)), dma((sq,)), dma((dp,)), dma((dp,)), dma((1,)), dma((1,)), dma((1,)), dma((1,))]
    return pl.pallas_call(
        functools.partial(layer_kernel, sizes),
        out_shape=[jax.ShapeDtypeStruct(*out) for out in outs],
        in_specs=whole_specs([S, S, V, V, V, V, V, A, A, A, A, A, A, A]),
        out_specs=whole_specs([V] * len(outs)),
        scratch_shapes=[pltpu.VMEM(*item) for item in scratch] + semaphores,
        compiler_params=pltpu.CompilerParams(collective_id=0, has_side_effects=True, vmem_limit_bytes=62 << 20),
        name="layer",
    )(*args)


def shards(hidden_in, memory, lengths, memory_lengths, self_in, self_out, cross_query, cross_memory, cross_out,
           ffn_in, ffn_bias, ffn_out, out_bias, gain_self, shift_self, gain_cross, shift_cross, gain_ffn, shift_ffn,
           exit_weight, grad_result, grad_halting):
    dp = lax.axis_size("dp")
    sq = lax.axis_size("seq")
    rows, width = hidden_in.shape
    mem_rows = memory.shape[0]
    inner = ffn_in.shape[1]
    sizes = (dp, sq, rows, mem_rows, width, inner)
    strip = width // dp
    big = inner // dp
    piece = min(big, LANES)
    vectors = jnp.stack([gain_self, shift_self, gain_cross, shift_cross, gain_ffn, shift_ffn, out_bias, exit_weight])
    packed_vec = jnp.concatenate([
        jnp.pad(vectors, ((0, 0), (0, LANES - strip))),
        jnp.pad(ffn_bias.reshape(big // piece, piece), ((0, 8 - big // piece), (0, LANES - piece)))])
    (result, halting, grad_hidden, grad_memory, out_si, out_cm, out_so, out_cq, out_co, out_fi, out_fo, out_vec) = run_layer(
        sizes, (lengths, memory_lengths, hidden_in, memory, packed_vec, grad_result, grad_halting.reshape(1, rows), self_in,
                cross_memory, self_out, cross_query, cross_out, ffn_in, ffn_out))
    place = lax.axis_index("dp")
    small = lax.dynamic_slice_in_dim(out_vec[:8], place * strip, strip, 1)
    grad_bias = lax.dynamic_slice_in_dim(out_vec[8:8 + inner // width].reshape(inner), place * big, big, 0)
    return (result, halting.reshape(rows), grad_hidden, grad_memory, out_si, out_so, out_cq, out_cm, out_co, out_fi,
            grad_bias, out_fo, small[6], small[0], small[1], small[2], small[3], small[4], small[5], small[7])


def solution(mesh):
    both = P(("dp", "seq"), None)
    matrix = P("dp", None)
    vector = P("dp")
    return jax.shard_map(
        shards,
        mesh=mesh,
        in_specs=(both, both, vector, vector, matrix, matrix, matrix, matrix, matrix, matrix, vector, matrix)
        + (vector,) * 8 + (both, P(("dp", "seq"))),
        out_specs=(both, P(("dp", "seq")), both, both) + (matrix,) * 6 + (vector, matrix) + (vector,) * 8,
        check_vma=False,
    )
```

```python
import functools
import jax
import jax.numpy as jnp
from jax import lax
from jax.experimental import pallas as pl
from jax.experimental.pallas import tpu as pltpu
from jax.sharding import PartitionSpec as P

bf16 = jnp.bfloat16
f32 = jnp.float32
i32 = jnp.int32
MESH = pl.DeviceIdType.MESH
HD = 64
LANES = 128
epsilon = 1e-05
masked_score = -1e30
gelu_scale = 0.7978845608028654
gelu_cubic = 0.044715
log2_e = 1.4426950408889634


def nn(left, right):
    return jnp.dot(left, right, preferred_element_type=f32)


def nt(left, right, precision=None):
    return lax.dot_general(
        left, right, (((1,), (1,)), ((), ())), preferred_element_type=f32, precision=precision
    )


def tn(left, right):
    return lax.dot_general(
        left, right, (((0,), (0,)), ((), ())), preferred_element_type=f32
    )


def many(count, step):
    if count <= 8:
        for index in range(count):
            step(index)
    else:
        lax.fori_loop(0, count, lambda index, carry: (step(index), carry)[1], 0)


def tiles(rows, size, step):
    lax.fori_loop(0, rows // size, lambda index, carry: (step(pl.ds(pl.multiple_of(index * size, size), size)), carry)[1], 0)


def unit_rows(value):
    average = jnp.mean(value, axis=-1, keepdims=True)
    centred = value - average
    variance = jnp.mean(centred * centred, axis=-1, keepdims=True)
    inverse = lax.rsqrt(variance + epsilon)
    return centred * inverse, inverse


def head_mask(head):
    lane = lax.broadcasted_iota(i32, (1, LANES), 1)
    return (lane < HD) == (head == 0)


def pick(value, mask):
    return jnp.where(mask, value, jnp.zeros_like(value))


def layer_kernel(sizes, *refs):
    dp, sq, rows, mem_rows, width, inner = sizes
    high = dp // 2
    strip = width // dp
    seq_rows = rows * sq
    all_mem = mem_rows * sq
    (len_ref, mlen_ref, hidden_ref, memory_ref, vec_ref, grad_ref, halt_grad_ref, self_in_ref, cross_memory_ref, self_out_ref,
     cross_query_ref, cross_out_ref, ffn_in_ref, ffn_out_ref,
     result_ref, halting_ref, grad_hidden_ref, grad_memory_ref, out_si, out_cm, out_so, out_cq, out_co, out_fi, out_fo, out_vec, out_bias,
     w_cm, w_so, w_cq, w_co, w_fi, w_fo, vec_full, bias_full, after_self, after_cross, normed_two, cross_q,
     mixed, mem_pair, cross_lse, att_tok, q_all, k_all, v_all, self_lse,
     w_in, hid_all, mem_all, vec_all, normed_all, o_heads,
     normed_three, active, grad_inner, slope, branch, cross_branch, grad_mixed, cross_delta,
     grad_heads, grad_in, grad_in_got, part_mem, part_mem_got,
     half_got, pair_got, far_got, sums, sums_seq, last_sums, vec_got, bias_got, quarter_got, last_in,
     g_cm, g_so, g_cq, g_co, g_fi, g_fo, p_cm, p_so, p_cq, p_co, p_fi, p_fo, x_cm, x_so, x_cq, x_co, x_fi, x_fo,
     h_cm, h_so, h_cq, h_co, h_fi, h_fo, f_cm, f_so, f_cq, f_co, f_fi, f_fo, y_cm, y_so, y_cq, y_co, y_fi, y_fo,
     loc_sem, hid_s, hid_r, mem_s, mem_r, vec_s, vec_r, in_s, in_r, z_s, z_r, x_s, x_r, c_s, c_r, a_s, a_r,
     gc_s, gc_r, gx_s, gx_r, gz_s, gz_r, gy_s, gy_r, gp_s, gp_r, gi_s, gi_r, go_s, go_r, gm_s, gm_r, da_s, da_r,
     w_s, w_r, gq_s, gq_r, ga_s, ga_r, yh_s, yh_r, yf_s, yf_r, yp_s, yp_r, s1_s, s1_r, s2_s, s2_r) = refs
    me_dp = lax.axis_index("dp")
    me_sq = lax.axis_index("seq")
    me_hi = me_dp // 2
    me_lo = me_dp % 2
    half = me_sq % 2
    pair = me_sq + 1 - 2 * half
    far = (me_sq + 2) % sq
    cross = (pair + 2) % sq
    shards = (cross_memory_ref, self_out_ref, cross_query_ref, cross_out_ref, ffn_in_ref, ffn_out_ref)
    wholes = (w_cm, w_so, w_cq, w_co, w_fi, w_fo)

    def remote(src, dst, send, recv, device):
        return pltpu.make_async_remote_copy(src_ref=src, dst_ref=dst, send_sem=send, recv_sem=recv, device_id=device, device_id_type=MESH)

    def other_dp(step):
        return (me_dp + 1 + step) % dp

    barrier = pltpu.get_barrier_semaphore()
    many(dp - 1, lambda k: pl.semaphore_signal(barrier, inc=1, device_id=(other_dp(k), me_sq), device_id_type=MESH))
    for peer in (pair, far, cross):
        pl.semaphore_signal(barrier, inc=1, device_id=(me_dp, peer), device_id_type=MESH)
    pl.semaphore_wait(barrier, dp - 1 + 3)

    def slab_copy(src, dst_all, slab, send, recv, peer):
        return remote(src, dst_all.at[slab], send, recv.at[slab], (me_dp, peer))

    def mem_slab(slab):
        return mem_all.at[pl.ds(pl.multiple_of(slab * mem_rows, mem_rows), mem_rows)]

    def mem_copy(src, slab, send, peer):
        return remote(src, mem_slab(slab), send, mem_r.at[slab], (me_dp, peer))

    own_hidden = pltpu.make_async_copy(hidden_ref, hid_all.at[me_sq], loc_sem.at[0])
    own_memory = pltpu.make_async_copy(memory_ref, mem_slab(me_sq), loc_sem.at[1])
    hid_far = slab_copy(hidden_ref, hid_all, me_sq, hid_s.at[1], hid_r, far)
    hid_pair = slab_copy(hidden_ref, hid_all, me_sq, hid_s.at[0], hid_r, pair)
    mem_far = mem_copy(memory_ref, me_sq, mem_s.at[1], far)
    mem_pair_copy = mem_copy(memory_ref, me_sq, mem_s.at[0], pair)
    hid_next = slab_copy(hid_all.at[far], hid_all, far, hid_s.at[2], hid_r, pair)
    mem_next = mem_copy(mem_slab(far), far, mem_s.at[2], pair)

    def vec_copy(peer, slot):
        return remote(vec_ref, vec_all.at[slot], vec_s.at[peer], vec_r.at[slot], (peer, me_sq))

    def in_copy(part, peer, slot):
        return remote(
            self_in_ref.at[:, pl.ds(pl.multiple_of(part * width + me_sq * LANES, LANES), LANES)],
            w_in.at[pl.ds(pl.multiple_of(slot * strip, strip), strip), pl.ds(part * LANES, LANES)],
            in_s.at[part, peer], in_r.at[part, slot], (peer, me_sq))

    own_vec = pltpu.make_async_copy(vec_ref, vec_all.at[me_dp], loc_sem.at[2])
    own_in = [pltpu.make_async_copy(
        self_in_ref.at[:, pl.ds(pl.multiple_of(part * width + me_sq * LANES, LANES), LANES)],
        w_in.at[pl.ds(pl.multiple_of(me_dp * strip, strip), strip), pl.ds(part * LANES, LANES)],
        loc_sem.at[3 + part]) for part in range(3)]

    hid_far.start()
    hid_pair.start()
    many(dp - 1, lambda k: vec_copy(other_dp(k), me_dp).start())
    many(dp - 1, lambda k: [in_copy(part, other_dp(k), me_dp).start() for part in range(3)])
    own_hidden.start()
    own_memory.start()
    own_vec.start()
    for copy in own_in:
        copy.start()

    def half_columns(index, side):
        size = shards[index].shape[1] // 2
        return pl.ds(pl.multiple_of(side * size, LANES), size)

    def columns(index):
        if index != 4:
            return half_columns(index, half)
        size = shards[index].shape[1] // 4
        return pl.ds(pl.multiple_of((half * 2 + me_sq // 2) * size, LANES), size)

    def block_rows(index, slot):
        size = shards[index].shape[0]
        return pl.ds(pl.multiple_of(slot * size, size), size)

    def z_copy(index, peer, slot):
        return remote(shards[index].at[:, columns(index)], wholes[index].at[block_rows(index, slot * 2 + me_lo), columns(index)],
                      z_s.at[index, peer], z_r.at[index, slot], (peer * 2 + me_lo, me_sq))

    def x_copy(index, slot, low, own):
        there = wholes[index].at[block_rows(index, slot * 2 + low), columns(index)]
        src = shards[index].at[:, columns(index)] if own else there
        return remote(src, there, x_s.at[index, slot], x_r.at[index, slot], (me_hi * 2 + 1 - me_lo, me_sq))

    def c_copy(index):
        there = wholes[index].at[:, half_columns(index, half)]
        return remote(there, there, c_s.at[index], c_r.at[index], (me_dp, pair))

    def c_wait(index):
        there = wholes[index].at[:, half_columns(index, 1 - half)]
        remote(there, there, c_s.at[index], c_r.at[index], (me_dp, pair)).wait_recv()

    def w_copy(index, block):
        there = wholes[index].at[block_rows(index, block), columns(index)]
        return remote(there, there, w_s.at[index - 4, block], w_r.at[index - 4, block], (me_dp, far))

    def w_wait(index, block):
        size = shards[index].shape[1] // 4
        there = wholes[index].at[block_rows(index, block), pl.ds(pl.multiple_of((half * 2 + far // 2) * size, LANES), size)]
        remote(there, there, w_s.at[index - 4, block], w_r.at[index - 4, block], (me_dp, far)).wait_recv()

    def own_copy(index):
        return pltpu.make_async_copy(shards[index].at[:, columns(index)], wholes[index].at[block_rows(index, me_dp), columns(index)], loc_sem.at[6 + index])

    def other_hi(step):
        return (me_hi + 1 + step) % high

    def own_stage(index):
        x_copy(index, me_hi, me_lo, True).start()
        own_copy(index).start()

    def first_stage(index):
        many(high - 1, lambda k: z_copy(index, other_hi(k), me_hi).start())

    def second_stage(index):
        if index == 4:
            own_copy(index).wait()
            w_copy(index, me_dp).start()

        def forward(k):
            z_copy(index, other_hi(k), other_hi(k)).wait_recv()
            x_copy(index, other_hi(k), me_lo, False).start()
            if index == 4:
                w_copy(index, other_hi(k) * 2 + me_lo).start()
        many(high - 1, forward)

    def third_stage(index):
        def arrive(k):
            x_copy(index, k, 1 - me_lo, False).wait_recv()
            if index == 4:
                w_copy(index, k * 2 + 1 - me_lo).start()
        many(high, arrive)
        if index != 4:
            own_copy(index).wait()
            c_copy(index).start()

    def fourth_stage(index):
        many(dp, lambda k: w_wait(index, k))
        c_copy(index).start()

    def finish_weight(index):
        many(high - 1, lambda k: z_copy(index, other_hi(k), me_hi).wait_send())
        many(high, lambda k: x_copy(index, k, me_lo, False).wait_send())
        if index == 4:
            many(dp, lambda k: w_copy(index, k).wait_send())
        c_copy(index).wait_send()

    for index in (1, 2, 0, 4, 5, 3):
        own_stage(index)

    own_vec.wait()
    many(dp - 1, lambda k: vec_copy(other_dp(k), other_dp(k)).wait_recv())
    vec_full[...] = jnp.zeros_like(vec_full)
    bias_full[...] = jnp.zeros_like(bias_full)
    lane_k = lax.broadcasted_iota(i32, (LANES, width), 0)
    lane_j = lax.broadcasted_iota(i32, (LANES, width), 1)
    big = inner // dp
    piece = min(big, LANES)
    big_k = lax.broadcasted_iota(i32, (LANES, inner), 0)
    big_j = lax.broadcasted_iota(i32, (LANES, inner), 1)

    def place(slot):
        hot = ((lane_j - slot * strip == lane_k) & (lane_k < strip)).astype(f32).astype(bf16)
        vec_full[...] = vec_full[...] + nn(vec_all[slot], hot)[:8]
        for part in range(big // piece):
            wide = ((big_j - slot * big - part * piece == big_k) & (big_k < piece)).astype(f32).astype(bf16)
            bias_full[...] = bias_full[...] + nn(vec_all[slot], wide)[8 + part:9 + part]
    lax.fori_loop(0, dp, lambda slot, carry: (place(slot), carry)[1], 0)
    gain_one, shift_one = vec_full[0:1], vec_full[1:2]
    gain_two, shift_two = vec_full[2:3], vec_full[3:4]

    def norm_slab(slab):
        def step(place_rows):
            unit, _ = unit_rows(hid_all[slab, place_rows].astype(f32))
            start = pl.multiple_of(slab * rows + place_rows.start, place_rows.size)
            normed_all[pl.ds(start, place_rows.size)] = (unit * gain_one + shift_one).astype(bf16)
        tiles(rows, 256, step)

    def project_slab(slab):
        def step(place_rows):
            here = pl.ds(pl.multiple_of(slab * rows + place_rows.start, place_rows.size), place_rows.size)
            packed = nn(normed_all[here], w_in[...]).astype(bf16)
            q_all[here] = packed[:, :LANES]
            k_all[here] = packed[:, LANES:2 * LANES]
            v_all[here] = packed[:, 2 * LANES:]
        tiles(rows, 256, step)

    own_hidden.wait()
    norm_slab(me_sq)
    hid_pair_in = slab_copy(hid_all.at[pair], hid_all, pair, hid_s.at[0], hid_r, pair)
    hid_pair_in.wait_recv()
    norm_slab(pair)
    for copy in own_in:
        copy.wait()
    many(dp - 1, lambda k: [in_copy(part, other_dp(k), other_dp(k)).wait_recv() for part in range(3)])
    for index in (1, 2, 0, 4, 5, 3):
        first_stage(index)
    project_slab(me_sq)
    project_slab(pair)
    slab_copy(hid_all.at[far], hid_all, far, hid_s.at[1], hid_r, far).wait_recv()
    hid_next.start()
    mem_far.start()
    mem_pair_copy.start()
    norm_slab(far)
    project_slab(far)
    slab_copy(hid_all.at[cross], hid_all, cross, hid_s.at[2], hid_r, pair).wait_recv()
    norm_slab(cross)
    project_slab(cross)

    limit = len_ref[0]
    mem_limit = mlen_ref[0]
    scale = HD ** (-0.5) * log2_e

    def softmax_block(scores, values):
        largest = jnp.max(scores, axis=1, keepdims=True)
        powers = jnp.exp2(scores - largest)
        total = jnp.sum(powers, axis=1, keepdims=True)
        return nn(powers.astype(bf16), values) / total, largest + jnp.log2(total)

    def att_copy(block, owner):
        return remote(o_heads.at[pl.ds(pl.multiple_of(block * rows, rows), rows)],
                      att_tok.at[:, pl.ds(pl.multiple_of(owner * LANES, LANES), LANES)],
                      a_s.at[block], a_r.at[owner], (me_dp, block))

    def self_block(block):
        here = pl.ds(block * rows, rows)
        query = q_all[here]
        head_queries = [pick(query, head_mask(head)) for head in range(2)]

        def key_part(index, carry, diagonal):
            there = pl.ds(pl.multiple_of(index * rows, rows), rows)
            place = index * rows + lax.broadcasted_iota(i32, (1, rows), 1)
            bias = jnp.where(place < limit, 0.0, masked_score)
            held = []
            for head in range(2):
                largest, total, out = carry[3 * head:3 * head + 3]
                scores = nt(head_queries[head], k_all[there]) * scale + bias
                if diagonal:
                    scores = jnp.where(lax.broadcasted_iota(i32, (rows, rows), 1) <= lax.broadcasted_iota(i32, (rows, rows), 0), scores, masked_score)
                higher = jnp.maximum(largest, jnp.max(scores, axis=1, keepdims=True))
                powers = jnp.exp2(scores - higher)
                shrink = jnp.exp2(largest - higher)
                total = total * shrink + jnp.sum(powers, axis=1, keepdims=True)
                held += [higher, total, out * shrink + nn(powers.astype(bf16), v_all[there])]
            return tuple(held)

        carry = (jnp.full((rows, 1), -3e38, f32), jnp.zeros((rows, 1), f32), jnp.zeros((rows, LANES), f32)) * 2
        if block:
            carry = lax.fori_loop(0, block, lambda index, held: key_part(index, held, False), carry)
        carry = key_part(block, carry, True)
        outs = [carry[3 * head + 2] / carry[3 * head + 1] for head in range(2)]
        spreads = [carry[3 * head] + jnp.log2(carry[3 * head + 1]) for head in range(2)]
        o_heads[here] = jnp.where(head_mask(0), outs[0], outs[1]).astype(bf16)
        turned = jnp.transpose(jnp.where(head_mask(0), spreads[0], spreads[1]))
        self_lse[0:1, here] = turned[0:1]
        self_lse[1:2, here] = turned[HD:HD + 1]

        @pl.when(me_sq != block)
        def _():
            att_copy(block, me_sq).start()

    def forward_memory():
        mem_copy(mem_slab(far), far, mem_s.at[1], far).wait_recv()
        mem_next.start()

    comm_steps = {3: lambda: (forward_memory(), second_stage(1), second_stage(2)), 2: lambda: second_stage(0),
                  1: lambda: second_stage(4), 0: lambda: (third_stage(1), third_stage(2), second_stage(5))}
    for block in range(sq - 1, -1, -1):
        self_block(block)
        comm_steps[block]()
    third_stage(0)
    third_stage(4)
    att_tok[:, pl.ds(pl.multiple_of(me_sq * LANES, LANES), LANES)] = o_heads[pl.ds(pl.multiple_of(me_sq * rows, rows), rows)]

    own_memory.wait()
    mem_copy(mem_slab(pair), pair, mem_s.at[0], pair).wait_recv()
    mem_copy(mem_slab(cross), cross, mem_s.at[2], pair).wait_recv()
    c_wait(0)

    def project_memory(slab, carry):
        place = pl.ds(pl.multiple_of(slab * mem_rows, mem_rows), mem_rows)
        mem_pair[place] = nn(mem_all[place], w_cm[...]).astype(bf16)
        return carry
    lax.fori_loop(0, sq, project_memory, 0)

    for peer in (pair, far, cross):
        att_copy(peer, peer).wait_recv()
    c_wait(1)
    c_wait(2)

    def step_two(here):
        value = hidden_ref[here].astype(f32) + nn(att_tok[here], w_so[...])
        after_self[here] = value
        unit, _ = unit_rows(value)
        normed = (unit * gain_two + shift_two).astype(bf16)
        normed_two[here] = normed
        cross_q[here] = nn(normed, w_cq[...]).astype(bf16)
    tiles(rows, 256, step_two)

    mem_bias = jnp.where(lax.broadcasted_iota(i32, (1, all_mem), 1) < mem_limit, 0.0, masked_score)

    def cross_pair(number, held):
        lanes = pl.ds(pl.multiple_of(number * LANES, LANES), LANES)
        value_lanes = pl.ds(pl.multiple_of(width + number * LANES, LANES), LANES)
        query = cross_q[:, lanes]
        outs, spreads = [], []
        for head in range(2):
            scores = nt(pick(query, head_mask(head)), mem_pair[:, lanes]) * scale + mem_bias
            out, spread = softmax_block(scores, mem_pair[:, value_lanes])
            outs.append(out)
            spreads.append(spread)
        mixed[:, lanes] = jnp.where(head_mask(0), outs[0], outs[1]).astype(bf16)
        turned = jnp.transpose(jnp.where(head_mask(0), spreads[0], spreads[1]))
        cross_lse[pl.ds(2 * number, 1)] = turned[0:1]
        cross_lse[pl.ds(2 * number + 1, 1)] = turned[HD:HD + 1]
        return held

    pairs = width // LANES
    second_stage(3)
    lax.fori_loop(0, 2, cross_pair, 0)
    third_stage(5)
    third_stage(3)
    fourth_stage(4)
    lax.fori_loop(2, pairs, cross_pair, 0)
    c_wait(3)

    def step_three(here):
        after_cross[here] = after_self[here] + nn(mixed[here], w_co[...])
    tiles(rows, 256, step_three)

    c_wait(4)
    c_wait(5)
    gain_three, shift_three, outer_bias, exit_row = vec_full[4:5], vec_full[5:6], vec_full[6:7], vec_full[7:8]
    parts = ((g_cm, p_cm, x_cm, h_cm, f_cm, y_cm, out_cm), (g_so, p_so, x_so, h_so, f_so, y_so, out_so),
             (g_cq, p_cq, x_cq, h_cq, f_cq, y_cq, out_cq), (g_co, p_co, x_co, h_co, f_co, y_co, out_co),
             (g_fi, p_fi, x_fi, h_fi, f_fi, y_fi, out_fi), (g_fo, p_fo, x_fo, h_fo, f_fo, y_fo, out_fo))
    chunk = 512

    def norm_back(grad, unit, inverse, gain):
        scaled = grad * gain
        first = jnp.mean(scaled, axis=-1, keepdims=True)
        second = jnp.mean(scaled * unit, axis=-1, keepdims=True)
        return inverse * (scaled - first - unit * second)

    def add_sum(index, value):
        sums[index:index + 1] = sums[index:index + 1] + jnp.sum(value, axis=0, keepdims=True)

    def gc_copy(index):
        size = shards[index].shape[1] // 2
        other = pl.ds(pl.multiple_of((1 - half) * size, LANES), size)
        return remote(parts[index][0].at[:, :, :, other], parts[index][1], gc_s.at[index], gc_r.at[index], (me_dp, pair))

    def gq_copy():
        return remote(parts[5][1].at[:, :, :, part_columns(5, far // 2)], quarter_got, gq_s.at[0], gq_r.at[0], (me_dp, far))

    def ga_copy(owner, peer):
        size = shards[5].shape[1] // 4
        there = out_fo.at[:, pl.ds(pl.multiple_of((owner % 2 * 2 + owner // 2) * size, LANES), size)]
        return remote(there, there, ga_s.at[peer], ga_r.at[owner], (me_dp, peer))

    def gx_copy(index):
        src = parts[index][1].at[:, 1 - me_lo, :, part_columns(index, me_sq // 2)] if index == 5 else parts[index][1].at[:, 1 - me_lo]
        return remote(src, parts[index][2], gx_s.at[index], gx_r.at[index], (me_hi * 2 + 1 - me_lo, me_sq))

    def gz_copy(index, peer, slot):
        return remote(parts[index][2].at[peer], parts[index][3].at[slot], gz_s.at[index, peer], gz_r.at[index, slot], (peer * 2 + me_lo, me_sq))

    def gy_copy(index):
        return remote(parts[index][4], parts[index][5], gy_s.at[index], gy_r.at[index], (me_dp, far))

    def gp_copy(index, side):
        size = shards[index].shape[1] // 2
        there = parts[index][6].at[:, pl.ds(pl.multiple_of(side * size, LANES), size)]
        return remote(there, there, gp_s.at[index], gp_r.at[index], (me_dp, pair))

    def reduce_pair(index):
        gc_copy(index).start()

    def reduce_low(index):
        gc_copy(index).wait_recv()
        whole_ref, part_ref = parts[index][0], parts[index][1]

        def add(place, carry):
            for low in range(2):
                part_ref[place, low] = (part_ref[place, low].astype(f32) + whole_ref[place, low, :, half_columns(index, half)].astype(f32)).astype(bf16)
            return carry
        lax.fori_loop(0, high, add, 0)
        if index == 5:
            gq_copy().start()
        else:
            gx_copy(index).start()

    def part_columns(index, side):
        size = shards[index].shape[1] // 4
        return pl.ds(pl.multiple_of(side * size, LANES), size)

    def reduce_across(index):
        gq_copy().wait_recv()
        part_ref = parts[index][1]

        def add(place, carry):
            for low in range(2):
                mine = part_columns(index, me_sq // 2)
                part_ref[place, low, :, mine] = (part_ref[place, low, :, mine].astype(f32) + quarter_got[place, low].astype(f32)).astype(bf16)
            return carry
        lax.fori_loop(0, high, add, 0)
        gx_copy(index).start()

    def reduce_high(index):
        gx_copy(index).wait_recv()
        part_ref, low_ref = parts[index][1], parts[index][2]

        def add(place, carry):
            mine = part_ref[place, me_lo, :, part_columns(index, me_sq // 2)] if index == 5 else part_ref[place, me_lo]
            low_ref[place] = (low_ref[place].astype(f32) + mine.astype(f32)).astype(bf16)
            return carry
        lax.fori_loop(0, high, add, 0)
        many(high - 1, lambda k: gz_copy(index, other_hi(k), me_hi).start())

    def reduce_far(index):
        low_ref, high_ref, far_ref = parts[index][2], parts[index][3], parts[index][4]
        high_ref[me_hi] = low_ref[me_hi]
        many(high - 1, lambda k: gz_copy(index, other_hi(k), other_hi(k)).wait_recv())
        def add(place, held):
            return held + high_ref[place].astype(f32)
        total = lax.fori_loop(1, high, add, high_ref[0].astype(f32))
        far_ref[...] = total if index == 5 else total.astype(bf16)
        if index == 5:
            size = shards[index].shape[1] // 4
            parts[index][6][:, pl.ds(pl.multiple_of((half * 2 + me_sq // 2) * size, LANES), size)] = far_ref[...]
            for peer in (far, cross, pair):
                ga_copy(me_sq, peer).start()
        else:
            gy_copy(index).start()

    def reduce_last(index):
        far_ref, got_ref, out_ref = parts[index][4], parts[index][5], parts[index][6]
        gy_copy(index).wait_recv()
        out_ref[:, half_columns(index, half)] = far_ref[...].astype(f32) + got_ref[...].astype(f32)
        gp_copy(index, half).start()

    def reduce_end(index):
        if index == 5:
            for peer in (far, cross, pair):
                ga_copy(peer, peer).wait_recv()
        else:
            gp_copy(index, 1 - half).wait_recv()

    def reduce_drain(index):
        gc_copy(index).wait_send()
        gx_copy(index).wait_send()
        many(high - 1, lambda k: gz_copy(index, other_hi(k), me_hi).wait_send())
        if index == 5:
            gq_copy().wait_send()
            for peer in (far, cross, pair):
                ga_copy(me_sq, peer).wait_send()
        else:
            gy_copy(index).wait_send()
            gp_copy(index, half).wait_send()

    def weight_grad(index, left, rights):
        out_ref = parts[index][0]
        size = shards[index].shape[0]
        pieces = max(1, 256 // size)

        def step(tile, carry):
            features = left(tile)
            for number, right in enumerate(rights):
                value = tn(features, right())
                span = min(size, 256)
                cols = pl.ds(number * value.shape[1], value.shape[1])
                for piece in range(pieces):
                    place = tile * pieces + piece
                    out_ref[place // 2, place % 2, :, cols] = value[piece * span:(piece + 1) * span].astype(bf16)
            return carry
        lax.fori_loop(0, size * dp // 256, step, 0)

    def feature_tile(ref):
        return lambda tile: ref[:, pl.ds(pl.multiple_of(tile * 256, 256), 256)]

    hid_next.wait_send()
    for index in range(6):
        finish_weight(index)
    grad_res = grad_hidden_ref
    grad_packed, sum_in, turned_q = w_fo, after_cross, slope
    packed_cols = pl.ds(0, 3 * LANES)
    turned_rows = pl.ds(0, LANES)
    sums[...] = jnp.zeros_like(sums)
    halting_ref[...] = jnp.zeros_like(halting_ref)

    def ffn_step(here):
        size = here.size
        unit, inverse = unit_rows(after_cross[here])
        normed = (unit * gain_three + shift_three).astype(bf16)
        normed_three[here] = normed
        out = after_cross[here] + outer_bias
        for part in range(inner // chunk):
            cols = pl.ds(part * chunk, chunk)
            pre = nn(normed, w_fi[:, cols]) + bias_full[:, cols]
            square = pre * pre
            bent = jnp.tanh(gelu_scale * (pre + gelu_cubic * square * pre))
            act = (0.5 * pre * (1.0 + bent)).astype(bf16)
            active[part, here] = act
            slope[:, cols] = 0.5 * (1.0 + bent) + 0.5 * pre * (1.0 - bent * bent) * gelu_scale * (1.0 + 3.0 * gelu_cubic * square)
            out = out + nn(act, w_fo[cols])
        result_ref[here] = out.astype(bf16)
        halt = 1.0 / (1.0 + jnp.exp(-jnp.sum(out * exit_row, axis=-1, keepdims=True)))
        place = here.start + lax.broadcasted_iota(i32, (size, rows), 0)
        same = place == lax.broadcasted_iota(i32, (size, rows), 1)
        halting_ref[...] = halting_ref[...] + jnp.sum(jnp.where(same, halt, 0.0), axis=0, keepdims=True)
        halt_grad = jnp.sum(jnp.where(same, halt_grad_ref[...], 0.0), axis=1, keepdims=True)
        live = (me_sq * rows + here.start + lax.broadcasted_iota(i32, (size, 1), 0) < limit).astype(f32)
        grad_logit = halt_grad * live * halt * (1.0 - halt)
        add_sum(7, grad_logit * out)
        grad_out = grad_ref[here].astype(f32) * live + grad_logit * exit_row
        grad_branch = grad_out.astype(bf16)
        branch[here] = grad_branch
        add_sum(6, grad_branch.astype(f32))
        grad_normed = jnp.zeros((size, width), f32)
        for part in range(inner // chunk):
            cols = pl.ds(part * chunk, chunk)
            grad_part = (nt(grad_branch, w_fo[cols]) * slope[:, cols]).astype(bf16)
            grad_inner[part, here] = grad_part
            add_sum(8 + part, grad_part.astype(f32))
            grad_normed = grad_normed + nt(grad_part, w_fi[:, cols])
        add_sum(4, grad_normed * unit)
        add_sum(5, grad_normed)
        grad_cross = grad_out + norm_back(grad_normed, unit, inverse, gain_three)
        grad_res[here] = grad_cross
        grad_cross_branch = grad_cross.astype(bf16)
        cross_branch[here] = grad_cross_branch
        grad_mixed[here] = nt(grad_cross_branch, w_co[...]).astype(bf16)
    tiles(rows, 256, ffn_step)
    weight_grad(5, lambda tile: active[tile // 2, :, pl.ds(pl.multiple_of(tile % 2 * 256, 256), 256)], [lambda: branch[...]])
    reduce_pair(5)
    weight_grad(4, feature_tile(normed_three), [functools.partial(lambda part: grad_inner[part], part) for part in range(inner // chunk)])
    reduce_pair(4)
    weight_grad(3, feature_tile(mixed), [lambda: cross_branch[...]])
    reduce_pair(3)

    select = (lax.broadcasted_iota(i32, (8, width), 1) // HD == lax.broadcasted_iota(i32, (8, width), 0)).astype(f32)
    cross_delta[...] = nt(select, grad_mixed[...].astype(f32) * mixed[...].astype(f32), lax.Precision.HIGHEST)
    score_scale = HD ** (-0.5)

    def attend_back(keys, values, query, grad, spread_rows, delta_rows, bias, mask):
        grad_keys, grad_values, grad_query = None, None, None
        for head in range(2):
            only = head_mask(head)
            head_keys = pick(keys, only)
            scores = nt(head_keys, query) * scale + bias
            if mask is not None:
                scores = jnp.where(mask, scores, masked_score)
            powers = jnp.exp2(scores - spread_rows[head])
            grad_powers = nt(pick(values, only), grad)
            grad_scores = (powers * (grad_powers - delta_rows[head])).astype(bf16)
            value_part = nn(powers.astype(bf16), pick(grad, only))
            key_part = nn(grad_scores, pick(query, only))
            query_part = nn(jnp.transpose(head_keys), grad_scores)
            grad_values = value_part if head == 0 else grad_values + value_part
            grad_keys = key_part if head == 0 else grad_keys + key_part
            grad_query = query_part if head == 0 else grad_query + query_part
        return grad_keys, grad_values, grad_query

    key_block = 512
    key_blocks = all_mem // key_block
    grad_pair = active
    grad_cq = branch
    grad_att = normed_three
    part_hid = hid_all
    cross_comm = {0: lambda: (reduce_low(5), reduce_low(4)), 1: lambda: reduce_low(3), 2: lambda: None, 3: lambda: (reduce_across(5), reduce_high(4))}
    def cross_back(number, held):
        lanes = pl.ds(pl.multiple_of(number * LANES, LANES), LANES)
        value_lanes = pl.ds(pl.multiple_of(width + number * LANES, LANES), LANES)

        def block_step(block, total):
            here = pl.ds(pl.multiple_of(block * key_block, key_block), key_block)
            key_place = block * key_block + lax.broadcasted_iota(i32, (key_block, 1), 0)
            grad_keys, grad_values, grad_query = attend_back(
                mem_pair[here, lanes], mem_pair[here, value_lanes], cross_q[:, lanes], grad_mixed[:, lanes],
                [cross_lse[pl.ds(2 * number + head, 1)] for head in range(2)],
                [cross_delta[pl.ds(2 * number + head, 1)] for head in range(2)],
                jnp.where(key_place < mem_limit, 0.0, masked_score), None)
            grad_pair[block, :, lanes] = (grad_keys * score_scale).astype(bf16)
            grad_pair[key_blocks + block, :, lanes] = grad_values.astype(bf16)
            return total + grad_query

        total = lax.fori_loop(0, key_blocks, block_step, jnp.zeros((LANES, rows), f32))
        grad_cq[:, lanes] = (jnp.transpose(total) * score_scale).astype(bf16)
        return held

    for number in range(pairs):
        lax.fori_loop(number, number + 1, cross_back, 0)
        cross_comm[number]()

    def step_two_back(here):
        grad_normed = nt(grad_cq[here], w_cq[...])
        unit, inverse = unit_rows(after_self[here])
        add_sum(2, grad_normed * unit)
        add_sum(3, grad_normed)
        grad_self = grad_res[here] + norm_back(grad_normed, unit, inverse, gain_two)
        grad_res[here] = grad_self
        grad_self_branch = grad_self.astype(bf16)
        cross_branch[here] = grad_self_branch
        grad_att[here] = nt(grad_self_branch, w_so[...]).astype(bf16)

    tiles(rows, 256, step_two_back)

    def da_copy(peer, owner):
        return remote(grad_att.at[:, pl.ds(pl.multiple_of(peer * LANES, LANES), LANES)],
                      grad_heads.at[pl.ds(pl.multiple_of(owner * rows, rows), rows)], da_s.at[peer], da_r.at[owner], (me_dp, peer))

    for peer in (far, cross, pair):
        da_copy(peer, me_sq).start()
    grad_heads[pl.ds(pl.multiple_of(me_sq * rows, rows), rows)] = grad_att[:, pl.ds(pl.multiple_of(me_sq * LANES, LANES), LANES)]

    def gm_copy(kind):
        source, target = ((cross, pair), (pair, pair), (far, far))[kind]
        return remote(part_mem.at[source], part_mem_got.at[kind], gm_s.at[kind], gm_r.at[kind], (me_dp, target))

    def memory_pair():
        gm_copy(0).start()
        gm_copy(1).start()

    def memory_far():
        gm_copy(0).wait_recv()
        part_mem[far] = (part_mem[far].astype(f32) + part_mem_got[0].astype(f32)).astype(bf16)
        gm_copy(2).start()

    def memory_end():
        gm_copy(1).wait_recv()
        gm_copy(2).wait_recv()
        grad_memory_ref[...] = (part_mem[me_sq].astype(f32) + part_mem_got[1].astype(f32)) + part_mem_got[2].astype(f32)

    def memory_part(slab, carry):
        per_block = key_block // mem_rows
        place = pl.ds(pl.multiple_of(slab % per_block * mem_rows, mem_rows), mem_rows)
        part_mem[slab] = (nt(grad_pair[slab // per_block, place], w_cm[:, :width])
                          + nt(grad_pair[key_blocks + slab // per_block, place], w_cm[:, width:])).astype(bf16)
        return carry

    reduce_high(3)
    weight_grad(0, feature_tile(mem_all), [functools.partial(lambda part: grad_pair[part * key_blocks:(part + 1) * key_blocks].reshape(all_mem, width), part) for part in range(2)])
    reduce_pair(0)
    weight_grad(1, feature_tile(att_tok), [lambda: cross_branch[...]])
    reduce_pair(1)
    weight_grad(2, feature_tile(normed_two), [lambda: grad_cq[...]])
    reduce_pair(2)
    reduce_high(5)
    lax.fori_loop(0, sq, memory_part, 0)
    memory_pair()

    def s1_copy(peer, owner):
        return remote(sums, sums_seq.at[owner], s1_s.at[peer], s1_r.at[owner], (me_dp, peer))

    for peer in (pair, far, cross):
        da_copy(peer, peer).wait_recv()
    select_two = (lax.broadcasted_iota(i32, (8, LANES), 1) // HD == lax.broadcasted_iota(i32, (8, LANES), 0)).astype(f32)
    deltas = nt(select_two, grad_heads[...].astype(f32) * o_heads[...].astype(f32), lax.Precision.HIGHEST)
    self_lse[2:4] = deltas[0:2]
    turned_q[turned_rows] = jnp.zeros((LANES, rows * sq), f32)
    half_rows = rows // 2

    def yh_copy(block):
        there = half_got.at[block % 2]
        return remote(part_hid.at[block, pl.ds(pl.multiple_of((1 - half) * half_rows, half_rows), half_rows)], there,
                      yh_s.at[block], yh_r.at[block], (me_dp, pair))

    def yf_copy(block, side):
        return remote(part_hid.at[block, pl.ds(pl.multiple_of(half * half_rows, half_rows), half_rows)], far_got.at[pl.ds(pl.multiple_of(side * half_rows, half_rows), half_rows)],
                      yf_s.at[block], yf_r.at[side], (me_dp, block))

    def yp_copy(block):
        return remote(part_hid.at[block], pair_got, yp_s.at[0], yp_r.at[0], (me_dp, pair))

    def away(block):
        return me_sq // 2 != block // 2

    def send_part(block):
        @pl.when(away(block))
        def _():
            yh_copy(block).start()

        @pl.when(pair == block)
        def _():
            yp_copy(block).start()

    def forward_part(block):
        @pl.when(away(block))
        def _():
            yh_copy(block).wait_recv()
            place = pl.ds(pl.multiple_of(half * half_rows, half_rows), half_rows)
            part_hid[block, place] = (part_hid[block, place].astype(f32) + half_got[block % 2].astype(f32)).astype(bf16)
            yf_copy(block, half).start()

    schedule = {
        (0, 0): lambda: (reduce_low(0), memory_far()), (0, 1): lambda: (reduce_low(1), reduce_low(2), reduce_far(4)),
        (0, 2): lambda: (reduce_far(3), reduce_far(5)), (0, 3): lambda: reduce_high(0), (0, sq): lambda: (reduce_high(1), reduce_high(2)),
        (1, 1): lambda: (forward_part(0), reduce_last(4)), (1, 2): lambda: (reduce_far(0), reduce_last(3)),
        (1, sq): lambda: (reduce_far(1), reduce_far(2)), (2, 2): lambda: forward_part(1), (2, sq): lambda: reduce_last(0),
        (3, 3): lambda: (forward_part(2), reduce_last(1), reduce_last(2))}

    def comm_point(block, index):
        if (block, index) in schedule:
            schedule[block, index]()

    def gi_copy(peer, slot):
        return remote(grad_in.at[peer], grad_in_got.at[slot], gi_s.at[peer], gi_r.at[slot], (peer, me_sq))

    def input_sums():
        for place in range(dp):
            grad_in[place] = sum_in[place * strip:(place + 1) * strip, packed_cols].astype(bf16)
        many(dp - 1, lambda k: gi_copy(other_dp(k), me_dp).start())

    def key_step(block):
        here = pl.ds(block * rows, rows)
        keys, values = k_all[here], v_all[here]
        bias = jnp.where(block * rows + lax.broadcasted_iota(i32, (rows, 1), 0) < limit, 0.0, masked_score)

        def query_step(index, carry, diagonal):
            there = pl.ds(pl.multiple_of(index * rows, rows), rows)
            mask = None
            if diagonal:
                mask = lax.broadcasted_iota(i32, (rows, rows), 0) <= lax.broadcasted_iota(i32, (rows, rows), 1)
            grad_keys, grad_values, grad_query = attend_back(
                keys, values, q_all[there], grad_heads[there],
                [self_lse[head:head + 1, there] for head in range(2)],
                [self_lse[2 + head:3 + head, there] for head in range(2)], bias, mask)
            turned_q[turned_rows, there] = turned_q[turned_rows, there] + grad_query
            return carry[0] + grad_keys, carry[1] + grad_values

        zero = jnp.zeros((rows, LANES), f32)
        carry = query_step(block, (zero, zero), True)
        comm_point(block, block)
        for index in range(block + 1, sq):
            carry = lax.fori_loop(index, index + 1, lambda place, held: query_step(place, held, False), carry)
            comm_point(block, index)
        grad_packed[here, pl.ds(LANES, LANES)] = (carry[0] * score_scale).astype(bf16)
        grad_packed[here, pl.ds(2 * LANES, LANES)] = carry[1].astype(bf16)
        grad_packed[here, pl.ds(0, LANES)] = (jnp.transpose(turned_q[turned_rows, here]) * score_scale).astype(bf16)

        def input_part(tile, held):
            cols = pl.ds(pl.multiple_of(tile * 256, 256), 256)
            value = tn(normed_all[here, cols], grad_packed[here, packed_cols])
            if block == 0:
                sum_in[cols, packed_cols] = value
            else:
                sum_in[cols, packed_cols] = sum_in[cols, packed_cols] + value
            return held
        lax.fori_loop(0, width // 256, input_part, 0)
        if block == sq - 1:
            input_sums()

        def hidden_part(place):
            rows_here = pl.ds(pl.multiple_of(block * rows + place.start, place.size), place.size)
            part_hid[block, place] = nt(grad_packed[rows_here, packed_cols], w_in[...]).astype(bf16)
        tiles(rows, 256, hidden_part)
        send_part(block)

    for block in range(sq):
        key_step(block)
        comm_point(block, sq)
    grad_in_got[me_dp] = grad_in[me_dp]
    forward_part(sq - 1)

    memory_end()

    yp_copy(me_sq).wait_recv()
    yf_copy(me_sq, 0).wait_recv()
    yf_copy(me_sq, 1).wait_recv()

    def last_step(here):
        grad_normed = part_hid[me_sq, here].astype(f32) + pair_got[here].astype(f32) + far_got[here].astype(f32)
        unit, inverse = unit_rows(hidden_ref[here].astype(f32))
        add_sum(0, grad_normed * unit)
        add_sum(1, grad_normed)
        grad_hidden_ref[here] = grad_res[here] + norm_back(grad_normed, unit, inverse, gain_one)
    tiles(rows, 256, last_step)

    for peer in (far, cross, pair):
        s1_copy(peer, me_sq).start()
    many(dp - 1, lambda k: gi_copy(other_dp(k), other_dp(k)).wait_recv())
    total_in = grad_in_got[0].astype(f32)
    for place in range(1, dp):
        total_in = total_in + grad_in_got[place].astype(f32)

    def go_copy(owner, peer):
        return remote(last_in.at[owner], last_in.at[owner], go_s.at[0, peer], go_r.at[0, owner], (me_dp, peer))
    last_in[me_sq] = total_in.astype(bf16)
    for peer in (far, cross, pair):
        go_copy(me_sq, peer).start()
    for peer in (far, cross, pair):
        s1_copy(peer, peer).wait_recv()
    sums_seq[me_sq] = sums[...]
    last_sums[...] = (sums_seq[0] + sums_seq[1]) + (sums_seq[2] + sums_seq[3])

    lanes_two = max(LANES, big)

    def v_blocks(peer):
        return (last_sums.at[pl.ds(0, 8), pl.ds(pl.multiple_of(peer * strip // LANES * LANES, LANES), LANES)],
                last_sums.at[pl.ds(8, 8), pl.ds(pl.multiple_of(peer * big % width // lanes_two * lanes_two, LANES), lanes_two)])

    def v_copy(peer, slot):
        one, two = v_blocks(peer)
        return (remote(one, vec_got.at[slot], s2_s.at[0, peer], s2_r.at[0, slot], (peer, me_sq)),
                remote(two, bias_got.at[slot], s2_s.at[1, peer], s2_r.at[1, slot], (peer, me_sq)))
    many(dp - 1, lambda k: [copy.start() for copy in v_copy(other_dp(k), me_dp)])
    one, two = v_blocks(me_dp)
    vec_got[me_dp] = one[...]
    bias_got[me_dp] = two[...]
    many(dp - 1, lambda k: [copy.wait_recv() for copy in v_copy(other_dp(k), other_dp(k))])
    out_vec[...] = vec_got[0]
    out_bias[...] = bias_got[0]

    def add_vec(place, carry):
        out_vec[...] = out_vec[...] + vec_got[place]
        out_bias[...] = out_bias[...] + bias_got[place]
        return carry
    lax.fori_loop(1, dp, add_vec, 0)
    for index in range(6):
        reduce_end(index)
    for peer in (far, cross, pair):
        go_copy(peer, peer).wait_recv()
    for owner in range(sq):
        for part in range(3):
            out_si[:, part * width + owner * LANES:part * width + (owner + 1) * LANES] = last_in[owner, :, part * LANES:(part + 1) * LANES].astype(f32)
    for index in range(6):
        reduce_drain(index)
    for peer in (far, cross, pair):
        da_copy(peer, me_sq).wait_send()
        s1_copy(peer, me_sq).wait_send()
        go_copy(me_sq, peer).wait_send()
    many(dp - 1, lambda k: gi_copy(other_dp(k), me_dp).wait_send())
    many(dp - 1, lambda k: [copy.wait_send() for copy in v_copy(other_dp(k), me_dp)])
    for kind in range(3):
        gm_copy(kind).wait_send()
    yp_copy(pair).wait_send()
    for block in range(sq):
        @pl.when(away(block))
        def _():
            yh_copy(block).wait_send()
            yf_copy(block, half).wait_send()
    for copy in (hid_far, hid_pair, mem_far, mem_pair_copy, mem_next):
        copy.wait_send()
    many(dp - 1, lambda k: vec_copy(other_dp(k), me_dp).wait_send())
    many(dp - 1, lambda k: [in_copy(part, other_dp(k), me_dp).wait_send() for part in range(3)])
    for peer in (pair, far, cross):
        att_copy(peer, me_sq).wait_send()


def whole_specs(names):
    return [pl.BlockSpec(memory_space=name) for name in names]


def run_layer(sizes, args):
    dp, sq, rows, mem_rows, width, inner = sizes
    seq_rows, all_mem = rows * sq, mem_rows * sq
    high, strip, big = dp // 2, width // dp, inner // dp
    V, A, S = pltpu.VMEM, pl.ANY, pltpu.SMEM
    dma = pltpu.SemaphoreType.DMA
    shard_shapes = [(strip, 2 * width), (strip, width), (strip, width), (strip, width), (strip, inner), (big, width)]
    outs = [((rows, width), bf16), ((1, rows), f32), ((rows, width), f32), ((mem_rows, width), f32),
            ((strip, 3 * width), f32)] + [(shape, f32) for shape in shard_shapes] + [((8, LANES), f32), ((8, max(LANES, big)), f32)]
    scratch = [((width, 2 * width), bf16), ((width, width), bf16), ((width, width), bf16), ((width, width), bf16),
               ((width, inner), bf16), ((inner, width), bf16), ((8, width), f32), ((1, inner), f32),
               ((rows, width), f32), ((rows, width), f32), ((rows, width), bf16), ((rows, width), bf16),
               ((rows, width), bf16), ((all_mem, 2 * width), bf16), ((8, rows), f32), ((rows, width), bf16),
               ((seq_rows, LANES), bf16), ((seq_rows, LANES), bf16), ((seq_rows, LANES), bf16), ((8, seq_rows), f32),
               ((width, 3 * LANES), bf16), ((sq, rows, width), bf16), ((all_mem, width), bf16),
               ((dp, 16, LANES), bf16), ((seq_rows, width), bf16), ((seq_rows, LANES), bf16),
               ((rows, width), bf16), ((inner // 512, rows, 512), bf16), ((inner // 512, rows, 512), bf16), ((256, inner), f32),
               ((rows, width), bf16), ((rows, width), bf16), ((rows, width), bf16), ((8, rows), f32),
               ((seq_rows, LANES), bf16),
               ((dp, strip, 3 * LANES), bf16), ((dp, strip, 3 * LANES), bf16),
               ((sq, mem_rows, width), bf16), ((3, mem_rows, width), bf16),
               ((2, rows // 2, width), bf16), ((rows, width), bf16), ((rows, width), bf16),
               ((16, width), f32), ((sq, 16, width), f32), ((16, width), f32), ((dp, 8, LANES), f32), ((dp, 8, max(LANES, big)), f32),
               ((high, 2, big, width // 4), bf16), ((sq, strip, 3 * LANES), bf16)]
    scratch += [((high, 2, size, columns), bf16) for size, columns in shard_shapes]
    scratch += [((high, 2, size, columns // 2), bf16) for size, columns in shard_shapes]
    ways = [2] * 5 + [4]
    scratch += [((high, size, columns // way), bf16) for (size, columns), way in zip(shard_shapes, ways)] * 2
    scratch += [((size, columns // 2), bf16) for size, columns in shard_shapes[:5]] + [((big, width // 4), f32)]
    scratch += [((size, columns // 2), bf16) for size, columns in shard_shapes[:5]] + [((8, LANES), f32)]
    semaphores = [dma((12,)), dma((3,)), dma((sq,)), dma((3,)), dma((sq,)), dma((dp,)), dma((dp,)), dma((3, dp)), dma((3, dp)),
                  dma((6, high)), dma((6, high)), dma((6, high)), dma((6, high)), dma((6,)), dma((6,)), dma((sq,)), dma((sq,)),
                  dma((6,)), dma((6,)), dma((6,)), dma((6,)), dma((6, high)), dma((6, high)), dma((6,)), dma((6,)), dma((6,)), dma((6,)),
                  dma((dp,)), dma((dp,)), dma((3, sq)), dma((3, sq)), dma((sq,)), dma((sq,)), dma((sq,)), dma((sq,)),
                  dma((2, dp)), dma((2, dp)), dma((1,)), dma((1,)), dma((sq,)), dma((sq,)),
                  dma((sq,)), dma((sq,)), dma((sq,)), dma((2,)), dma((1,)), dma((1,)),
                  dma((sq,)), dma((sq,)), dma((2, dp)), dma((2, dp))]
    return pl.pallas_call(
        functools.partial(layer_kernel, sizes),
        out_shape=[jax.ShapeDtypeStruct(*out) for out in outs],
        in_specs=whole_specs([S, S, V, V, V, V, V, A, A, A, A, A, A, A]),
        out_specs=whole_specs([V] * len(outs)),
        scratch_shapes=[pltpu.VMEM(*item) for item in scratch] + semaphores,
        compiler_params=pltpu.CompilerParams(collective_id=0, has_side_effects=True, vmem_limit_bytes=62 << 20),
        name="layer",
    )(*args)


def finish_kernel(count, strip, big, width, *refs):
    sources, (vec_ref, bias_ref) = refs[:count], refs[count:count + 2]
    targets, vectors, bias_out = refs[count + 2:2 * count + 2], refs[2 * count + 2:2 * count + 10], refs[2 * count + 10]
    held, (sem_in, sem_out) = refs[2 * count + 11:-2], refs[-2:]
    loads = [pltpu.make_async_copy(sources[index], held[index], sem_in.at[index]) for index in range(count)]
    copies = [pltpu.make_async_copy(held[index], targets[index], sem_out.at[index]) for index in range(count)]
    for load in loads:
        load.start()
    for load, copy in zip(loads, copies):
        load.wait()
        copy.start()
    place = lax.axis_index("dp")
    turned = pltpu.roll(vec_ref[...], (LANES - place * strip % LANES) % LANES, 1)
    for row in range(8):
        vectors[row][...] = turned[row, :strip]
    span = bias_ref.shape[1]
    chosen = lax.broadcasted_iota(i32, (8, span), 0) == place * big // width
    line = jnp.sum(jnp.where(chosen, bias_ref[...], 0.0), axis=0, keepdims=True)
    lines = pltpu.roll(jnp.broadcast_to(line, (8, span)), (span - place * big % span) % span, 1)
    bias_out[...] = lines[0, :big]
    for copy in copies:
        copy.wait()


def run_finish(strip, big, width, arrays, vec, bias):
    count = len(arrays)
    V, A = pltpu.VMEM, pl.ANY
    shapes = [jax.ShapeDtypeStruct(array.shape, array.dtype) for array in arrays]
    shapes += [jax.ShapeDtypeStruct((strip,), f32)] * 8 + [jax.ShapeDtypeStruct((big,), f32)]
    return pl.pallas_call(
        functools.partial(finish_kernel, count, strip, big, width),
        out_shape=shapes,
        in_specs=whole_specs([A] * count + [V, V]),
        out_specs=whole_specs([A] * count + [V] * 9),
        scratch_shapes=[pltpu.VMEM(array.shape, array.dtype) for array in arrays] + [pltpu.SemaphoreType.DMA((count,))] * 2,
        name="finish",
    )(*arrays, vec, bias)


def shards(hidden_in, memory, lengths, memory_lengths, self_in, self_out, cross_query, cross_memory, cross_out,
           ffn_in, ffn_bias, ffn_out, out_bias, gain_self, shift_self, gain_cross, shift_cross, gain_ffn, shift_ffn,
           exit_weight, grad_result, grad_halting):
    dp = lax.axis_size("dp")
    sq = lax.axis_size("seq")
    rows, width = hidden_in.shape
    mem_rows = memory.shape[0]
    inner = ffn_in.shape[1]
    sizes = (dp, sq, rows, mem_rows, width, inner)
    strip = width // dp
    big = inner // dp
    piece = min(big, LANES)
    vectors = jnp.stack([gain_self, shift_self, gain_cross, shift_cross, gain_ffn, shift_ffn, out_bias, exit_weight])
    packed_vec = jnp.concatenate([
        jnp.pad(vectors, ((0, 0), (0, LANES - strip))),
        jnp.pad(ffn_bias.reshape(big // piece, piece), ((0, 8 - big // piece), (0, LANES - piece)))])
    outs = run_layer(
        sizes, (lengths, memory_lengths, hidden_in, memory, packed_vec, grad_result, grad_halting.reshape(1, rows), self_in,
                cross_memory, self_out, cross_query, cross_out, ffn_in, ffn_out))
    finished = run_finish(strip, big, width, outs[:11], outs[11], outs[12])
    (result, halting, grad_hidden, grad_memory, out_si, out_cm, out_so, out_cq, out_co, out_fi, out_fo) = finished[:11]
    small, grad_bias = finished[11:19], finished[19]
    return (result, halting.reshape(rows), grad_hidden, grad_memory, out_si, out_so, out_cq, out_cm, out_co, out_fi,
            grad_bias, out_fo, small[6], small[0], small[1], small[2], small[3], small[4], small[5], small[7])


def solution(mesh):
    both = P(("dp", "seq"), None)
    matrix = P("dp", None)
    vector = P("dp")
    return jax.shard_map(
        shards,
        mesh=mesh,
        in_specs=(both, both, vector, vector, matrix, matrix, matrix, matrix, matrix, matrix, vector, matrix)
        + (vector,) * 8 + (both, P(("dp", "seq"))),
        out_specs=(both, P(("dp", "seq")), both, both) + (matrix,) * 6 + (vector, matrix) + (vector,) * 8,
        check_vma=False,
    )
```

```python
import functools
import jax
import jax.numpy as jnp
from jax import lax
from jax.experimental import pallas as pl
from jax.experimental.pallas import tpu as pltpu
from jax.sharding import PartitionSpec as P

bf16 = jnp.bfloat16
f32 = jnp.float32
i32 = jnp.int32
MESH = pl.DeviceIdType.MESH
HD = 64
LANES = 128
epsilon = 1e-05
masked_score = -1e30
gelu_scale = 0.7978845608028654
gelu_cubic = 0.044715
log2_e = 1.4426950408889634


def nn(left, right):
    return jnp.dot(left, right, preferred_element_type=f32)


def nt(left, right, precision=None):
    return lax.dot_general(
        left, right, (((1,), (1,)), ((), ())), preferred_element_type=f32, precision=precision
    )


def tn(left, right):
    return lax.dot_general(
        left, right, (((0,), (0,)), ((), ())), preferred_element_type=f32
    )


def many(count, step):
    if count <= 8:
        for index in range(count):
            step(index)
    else:
        lax.fori_loop(0, count, lambda index, carry: (step(index), carry)[1], 0)


def tiles(rows, size, step):
    lax.fori_loop(0, rows // size, lambda index, carry: (step(pl.ds(pl.multiple_of(index * size, size), size)), carry)[1], 0)


def unit_rows(value):
    average = jnp.mean(value, axis=-1, keepdims=True)
    centred = value - average
    variance = jnp.mean(centred * centred, axis=-1, keepdims=True)
    inverse = lax.rsqrt(variance + epsilon)
    return centred * inverse, inverse


def head_mask(head):
    lane = lax.broadcasted_iota(i32, (1, LANES), 1)
    return (lane < HD) == (head == 0)


def pick(value, mask):
    return jnp.where(mask, value, jnp.zeros_like(value))


def layer_kernel(sizes, *refs):
    dp, sq, rows, mem_rows, width, inner = sizes
    high = dp // 2
    strip = width // dp
    seq_rows = rows * sq
    all_mem = mem_rows * sq
    (len_ref, mlen_ref, hidden_ref, memory_ref, vec_ref, grad_ref, halt_grad_ref, self_in_ref, cross_memory_ref, self_out_ref,
     cross_query_ref, cross_out_ref, ffn_in_ref, ffn_out_ref,
     result_ref, halting_ref, grad_hidden_ref, grad_memory_ref, out_si, out_cm, out_so, out_cq, out_co, out_fi, out_fo, out_vec, out_bias,
     w_cm, w_so, w_cq, w_co, w_fi, w_fo, vec_full, bias_full, after_self, after_cross, normed_two, cross_q,
     mixed, mem_pair, cross_lse, att_tok, q_all, k_all, v_all, self_lse,
     w_in, hid_all, mem_all, vec_all, normed_all, o_heads,
     normed_three, active, grad_inner, slope, branch, cross_branch, grad_mixed, cross_delta,
     grad_heads, grad_in, grad_in_got, part_mem, part_mem_got,
     half_got, pair_got, far_got, sums, sums_seq, last_sums, vec_got, bias_got, quarter_got, last_in,
     g_cm, g_so, g_cq, g_co, g_fi, g_fo, p_cm, p_so, p_cq, p_co, p_fi, p_fo, x_cm, x_so, x_cq, x_co, x_fi, x_fo,
     h_cm, h_so, h_cq, h_co, h_fi, h_fo, f_cm, f_so, f_cq, f_co, f_fi, f_fo, y_cm, y_so, y_cq, y_co, y_fi, y_fo,
     loc_sem, hid_s, hid_r, mem_s, mem_r, vec_s, vec_r, in_s, in_r, z_s, z_r, x_s, x_r, c_s, c_r, a_s, a_r,
     gc_s, gc_r, gx_s, gx_r, gz_s, gz_r, gy_s, gy_r, gp_s, gp_r, gi_s, gi_r, go_s, go_r, gm_s, gm_r, da_s, da_r,
     hop_s, w_s, w_r, gq_s, gq_r, ga_s, ga_r, yh_s, yh_r, yf_s, yf_r, yp_s, yp_r, s1_s, s1_r, s2_s, s2_r) = refs
    me_dp = lax.axis_index("dp")
    me_sq = lax.axis_index("seq")
    me_hi = me_dp // 2
    me_lo = me_dp % 2
    half = me_sq % 2
    pair = me_sq + 1 - 2 * half
    far = (me_sq + 2) % sq
    cross = (pair + 2) % sq
    shards = (cross_memory_ref, self_out_ref, cross_query_ref, cross_out_ref, ffn_in_ref, ffn_out_ref, ffn_out_ref)
    wholes = (w_cm, w_so, w_cq, w_co, w_fi, w_fo, w_fo)

    def remote(src, dst, send, recv, device):
        return pltpu.make_async_remote_copy(src_ref=src, dst_ref=dst, send_sem=send, recv_sem=recv, device_id=device, device_id_type=MESH)

    def other_dp(step):
        return (me_dp + 1 + step) % dp

    barrier = pltpu.get_barrier_semaphore()
    many(dp - 1, lambda k: pl.semaphore_signal(barrier, inc=1, device_id=(other_dp(k), me_sq), device_id_type=MESH))
    for peer in (pair, far, cross):
        pl.semaphore_signal(barrier, inc=1, device_id=(me_dp, peer), device_id_type=MESH)
    pl.semaphore_wait(barrier, dp - 1 + 3)

    def slab_copy(src, dst_all, slab, send, recv, peer):
        return remote(src, dst_all.at[slab], send, recv.at[slab], (me_dp, peer))

    def mem_slab(slab):
        return mem_all.at[pl.ds(pl.multiple_of(slab * mem_rows, mem_rows), mem_rows)]

    def mem_copy(src, slab, send, peer):
        return remote(src, mem_slab(slab), send, mem_r.at[slab], (me_dp, peer))

    own_hidden = pltpu.make_async_copy(hidden_ref, hid_all.at[me_sq], loc_sem.at[0])
    own_memory = pltpu.make_async_copy(memory_ref, mem_slab(me_sq), loc_sem.at[1])
    hid_far = slab_copy(hidden_ref, hid_all, me_sq, hid_s.at[1], hid_r, far)
    hid_pair = slab_copy(hidden_ref, hid_all, me_sq, hid_s.at[0], hid_r, pair)
    mem_far = mem_copy(memory_ref, me_sq, mem_s.at[1], far)
    mem_pair_copy = mem_copy(memory_ref, me_sq, mem_s.at[0], pair)
    hid_next = slab_copy(hid_all.at[far], hid_all, far, hid_s.at[2], hid_r, pair)
    mem_next = mem_copy(mem_slab(far), far, mem_s.at[2], pair)

    def vec_copy(peer, slot):
        return remote(vec_ref, vec_all.at[slot], vec_s.at[peer], vec_r.at[slot], (peer, me_sq))

    def in_copy(part, peer, slot):
        return remote(
            self_in_ref.at[:, pl.ds(pl.multiple_of(part * width + me_sq * LANES, LANES), LANES)],
            w_in.at[pl.ds(pl.multiple_of(slot * strip, strip), strip), pl.ds(part * LANES, LANES)],
            in_s.at[part, peer], in_r.at[part, slot], (peer, me_sq))

    own_vec = pltpu.make_async_copy(vec_ref, vec_all.at[me_dp], loc_sem.at[2])
    own_in = [pltpu.make_async_copy(
        self_in_ref.at[:, pl.ds(pl.multiple_of(part * width + me_sq * LANES, LANES), LANES)],
        w_in.at[pl.ds(pl.multiple_of(me_dp * strip, strip), strip), pl.ds(part * LANES, LANES)],
        loc_sem.at[3 + part]) for part in range(3)]

    hid_far.start()
    hid_pair.start()
    many(dp - 1, lambda k: vec_copy(other_dp(k), me_dp).start())
    many(dp - 1, lambda k: [in_copy(part, other_dp(k), me_dp).start() for part in range(3)])
    own_hidden.start()
    own_memory.start()
    own_vec.start()
    for copy in own_in:
        copy.start()

    def half_columns(index, side):
        size = shards[index].shape[1] // 2
        return pl.ds(pl.multiple_of(side * size, LANES), size)

    def columns(index, side=None):
        side = half if side is None else side
        if index < 4:
            return half_columns(index, side)
        size = shards[index].shape[1] // 4
        part = me_sq // 2 if index == 4 else index - 5
        return pl.ds(pl.multiple_of((side * 2 + part) * size, LANES), size)

    def sent_columns(index, side):
        return half_columns(index, side) if index <= 4 else columns(index, side)

    def block_rows(index, slot):
        size = shards[index].shape[0]
        return pl.ds(pl.multiple_of(slot * size, size), size)

    def z_copy(index, peer, slot):
        return remote(shards[index].at[:, columns(index)], wholes[index].at[block_rows(index, slot * 2 + me_lo), columns(index)],
                      z_s.at[index, peer], z_r.at[index, slot], (peer * 2 + me_lo, me_sq))

    def x_copy(index, slot, low, own):
        there = wholes[index].at[block_rows(index, slot * 2 + low), columns(index)]
        src = shards[index].at[:, columns(index)] if own else there
        return remote(src, there, x_s.at[index, slot], x_r.at[index, slot], (me_hi * 2 + 1 - me_lo, me_sq))

    def c_copy(index):
        there = wholes[index].at[:, sent_columns(index, half)]
        return remote(there, there, c_s.at[index], c_r.at[index], (me_dp, pair))

    def c_wait(index):
        there = wholes[index].at[:, sent_columns(index, 1 - half)]
        remote(there, there, c_s.at[index], c_r.at[index], (me_dp, pair)).wait_recv()

    def w_copy(index, block):
        there = wholes[index].at[block_rows(index, block), columns(index)]
        return remote(there, there, w_s.at[index - 4, block], w_r.at[index - 4, block], (me_dp, far))

    def w_wait(index, block):
        size = shards[index].shape[1] // 4
        there = wholes[index].at[block_rows(index, block), pl.ds(pl.multiple_of((half * 2 + far // 2) * size, LANES), size)]
        remote(there, there, w_s.at[index - 4, block], w_r.at[index - 4, block], (me_dp, far)).wait_recv()

    def own_copy(index):
        return pltpu.make_async_copy(shards[index].at[:, columns(index)], wholes[index].at[block_rows(index, me_dp), columns(index)], loc_sem.at[6 + index])

    def other_hi(step):
        return (me_hi + 1 + step) % high

    def own_stage(index):
        x_copy(index, me_hi, me_lo, True).start()
        own_copy(index).start()

    line = high == 4

    def unless_outer(block, step):
        if line:
            pl.when((block - me_hi) * (block - me_hi) != 9)(step)
        else:
            step()

    def hop_copy(index):
        block = 3 * (2 - me_hi) % 4
        there = wholes[index].at[block_rows(index, block * 2 + me_lo), columns(index)]
        return remote(there, there, hop_s.at[index], z_r.at[index, block], ((3 - block) * 2 + me_lo, me_sq))

    def first_stage(index):
        many(high - 1, lambda k: unless_outer(other_hi(k), lambda: z_copy(index, other_hi(k), me_hi).start()))

    def arrive_high(index, block):
        z_copy(index, block, block).wait_recv()
        x_copy(index, block, me_lo, False).start()
        if index == 4:
            w_copy(index, block * 2 + me_lo).start()

    def second_stage(index):
        if index == 4:
            own_copy(index).wait()
            w_copy(index, me_dp).start()
        many(high - 1, lambda k: unless_outer(other_hi(k), lambda: arrive_high(index, other_hi(k))))
        if line:
            pl.when((me_hi == 1) | (me_hi == 2))(lambda: hop_copy(index).start())

    def late_stage(index):
        if line:
            pl.when((me_hi == 0) | (me_hi == 3))(lambda: arrive_high(index, 3 - me_hi))

    def third_stage(index):
        def arrive(k):
            x_copy(index, k, 1 - me_lo, False).wait_recv()
            if index == 4:
                w_copy(index, k * 2 + 1 - me_lo).start()
        many(high, arrive)
        if index != 4:
            own_copy(index).wait()
            c_copy(index).start()

    def fourth_stage(index):
        many(dp, lambda k: w_wait(index, k))
        c_copy(index).start()

    def finish_weight(index):
        many(high - 1, lambda k: unless_outer(other_hi(k), lambda: z_copy(index, other_hi(k), me_hi).wait_send()))
        if line:
            pl.when((me_hi == 1) | (me_hi == 2))(lambda: hop_copy(index).wait_send())
        many(high, lambda k: x_copy(index, k, me_lo, False).wait_send())
        if index == 4:
            many(dp, lambda k: w_copy(index, k).wait_send())
        c_copy(index).wait_send()

    for index in (0, 1, 2, 4, 5, 6, 3):
        own_stage(index)

    own_vec.wait()
    many(dp - 1, lambda k: vec_copy(other_dp(k), other_dp(k)).wait_recv())
    vec_full[...] = jnp.zeros_like(vec_full)
    bias_full[...] = jnp.zeros_like(bias_full)
    lane_k = lax.broadcasted_iota(i32, (LANES, width), 0)
    lane_j = lax.broadcasted_iota(i32, (LANES, width), 1)
    big = inner // dp
    piece = min(big, LANES)
    big_k = lax.broadcasted_iota(i32, (LANES, inner), 0)
    big_j = lax.broadcasted_iota(i32, (LANES, inner), 1)

    def place(slot):
        hot = ((lane_j - slot * strip == lane_k) & (lane_k < strip)).astype(f32).astype(bf16)
        vec_full[...] = vec_full[...] + nn(vec_all[slot], hot)[:8]
        for part in range(big // piece):
            wide = ((big_j - slot * big - part * piece == big_k) & (big_k < piece)).astype(f32).astype(bf16)
            bias_full[...] = bias_full[...] + nn(vec_all[slot], wide)[8 + part:9 + part]
    lax.fori_loop(0, dp, lambda slot, carry: (place(slot), carry)[1], 0)
    gain_one, shift_one = vec_full[0:1], vec_full[1:2]
    gain_two, shift_two = vec_full[2:3], vec_full[3:4]

    def norm_slab(slab):
        def step(place_rows):
            unit, _ = unit_rows(hid_all[slab, place_rows].astype(f32))
            start = pl.multiple_of(slab * rows + place_rows.start, place_rows.size)
            normed_all[pl.ds(start, place_rows.size)] = (unit * gain_one + shift_one).astype(bf16)
        tiles(rows, 256, step)

    def project_slab(slab):
        def step(place_rows):
            here = pl.ds(pl.multiple_of(slab * rows + place_rows.start, place_rows.size), place_rows.size)
            packed = nn(normed_all[here], w_in[...]).astype(bf16)
            q_all[here] = packed[:, :LANES]
            k_all[here] = packed[:, LANES:2 * LANES]
            v_all[here] = packed[:, 2 * LANES:]
        tiles(rows, 256, step)

    own_hidden.wait()
    norm_slab(me_sq)
    hid_pair_in = slab_copy(hid_all.at[pair], hid_all, pair, hid_s.at[0], hid_r, pair)
    hid_pair_in.wait_recv()
    norm_slab(pair)
    for copy in own_in:
        copy.wait()
    many(dp - 1, lambda k: [in_copy(part, other_dp(k), other_dp(k)).wait_recv() for part in range(3)])
    for index in (0, 1, 2):
        first_stage(index)
    project_slab(me_sq)
    project_slab(pair)
    slab_copy(hid_all.at[far], hid_all, far, hid_s.at[1], hid_r, far).wait_recv()
    hid_next.start()
    mem_far.start()
    mem_pair_copy.start()
    norm_slab(far)
    project_slab(far)
    slab_copy(hid_all.at[cross], hid_all, cross, hid_s.at[2], hid_r, pair).wait_recv()
    norm_slab(cross)
    project_slab(cross)

    limit = len_ref[0]
    mem_limit = mlen_ref[0]
    scale = HD ** (-0.5) * log2_e

    def softmax_block(scores, values):
        largest = jnp.max(scores, axis=1, keepdims=True)
        powers = jnp.exp2(scores - largest)
        total = jnp.sum(powers, axis=1, keepdims=True)
        return nn(powers.astype(bf16), values) / total, largest + jnp.log2(total)

    def att_copy(block, owner):
        return remote(o_heads.at[pl.ds(pl.multiple_of(block * rows, rows), rows)],
                      att_tok.at[:, pl.ds(pl.multiple_of(owner * LANES, LANES), LANES)],
                      a_s.at[block], a_r.at[owner], (me_dp, block))

    def self_block(block):
        here = pl.ds(block * rows, rows)
        query = q_all[here]
        head_queries = [pick(query, head_mask(head)) for head in range(2)]

        def key_part(index, carry, diagonal):
            there = pl.ds(pl.multiple_of(index * rows, rows), rows)
            place = index * rows + lax.broadcasted_iota(i32, (1, rows), 1)
            bias = jnp.where(place < limit, 0.0, masked_score)
            held = []
            for head in range(2):
                largest, total, out = carry[3 * head:3 * head + 3]
                scores = nt(head_queries[head], k_all[there]) * scale + bias
                if diagonal:
                    scores = jnp.where(lax.broadcasted_iota(i32, (rows, rows), 1) <= lax.broadcasted_iota(i32, (rows, rows), 0), scores, masked_score)
                higher = jnp.maximum(largest, jnp.max(scores, axis=1, keepdims=True))
                powers = jnp.exp2(scores - higher)
                shrink = jnp.exp2(largest - higher)
                total = total * shrink + jnp.sum(powers, axis=1, keepdims=True)
                held += [higher, total, out * shrink + nn(powers.astype(bf16), v_all[there])]
            return tuple(held)

        carry = (jnp.full((rows, 1), -3e38, f32), jnp.zeros((rows, 1), f32), jnp.zeros((rows, LANES), f32)) * 2
        if block:
            carry = lax.fori_loop(0, block, lambda index, held: key_part(index, held, False), carry)
        carry = key_part(block, carry, True)
        outs = [carry[3 * head + 2] / carry[3 * head + 1] for head in range(2)]
        spreads = [carry[3 * head] + jnp.log2(carry[3 * head + 1]) for head in range(2)]
        o_heads[here] = jnp.where(head_mask(0), outs[0], outs[1]).astype(bf16)
        turned = jnp.transpose(jnp.where(head_mask(0), spreads[0], spreads[1]))
        self_lse[0:1, here] = turned[0:1]
        self_lse[1:2, here] = turned[HD:HD + 1]

        @pl.when(me_sq != block)
        def _():
            att_copy(block, me_sq).start()

    def forward_memory():
        mem_copy(mem_slab(far), far, mem_s.at[1], far).wait_recv()
        mem_next.start()

    def each(stage, *indices):
        for index in indices:
            stage(index)

    comm_steps = {3: lambda: (each(second_stage, 0, 1, 2), first_stage(5)),
                  2: lambda: (forward_memory(), each(late_stage, 0, 1, 2), second_stage(4), first_stage(6)),
                  1: lambda: (late_stage(4), first_stage(3)), 0: lambda: (third_stage(0), second_stage(5))}
    first_stage(4)
    for block in range(sq - 1, -1, -1):
        self_block(block)
        comm_steps[block]()
    each(third_stage, 1, 2)
    late_stage(5)
    att_tok[:, pl.ds(pl.multiple_of(me_sq * LANES, LANES), LANES)] = o_heads[pl.ds(pl.multiple_of(me_sq * rows, rows), rows)]

    own_memory.wait()
    mem_copy(mem_slab(pair), pair, mem_s.at[0], pair).wait_recv()
    mem_copy(mem_slab(cross), cross, mem_s.at[2], pair).wait_recv()
    c_wait(0)

    def project_memory(slab, carry):
        place = pl.ds(pl.multiple_of(slab * mem_rows, mem_rows), mem_rows)
        mem_pair[place] = nn(mem_all[place], w_cm[...]).astype(bf16)
        return carry
    lax.fori_loop(0, sq, project_memory, 0)

    for peer in (pair, far, cross):
        att_copy(peer, peer).wait_recv()
    c_wait(1)
    c_wait(2)

    def step_two(here):
        value = hidden_ref[here].astype(f32) + nn(att_tok[here], w_so[...])
        after_self[here] = value
        unit, _ = unit_rows(value)
        normed = (unit * gain_two + shift_two).astype(bf16)
        normed_two[here] = normed
        cross_q[here] = nn(normed, w_cq[...]).astype(bf16)
    tiles(rows, 256, step_two)

    mem_bias = jnp.where(lax.broadcasted_iota(i32, (1, all_mem), 1) < mem_limit, 0.0, masked_score)

    def cross_pair(number, held):
        lanes = pl.ds(pl.multiple_of(number * LANES, LANES), LANES)
        value_lanes = pl.ds(pl.multiple_of(width + number * LANES, LANES), LANES)
        query = cross_q[:, lanes]
        outs, spreads = [], []
        for head in range(2):
            scores = nt(pick(query, head_mask(head)), mem_pair[:, lanes]) * scale + mem_bias
            out, spread = softmax_block(scores, mem_pair[:, value_lanes])
            outs.append(out)
            spreads.append(spread)
        mixed[:, lanes] = jnp.where(head_mask(0), outs[0], outs[1]).astype(bf16)
        turned = jnp.transpose(jnp.where(head_mask(0), spreads[0], spreads[1]))
        cross_lse[pl.ds(2 * number, 1)] = turned[0:1]
        cross_lse[pl.ds(2 * number + 1, 1)] = turned[HD:HD + 1]
        return held

    pairs = width // LANES
    each(second_stage, 6, 3)
    third_stage(4)
    lax.fori_loop(0, 1, cross_pair, 0)
    each(late_stage, 6, 3)
    third_stage(5)
    lax.fori_loop(1, 2, cross_pair, 0)
    fourth_stage(4)
    lax.fori_loop(2, 3, cross_pair, 0)
    each(third_stage, 6, 3)
    lax.fori_loop(3, pairs, cross_pair, 0)
    c_wait(3)

    def step_three(here):
        after_cross[here] = after_self[here] + nn(mixed[here], w_co[...])
    tiles(rows, 256, step_three)

    c_wait(4)
    c_wait(5)
    c_wait(6)
    gain_three, shift_three, outer_bias, exit_row = vec_full[4:5], vec_full[5:6], vec_full[6:7], vec_full[7:8]
    parts = ((g_cm, p_cm, x_cm, h_cm, f_cm, y_cm, out_cm), (g_so, p_so, x_so, h_so, f_so, y_so, out_so),
             (g_cq, p_cq, x_cq, h_cq, f_cq, y_cq, out_cq), (g_co, p_co, x_co, h_co, f_co, y_co, out_co),
             (g_fi, p_fi, x_fi, h_fi, f_fi, y_fi, out_fi), (g_fo, p_fo, x_fo, h_fo, f_fo, y_fo, out_fo))
    chunk = 512

    def norm_back(grad, unit, inverse, gain):
        scaled = grad * gain
        first = jnp.mean(scaled, axis=-1, keepdims=True)
        second = jnp.mean(scaled * unit, axis=-1, keepdims=True)
        return inverse * (scaled - first - unit * second)

    def add_sum(index, value):
        sums[index:index + 1] = sums[index:index + 1] + jnp.sum(value, axis=0, keepdims=True)

    def gc_copy(index):
        size = shards[index].shape[1] // 2
        other = pl.ds(pl.multiple_of((1 - half) * size, LANES), size)
        return remote(parts[index][0].at[:, :, :, other], parts[index][1], gc_s.at[index], gc_r.at[index], (me_dp, pair))

    def gq_copy():
        return remote(parts[5][1].at[:, :, :, part_columns(5, far // 2)], quarter_got, gq_s.at[0], gq_r.at[0], (me_dp, far))

    def ga_copy(owner, peer):
        size = shards[5].shape[1] // 4
        there = out_fo.at[:, pl.ds(pl.multiple_of((owner % 2 * 2 + owner // 2) * size, LANES), size)]
        return remote(there, there, ga_s.at[peer], ga_r.at[owner], (me_dp, peer))

    def gx_copy(index):
        src = parts[index][1].at[:, 1 - me_lo, :, part_columns(index, me_sq // 2)] if index == 5 else parts[index][1].at[:, 1 - me_lo]
        return remote(src, parts[index][2], gx_s.at[index], gx_r.at[index], (me_hi * 2 + 1 - me_lo, me_sq))

    def gz_copy(index, peer, slot):
        return remote(parts[index][2].at[peer], parts[index][3].at[slot], gz_s.at[index, peer], gz_r.at[index, slot], (peer * 2 + me_lo, me_sq))

    def gy_copy(index):
        return remote(parts[index][4], parts[index][5], gy_s.at[index], gy_r.at[index], (me_dp, far))

    def gp_copy(index, side):
        size = shards[index].shape[1] // 2
        there = parts[index][6].at[:, pl.ds(pl.multiple_of(side * size, LANES), size)]
        return remote(there, there, gp_s.at[index], gp_r.at[index], (me_dp, pair))

    def reduce_pair(index):
        gc_copy(index).start()

    def reduce_low(index):
        gc_copy(index).wait_recv()
        whole_ref, part_ref = parts[index][0], parts[index][1]

        def add(place, carry):
            for low in range(2):
                part_ref[place, low] = (part_ref[place, low].astype(f32) + whole_ref[place, low, :, half_columns(index, half)].astype(f32)).astype(bf16)
            return carry
        lax.fori_loop(0, high, add, 0)
        if index == 5:
            gq_copy().start()
        else:
            gx_copy(index).start()

    def part_columns(index, side):
        size = shards[index].shape[1] // 4
        return pl.ds(pl.multiple_of(side * size, LANES), size)

    def reduce_across(index):
        gq_copy().wait_recv()
        part_ref = parts[index][1]

        def add(place, carry):
            for low in range(2):
                mine = part_columns(index, me_sq // 2)
                part_ref[place, low, :, mine] = (part_ref[place, low, :, mine].astype(f32) + quarter_got[place, low].astype(f32)).astype(bf16)
            return carry
        lax.fori_loop(0, high, add, 0)
        gx_copy(index).start()

    def reduce_high(index):
        gx_copy(index).wait_recv()
        part_ref, low_ref = parts[index][1], parts[index][2]

        def add(place, carry):
            mine = part_ref[place, me_lo, :, part_columns(index, me_sq // 2)] if index == 5 else part_ref[place, me_lo]
            low_ref[place] = (low_ref[place].astype(f32) + mine.astype(f32)).astype(bf16)
            return carry
        lax.fori_loop(0, high, add, 0)
        many(high - 1, lambda k: gz_copy(index, other_hi(k), me_hi).start())

    def reduce_far(index):
        low_ref, high_ref, far_ref = parts[index][2], parts[index][3], parts[index][4]
        high_ref[me_hi] = low_ref[me_hi]
        many(high - 1, lambda k: gz_copy(index, other_hi(k), other_hi(k)).wait_recv())
        def add(place, held):
            return held + high_ref[place].astype(f32)
        total = lax.fori_loop(1, high, add, high_ref[0].astype(f32))
        far_ref[...] = total if index == 5 else total.astype(bf16)
        if index == 5:
            size = shards[index].shape[1] // 4
            parts[index][6][:, pl.ds(pl.multiple_of((half * 2 + me_sq // 2) * size, LANES), size)] = far_ref[...]
            for peer in (far, cross, pair):
                ga_copy(me_sq, peer).start()
        else:
            gy_copy(index).start()

    def reduce_last(index):
        far_ref, got_ref, out_ref = parts[index][4], parts[index][5], parts[index][6]
        gy_copy(index).wait_recv()
        out_ref[:, half_columns(index, half)] = far_ref[...].astype(f32) + got_ref[...].astype(f32)
        gp_copy(index, half).start()

    def reduce_end(index):
        if index == 5:
            for peer in (far, cross, pair):
                ga_copy(peer, peer).wait_recv()
        else:
            gp_copy(index, 1 - half).wait_recv()

    def reduce_drain(index):
        gc_copy(index).wait_send()
        gx_copy(index).wait_send()
        many(high - 1, lambda k: gz_copy(index, other_hi(k), me_hi).wait_send())
        if index == 5:
            gq_copy().wait_send()
            for peer in (far, cross, pair):
                ga_copy(me_sq, peer).wait_send()
        else:
            gy_copy(index).wait_send()
            gp_copy(index, half).wait_send()

    def weight_grad(index, left, rights):
        out_ref = parts[index][0]
        size = shards[index].shape[0]
        pieces = max(1, 256 // size)

        def step(tile, carry):
            features = left(tile)
            for number, right in enumerate(rights):
                value = tn(features, right())
                span = min(size, 256)
                cols = pl.ds(number * value.shape[1], value.shape[1])
                for piece in range(pieces):
                    place = tile * pieces + piece
                    out_ref[place // 2, place % 2, :, cols] = value[piece * span:(piece + 1) * span].astype(bf16)
            return carry
        lax.fori_loop(0, size * dp // 256, step, 0)

    def feature_tile(ref):
        return lambda tile: ref[:, pl.ds(pl.multiple_of(tile * 256, 256), 256)]

    hid_next.wait_send()
    for index in range(7):
        finish_weight(index)
    grad_res = grad_hidden_ref
    grad_packed, sum_in, turned_q = w_fo, after_cross, slope
    packed_cols = pl.ds(0, 3 * LANES)
    turned_rows = pl.ds(0, LANES)
    sums[...] = jnp.zeros_like(sums)
    halting_ref[...] = jnp.zeros_like(halting_ref)

    def ffn_step(here):
        size = here.size
        unit, inverse = unit_rows(after_cross[here])
        normed = (unit * gain_three + shift_three).astype(bf16)
        normed_three[here] = normed
        out = after_cross[here] + outer_bias
        for part in range(inner // chunk):
            cols = pl.ds(part * chunk, chunk)
            pre = nn(normed, w_fi[:, cols]) + bias_full[:, cols]
            square = pre * pre
            bent = jnp.tanh(gelu_scale * (pre + gelu_cubic * square * pre))
            act = (0.5 * pre * (1.0 + bent)).astype(bf16)
            active[part, here] = act
            slope[:, cols] = 0.5 * (1.0 + bent) + 0.5 * pre * (1.0 - bent * bent) * gelu_scale * (1.0 + 3.0 * gelu_cubic * square)
            out = out + nn(act, w_fo[cols])
        result_ref[here] = out.astype(bf16)
        halt = 1.0 / (1.0 + jnp.exp(-jnp.sum(out * exit_row, axis=-1, keepdims=True)))
        place = here.start + lax.broadcasted_iota(i32, (size, rows), 0)
        same = place == lax.broadcasted_iota(i32, (size, rows), 1)
        halting_ref[...] = halting_ref[...] + jnp.sum(jnp.where(same, halt, 0.0), axis=0, keepdims=True)
        halt_grad = jnp.sum(jnp.where(same, halt_grad_ref[...], 0.0), axis=1, keepdims=True)
        live = (me_sq * rows + here.start + lax.broadcasted_iota(i32, (size, 1), 0) < limit).astype(f32)
        grad_logit = halt_grad * live * halt * (1.0 - halt)
        add_sum(7, grad_logit * out)
        grad_out = grad_ref[here].astype(f32) * live + grad_logit * exit_row
        grad_branch = grad_out.astype(bf16)
        branch[here] = grad_branch
        add_sum(6, grad_branch.astype(f32))
        grad_normed = jnp.zeros((size, width), f32)
        for part in range(inner // chunk):
            cols = pl.ds(part * chunk, chunk)
            grad_part = (nt(grad_branch, w_fo[cols]) * slope[:, cols]).astype(bf16)
            grad_inner[part, here] = grad_part
            add_sum(8 + part, grad_part.astype(f32))
            grad_normed = grad_normed + nt(grad_part, w_fi[:, cols])
        add_sum(4, grad_normed * unit)
        add_sum(5, grad_normed)
        grad_cross = grad_out + norm_back(grad_normed, unit, inverse, gain_three)
        grad_res[here] = grad_cross
        grad_cross_branch = grad_cross.astype(bf16)
        cross_branch[here] = grad_cross_branch
        grad_mixed[here] = nt(grad_cross_branch, w_co[...]).astype(bf16)
    tiles(rows, 256, ffn_step)
    weight_grad(5, lambda tile: active[tile // 2, :, pl.ds(pl.multiple_of(tile % 2 * 256, 256), 256)], [lambda: branch[...]])
    reduce_pair(5)
    weight_grad(4, feature_tile(normed_three), [functools.partial(lambda part: grad_inner[part], part) for part in range(inner // chunk)])
    reduce_pair(4)
    weight_grad(3, feature_tile(mixed), [lambda: cross_branch[...]])
    reduce_pair(3)

    select = (lax.broadcasted_iota(i32, (8, width), 1) // HD == lax.broadcasted_iota(i32, (8, width), 0)).astype(f32)
    cross_delta[...] = nt(select, grad_mixed[...].astype(f32) * mixed[...].astype(f32), lax.Precision.HIGHEST)
    score_scale = HD ** (-0.5)

    def attend_back(keys, values, query, grad, spread_rows, delta_rows, bias, mask):
        grad_keys, grad_values, grad_query = None, None, None
        for head in range(2):
            only = head_mask(head)
            head_keys = pick(keys, only)
            scores = nt(head_keys, query) * scale + bias
            if mask is not None:
                scores = jnp.where(mask, scores, masked_score)
            powers = jnp.exp2(scores - spread_rows[head])
            grad_powers = nt(pick(values, only), grad)
            grad_scores = (powers * (grad_powers - delta_rows[head])).astype(bf16)
            value_part = nn(powers.astype(bf16), pick(grad, only))
            key_part = nn(grad_scores, pick(query, only))
            query_part = nn(jnp.transpose(head_keys), grad_scores)
            grad_values = value_part if head == 0 else grad_values + value_part
            grad_keys = key_part if head == 0 else grad_keys + key_part
            grad_query = query_part if head == 0 else grad_query + query_part
        return grad_keys, grad_values, grad_query

    key_block = 512
    key_blocks = all_mem // key_block
    grad_pair = active
    grad_cq = branch
    grad_att = normed_three
    part_hid = hid_all
    cross_comm = {0: lambda: (reduce_low(5), reduce_low(4)), 1: lambda: reduce_low(3), 2: lambda: None, 3: lambda: None}
    def cross_back(number, held):
        lanes = pl.ds(pl.multiple_of(number * LANES, LANES), LANES)
        value_lanes = pl.ds(pl.multiple_of(width + number * LANES, LANES), LANES)

        def block_step(block, total):
            here = pl.ds(pl.multiple_of(block * key_block, key_block), key_block)
            key_place = block * key_block + lax.broadcasted_iota(i32, (key_block, 1), 0)
            grad_keys, grad_values, grad_query = attend_back(
                mem_pair[here, lanes], mem_pair[here, value_lanes], cross_q[:, lanes], grad_mixed[:, lanes],
                [cross_lse[pl.ds(2 * number + head, 1)] for head in range(2)],
                [cross_delta[pl.ds(2 * number + head, 1)] for head in range(2)],
                jnp.where(key_place < mem_limit, 0.0, masked_score), None)
            grad_pair[block, :, lanes] = (grad_keys * score_scale).astype(bf16)
            grad_pair[key_blocks + block, :, lanes] = grad_values.astype(bf16)
            return total + grad_query

        total = lax.fori_loop(0, key_blocks, block_step, jnp.zeros((LANES, rows), f32))
        grad_cq[:, lanes] = (jnp.transpose(total) * score_scale).astype(bf16)
        return held

    for number in range(pairs):
        lax.fori_loop(number, number + 1, cross_back, 0)
        cross_comm[number]()

    def step_two_back(here):
        grad_normed = nt(grad_cq[here], w_cq[...])
        unit, inverse = unit_rows(after_self[here])
        add_sum(2, grad_normed * unit)
        add_sum(3, grad_normed)
        grad_self = grad_res[here] + norm_back(grad_normed, unit, inverse, gain_two)
        grad_res[here] = grad_self
        grad_self_branch = grad_self.astype(bf16)
        cross_branch[here] = grad_self_branch
        grad_att[here] = nt(grad_self_branch, w_so[...]).astype(bf16)

    tiles(rows, 256, step_two_back)

    def da_copy(peer, owner):
        return remote(grad_att.at[:, pl.ds(pl.multiple_of(peer * LANES, LANES), LANES)],
                      grad_heads.at[pl.ds(pl.multiple_of(owner * rows, rows), rows)], da_s.at[peer], da_r.at[owner], (me_dp, peer))

    for peer in (far, cross, pair):
        da_copy(peer, me_sq).start()
    grad_heads[pl.ds(pl.multiple_of(me_sq * rows, rows), rows)] = grad_att[:, pl.ds(pl.multiple_of(me_sq * LANES, LANES), LANES)]

    def gm_copy(kind):
        source, target = ((cross, pair), (pair, pair), (far, far))[kind]
        return remote(part_mem.at[source], part_mem_got.at[kind], gm_s.at[kind], gm_r.at[kind], (me_dp, target))

    def memory_pair():
        gm_copy(0).start()
        gm_copy(1).start()

    def memory_far():
        gm_copy(0).wait_recv()
        part_mem[far] = (part_mem[far].astype(f32) + part_mem_got[0].astype(f32)).astype(bf16)
        gm_copy(2).start()

    def memory_end():
        gm_copy(1).wait_recv()
        gm_copy(2).wait_recv()
        grad_memory_ref[...] = (part_mem[me_sq].astype(f32) + part_mem_got[1].astype(f32)) + part_mem_got[2].astype(f32)

    def memory_part(slab, carry):
        per_block = key_block // mem_rows
        place = pl.ds(pl.multiple_of(slab % per_block * mem_rows, mem_rows), mem_rows)
        part_mem[slab] = (nt(grad_pair[slab // per_block, place], w_cm[:, :width])
                          + nt(grad_pair[key_blocks + slab // per_block, place], w_cm[:, width:])).astype(bf16)
        return carry

    reduce_across(5)
    reduce_high(4)
    weight_grad(0, feature_tile(mem_all), [functools.partial(lambda part: grad_pair[part * key_blocks:(part + 1) * key_blocks].reshape(all_mem, width), part) for part in range(2)])
    reduce_pair(0)
    reduce_high(3)
    weight_grad(1, feature_tile(att_tok), [lambda: cross_branch[...]])
    reduce_pair(1)
    weight_grad(2, feature_tile(normed_two), [lambda: grad_cq[...]])
    reduce_pair(2)
    lax.fori_loop(0, sq, memory_part, 0)
    memory_pair()

    def s1_copy(peer, owner):
        return remote(sums, sums_seq.at[owner], s1_s.at[peer], s1_r.at[owner], (me_dp, peer))

    for peer in (pair, far, cross):
        da_copy(peer, peer).wait_recv()
    select_two = (lax.broadcasted_iota(i32, (8, LANES), 1) // HD == lax.broadcasted_iota(i32, (8, LANES), 0)).astype(f32)
    deltas = nt(select_two, grad_heads[...].astype(f32) * o_heads[...].astype(f32), lax.Precision.HIGHEST)
    self_lse[2:4] = deltas[0:2]
    turned_q[turned_rows] = jnp.zeros((LANES, rows * sq), f32)
    half_rows = rows // 2

    def yh_copy(block):
        there = half_got.at[block % 2]
        return remote(part_hid.at[block, pl.ds(pl.multiple_of((1 - half) * half_rows, half_rows), half_rows)], there,
                      yh_s.at[block], yh_r.at[block], (me_dp, pair))

    def yf_copy(block, side):
        return remote(part_hid.at[block, pl.ds(pl.multiple_of(half * half_rows, half_rows), half_rows)], far_got.at[pl.ds(pl.multiple_of(side * half_rows, half_rows), half_rows)],
                      yf_s.at[block], yf_r.at[side], (me_dp, block))

    def yp_copy(block):
        return remote(part_hid.at[block], pair_got, yp_s.at[0], yp_r.at[0], (me_dp, pair))

    def away(block):
        return me_sq // 2 != block // 2

    def send_part(block):
        @pl.when(away(block))
        def _():
            yh_copy(block).start()

        @pl.when(pair == block)
        def _():
            yp_copy(block).start()

    def forward_part(block):
        @pl.when(away(block))
        def _():
            yh_copy(block).wait_recv()
            place = pl.ds(pl.multiple_of(half * half_rows, half_rows), half_rows)
            part_hid[block, place] = (part_hid[block, place].astype(f32) + half_got[block % 2].astype(f32)).astype(bf16)
            yf_copy(block, half).start()

    schedule = {
        (0, 0): lambda: (reduce_high(5), memory_far()), (0, 1): lambda: reduce_low(0), (0, 2): lambda: (reduce_low(1), reduce_low(2)),
        (0, 3): lambda: (reduce_far(4), reduce_far(3)), (0, sq): lambda: (reduce_high(0), reduce_far(5)),
        (1, 1): lambda: forward_part(0), (1, 2): lambda: (reduce_high(1), reduce_high(2), reduce_last(4)),
        (1, sq): lambda: (reduce_far(0), reduce_last(3)), (2, 2): lambda: forward_part(1), (2, sq): lambda: (reduce_far(1), reduce_far(2)),
        (3, sq): lambda: (forward_part(2), reduce_last(0))}

    def comm_point(block, index):
        if (block, index) in schedule:
            schedule[block, index]()

    def gi_copy(peer, slot):
        return remote(grad_in.at[peer], grad_in_got.at[slot], gi_s.at[peer], gi_r.at[slot], (peer, me_sq))

    def input_sums():
        for place in range(dp):
            grad_in[place] = sum_in[place * strip:(place + 1) * strip, packed_cols].astype(bf16)
        many(dp - 1, lambda k: gi_copy(other_dp(k), me_dp).start())

    def key_step(block):
        here = pl.ds(block * rows, rows)
        keys, values = k_all[here], v_all[here]
        bias = jnp.where(block * rows + lax.broadcasted_iota(i32, (rows, 1), 0) < limit, 0.0, masked_score)

        def query_step(index, carry, diagonal):
            there = pl.ds(pl.multiple_of(index * rows, rows), rows)
            mask = None
            if diagonal:
                mask = lax.broadcasted_iota(i32, (rows, rows), 0) <= lax.broadcasted_iota(i32, (rows, rows), 1)
            grad_keys, grad_values, grad_query = attend_back(
                keys, values, q_all[there], grad_heads[there],
                [self_lse[head:head + 1, there] for head in range(2)],
                [self_lse[2 + head:3 + head, there] for head in range(2)], bias, mask)
            turned_q[turned_rows, there] = turned_q[turned_rows, there] + grad_query
            return carry[0] + grad_keys, carry[1] + grad_values

        zero = jnp.zeros((rows, LANES), f32)
        carry = query_step(block, (zero, zero), True)
        comm_point(block, block)
        for index in range(block + 1, sq):
            carry = lax.fori_loop(index, index + 1, lambda place, held: query_step(place, held, False), carry)
            comm_point(block, index)
        grad_packed[here, pl.ds(LANES, LANES)] = (carry[0] * score_scale).astype(bf16)
        grad_packed[here, pl.ds(2 * LANES, LANES)] = carry[1].astype(bf16)
        grad_packed[here, pl.ds(0, LANES)] = (jnp.transpose(turned_q[turned_rows, here]) * score_scale).astype(bf16)

        def input_part(tile, held):
            cols = pl.ds(pl.multiple_of(tile * 256, 256), 256)
            value = tn(normed_all[here, cols], grad_packed[here, packed_cols])
            if block == 0:
                sum_in[cols, packed_cols] = value
            else:
                sum_in[cols, packed_cols] = sum_in[cols, packed_cols] + value
            return held
        lax.fori_loop(0, width // 256, input_part, 0)
        if block == sq - 1:
            input_sums()

        def hidden_part(place):
            rows_here = pl.ds(pl.multiple_of(block * rows + place.start, place.size), place.size)
            part_hid[block, place] = nt(grad_packed[rows_here, packed_cols], w_in[...]).astype(bf16)
        tiles(rows, 256, hidden_part)
        send_part(block)

    for block in range(sq):
        key_step(block)
        comm_point(block, sq)
    grad_in_got[me_dp] = grad_in[me_dp]
    forward_part(sq - 1)

    memory_end()
    reduce_last(1)
    reduce_last(2)

    yp_copy(me_sq).wait_recv()
    yf_copy(me_sq, 0).wait_recv()
    yf_copy(me_sq, 1).wait_recv()

    def last_step(here):
        grad_normed = part_hid[me_sq, here].astype(f32) + pair_got[here].astype(f32) + far_got[here].astype(f32)
        unit, inverse = unit_rows(hidden_ref[here].astype(f32))
        add_sum(0, grad_normed * unit)
        add_sum(1, grad_normed)
        grad_hidden_ref[here] = grad_res[here] + norm_back(grad_normed, unit, inverse, gain_one)
    tiles(rows, 256, last_step)

    for peer in (far, cross, pair):
        s1_copy(peer, me_sq).start()
    many(dp - 1, lambda k: gi_copy(other_dp(k), other_dp(k)).wait_recv())
    total_in = grad_in_got[0].astype(f32)
    for place in range(1, dp):
        total_in = total_in + grad_in_got[place].astype(f32)

    def go_copy(owner, peer):
        return remote(last_in.at[owner], last_in.at[owner], go_s.at[0, peer], go_r.at[0, owner], (me_dp, peer))
    last_in[me_sq] = total_in.astype(bf16)
    for peer in (far, cross, pair):
        go_copy(me_sq, peer).start()
    for peer in (far, cross, pair):
        s1_copy(peer, peer).wait_recv()
    sums_seq[me_sq] = sums[...]
    last_sums[...] = (sums_seq[0] + sums_seq[1]) + (sums_seq[2] + sums_seq[3])

    lanes_two = max(LANES, big)

    def v_blocks(peer):
        return (last_sums.at[pl.ds(0, 8), pl.ds(pl.multiple_of(peer * strip // LANES * LANES, LANES), LANES)],
                last_sums.at[pl.ds(8, 8), pl.ds(pl.multiple_of(peer * big % width // lanes_two * lanes_two, LANES), lanes_two)])

    def v_copy(peer, slot):
        one, two = v_blocks(peer)
        return (remote(one, vec_got.at[slot], s2_s.at[0, peer], s2_r.at[0, slot], (peer, me_sq)),
                remote(two, bias_got.at[slot], s2_s.at[1, peer], s2_r.at[1, slot], (peer, me_sq)))
    many(dp - 1, lambda k: [copy.start() for copy in v_copy(other_dp(k), me_dp)])
    one, two = v_blocks(me_dp)
    vec_got[me_dp] = one[...]
    bias_got[me_dp] = two[...]
    many(dp - 1, lambda k: [copy.wait_recv() for copy in v_copy(other_dp(k), other_dp(k))])
    out_vec[...] = vec_got[0]
    out_bias[...] = bias_got[0]

    def add_vec(place, carry):
        out_vec[...] = out_vec[...] + vec_got[place]
        out_bias[...] = out_bias[...] + bias_got[place]
        return carry
    lax.fori_loop(1, dp, add_vec, 0)
    for index in range(6):
        reduce_end(index)
    for peer in (far, cross, pair):
        go_copy(peer, peer).wait_recv()
    for owner in range(sq):
        for part in range(3):
            out_si[:, part * width + owner * LANES:part * width + (owner + 1) * LANES] = last_in[owner, :, part * LANES:(part + 1) * LANES].astype(f32)
    for index in range(6):
        reduce_drain(index)
    for peer in (far, cross, pair):
        da_copy(peer, me_sq).wait_send()
        s1_copy(peer, me_sq).wait_send()
        go_copy(me_sq, peer).wait_send()
    many(dp - 1, lambda k: gi_copy(other_dp(k), me_dp).wait_send())
    many(dp - 1, lambda k: [copy.wait_send() for copy in v_copy(other_dp(k), me_dp)])
    for kind in range(3):
        gm_copy(kind).wait_send()
    yp_copy(pair).wait_send()
    for block in range(sq):
        @pl.when(away(block))
        def _():
            yh_copy(block).wait_send()
            yf_copy(block, half).wait_send()
    for copy in (hid_far, hid_pair, mem_far, mem_pair_copy, mem_next):
        copy.wait_send()
    many(dp - 1, lambda k: vec_copy(other_dp(k), me_dp).wait_send())
    many(dp - 1, lambda k: [in_copy(part, other_dp(k), me_dp).wait_send() for part in range(3)])
    for peer in (pair, far, cross):
        att_copy(peer, me_sq).wait_send()


def whole_specs(names):
    return [pl.BlockSpec(memory_space=name) for name in names]


def run_layer(sizes, args):
    dp, sq, rows, mem_rows, width, inner = sizes
    seq_rows, all_mem = rows * sq, mem_rows * sq
    high, strip, big = dp // 2, width // dp, inner // dp
    V, A, S = pltpu.VMEM, pl.ANY, pltpu.SMEM
    dma = pltpu.SemaphoreType.DMA
    shard_shapes = [(strip, 2 * width), (strip, width), (strip, width), (strip, width), (strip, inner), (big, width)]
    outs = [((rows, width), bf16), ((1, rows), f32), ((rows, width), f32), ((mem_rows, width), f32),
            ((strip, 3 * width), f32)] + [(shape, f32) for shape in shard_shapes] + [((8, LANES), f32), ((8, max(LANES, big)), f32)]
    scratch = [((width, 2 * width), bf16), ((width, width), bf16), ((width, width), bf16), ((width, width), bf16),
               ((width, inner), bf16), ((inner, width), bf16), ((8, width), f32), ((1, inner), f32),
               ((rows, width), f32), ((rows, width), f32), ((rows, width), bf16), ((rows, width), bf16),
               ((rows, width), bf16), ((all_mem, 2 * width), bf16), ((8, rows), f32), ((rows, width), bf16),
               ((seq_rows, LANES), bf16), ((seq_rows, LANES), bf16), ((seq_rows, LANES), bf16), ((8, seq_rows), f32),
               ((width, 3 * LANES), bf16), ((sq, rows, width), bf16), ((all_mem, width), bf16),
               ((dp, 16, LANES), bf16), ((seq_rows, width), bf16), ((seq_rows, LANES), bf16),
               ((rows, width), bf16), ((inner // 512, rows, 512), bf16), ((inner // 512, rows, 512), bf16), ((256, inner), f32),
               ((rows, width), bf16), ((rows, width), bf16), ((rows, width), bf16), ((8, rows), f32),
               ((seq_rows, LANES), bf16),
               ((dp, strip, 3 * LANES), bf16), ((dp, strip, 3 * LANES), bf16),
               ((sq, mem_rows, width), bf16), ((3, mem_rows, width), bf16),
               ((2, rows // 2, width), bf16), ((rows, width), bf16), ((rows, width), bf16),
               ((16, width), f32), ((sq, 16, width), f32), ((16, width), f32), ((dp, 8, LANES), f32), ((dp, 8, max(LANES, big)), f32),
               ((high, 2, big, width // 4), bf16), ((sq, strip, 3 * LANES), bf16)]
    scratch += [((high, 2, size, columns), bf16) for size, columns in shard_shapes]
    scratch += [((high, 2, size, columns // 2), bf16) for size, columns in shard_shapes]
    ways = [2] * 5 + [4]
    scratch += [((high, size, columns // way), bf16) for (size, columns), way in zip(shard_shapes, ways)] * 2
    scratch += [((size, columns // 2), bf16) for size, columns in shard_shapes[:5]] + [((big, width // 4), f32)]
    scratch += [((size, columns // 2), bf16) for size, columns in shard_shapes[:5]] + [((8, LANES), f32)]
    semaphores = [dma((13,)), dma((3,)), dma((sq,)), dma((3,)), dma((sq,)), dma((dp,)), dma((dp,)), dma((3, dp)), dma((3, dp)),
                  dma((7, high)), dma((7, high)), dma((7, high)), dma((7, high)), dma((7,)), dma((7,)), dma((sq,)), dma((sq,)),
                  dma((6,)), dma((6,)), dma((6,)), dma((6,)), dma((6, high)), dma((6, high)), dma((6,)), dma((6,)), dma((6,)), dma((6,)),
                  dma((dp,)), dma((dp,)), dma((3, sq)), dma((3, sq)), dma((sq,)), dma((sq,)), dma((sq,)), dma((sq,)),
                  dma((7,)), dma((1, dp)), dma((1, dp)), dma((1,)), dma((1,)), dma((sq,)), dma((sq,)),
                  dma((sq,)), dma((sq,)), dma((sq,)), dma((2,)), dma((1,)), dma((1,)),
                  dma((sq,)), dma((sq,)), dma((2, dp)), dma((2, dp))]
    return pl.pallas_call(
        functools.partial(layer_kernel, sizes),
        out_shape=[jax.ShapeDtypeStruct(*out) for out in outs],
        in_specs=whole_specs([S, S, V, V, V, V, V, A, A, A, A, A, A, A]),
        out_specs=whole_specs([V] * len(outs)),
        scratch_shapes=[pltpu.VMEM(*item) for item in scratch] + semaphores,
        compiler_params=pltpu.CompilerParams(collective_id=0, has_side_effects=True, vmem_limit_bytes=62 << 20),
        name="layer",
    )(*args)


def finish_kernel(count, strip, big, width, *refs):
    sources, (vec_ref, bias_ref) = refs[:count], refs[count:count + 2]
    targets, vectors, bias_out = refs[count + 2:2 * count + 2], refs[2 * count + 2:2 * count + 10], refs[2 * count + 10]
    held, (sem_in, sem_out) = refs[2 * count + 11:-2], refs[-2:]
    loads = [pltpu.make_async_copy(sources[index], held[index], sem_in.at[index]) for index in range(count)]
    copies = [pltpu.make_async_copy(held[index], targets[index], sem_out.at[index]) for index in range(count)]
    for load in loads:
        load.start()
    for load, copy in zip(loads, copies):
        load.wait()
        copy.start()
    place = lax.axis_index("dp")
    turned = pltpu.roll(vec_ref[...], (LANES - place * strip % LANES) % LANES, 1)
    for row in range(8):
        vectors[row][...] = turned[row, :strip]
    span = bias_ref.shape[1]
    chosen = lax.broadcasted_iota(i32, (8, span), 0) == place * big // width
    line = jnp.sum(jnp.where(chosen, bias_ref[...], 0.0), axis=0, keepdims=True)
    lines = pltpu.roll(jnp.broadcast_to(line, (8, span)), (span - place * big % span) % span, 1)
    bias_out[...] = lines[0, :big]
    for copy in copies:
        copy.wait()


def run_finish(strip, big, width, arrays, vec, bias):
    count = len(arrays)
    V, A = pltpu.VMEM, pl.ANY
    shapes = [jax.ShapeDtypeStruct(array.shape, array.dtype) for array in arrays]
    shapes += [jax.ShapeDtypeStruct((strip,), f32)] * 8 + [jax.ShapeDtypeStruct((big,), f32)]
    return pl.pallas_call(
        functools.partial(finish_kernel, count, strip, big, width),
        out_shape=shapes,
        in_specs=whole_specs([A] * count + [V, V]),
        out_specs=whole_specs([A] * count + [V] * 9),
        scratch_shapes=[pltpu.VMEM(array.shape, array.dtype) for array in arrays] + [pltpu.SemaphoreType.DMA((count,))] * 2,
        name="finish",
    )(*arrays, vec, bias)


def shards(hidden_in, memory, lengths, memory_lengths, self_in, self_out, cross_query, cross_memory, cross_out,
           ffn_in, ffn_bias, ffn_out, out_bias, gain_self, shift_self, gain_cross, shift_cross, gain_ffn, shift_ffn,
           exit_weight, grad_result, grad_halting):
    dp = lax.axis_size("dp")
    sq = lax.axis_size("seq")
    rows, width = hidden_in.shape
    mem_rows = memory.shape[0]
    inner = ffn_in.shape[1]
    sizes = (dp, sq, rows, mem_rows, width, inner)
    strip = width // dp
    big = inner // dp
    piece = min(big, LANES)
    vectors = jnp.stack([gain_self, shift_self, gain_cross, shift_cross, gain_ffn, shift_ffn, out_bias, exit_weight])
    packed_vec = jnp.concatenate([
        jnp.pad(vectors, ((0, 0), (0, LANES - strip))),
        jnp.pad(ffn_bias.reshape(big // piece, piece), ((0, 8 - big // piece), (0, LANES - piece)))])
    outs = run_layer(
        sizes, (lengths, memory_lengths, hidden_in, memory, packed_vec, grad_result, grad_halting.reshape(1, rows), self_in,
                cross_memory, self_out, cross_query, cross_out, ffn_in, ffn_out))
    finished = run_finish(strip, big, width, outs[:11], outs[11], outs[12])
    (result, halting, grad_hidden, grad_memory, out_si, out_cm, out_so, out_cq, out_co, out_fi, out_fo) = finished[:11]
    small, grad_bias = finished[11:19], finished[19]
    return (result, halting.reshape(rows), grad_hidden, grad_memory, out_si, out_so, out_cq, out_cm, out_co, out_fi,
            grad_bias, out_fo, small[6], small[0], small[1], small[2], small[3], small[4], small[5], small[7])


def solution(mesh):
    both = P(("dp", "seq"), None)
    matrix = P("dp", None)
    vector = P("dp")
    return jax.shard_map(
        shards,
        mesh=mesh,
        in_specs=(both, both, vector, vector, matrix, matrix, matrix, matrix, matrix, matrix, vector, matrix)
        + (vector,) * 8 + (both, P(("dp", "seq"))),
        out_specs=(both, P(("dp", "seq")), both, both) + (matrix,) * 6 + (vector, matrix) + (vector,) * 8,
        check_vma=False,
    )
```

```python
import functools
import jax
import jax.numpy as jnp
from jax import lax
from jax.experimental import pallas as pl
from jax.experimental.pallas import tpu as pltpu
from jax.sharding import PartitionSpec as P

bf16 = jnp.bfloat16
f32 = jnp.float32
i32 = jnp.int32
MESH = pl.DeviceIdType.MESH
HD = 64
LANES = 128
epsilon = 1e-05
masked_score = -1e30
gelu_scale = 0.7978845608028654
gelu_cubic = 0.044715
log2_e = 1.4426950408889634


def nn(left, right):
    return jnp.dot(left, right, preferred_element_type=f32)


def nt(left, right, precision=None):
    return lax.dot_general(
        left, right, (((1,), (1,)), ((), ())), preferred_element_type=f32, precision=precision
    )


def tn(left, right):
    return lax.dot_general(
        left, right, (((0,), (0,)), ((), ())), preferred_element_type=f32
    )


def many(count, step):
    if count <= 8:
        for index in range(count):
            step(index)
    else:
        lax.fori_loop(0, count, lambda index, carry: (step(index), carry)[1], 0)


def tiles(rows, size, step):
    lax.fori_loop(0, rows // size, lambda index, carry: (step(pl.ds(pl.multiple_of(index * size, size), size)), carry)[1], 0)


def unit_rows(value):
    average = jnp.mean(value, axis=-1, keepdims=True)
    centred = value - average
    variance = jnp.mean(centred * centred, axis=-1, keepdims=True)
    inverse = lax.rsqrt(variance + epsilon)
    return centred * inverse, inverse


def head_mask(head):
    lane = lax.broadcasted_iota(i32, (1, LANES), 1)
    return (lane < HD) == (head == 0)


def pick(value, mask):
    return jnp.where(mask, value, jnp.zeros_like(value))


def layer_kernel(sizes, *refs):
    dp, sq, rows, mem_rows, width, inner = sizes
    high = dp // 2
    strip = width // dp
    seq_rows = rows * sq
    all_mem = mem_rows * sq
    (len_ref, mlen_ref, hidden_ref, memory_ref, vec_ref, grad_ref, halt_grad_ref, self_in_ref, cross_memory_ref, self_out_ref,
     cross_query_ref, cross_out_ref, ffn_in_ref, ffn_out_ref,
     result_ref, halting_ref, grad_hidden_ref, grad_memory_ref, out_si, out_cm, out_so, out_cq, out_co, out_fi, out_fo, out_vec, out_bias,
     w_cm, w_so, w_cq, w_co, w_fi, w_fo, vec_full, bias_full, after_self, after_cross, normed_two, cross_q,
     mixed, mem_pair, cross_lse, att_tok, q_all, k_all, v_all, self_lse,
     w_in, hid_all, mem_all, vec_all, normed_all, o_heads,
     normed_three, active, grad_inner, slope, branch, cross_branch, grad_mixed, cross_delta,
     grad_heads, grad_in, grad_in_got, part_mem, part_mem_got,
     half_got, pair_got, far_got, sums, sums_seq, last_sums, vec_got, bias_got, quarter_got, last_in,
     g_cm, g_so, g_cq, g_co, g_fi, g_fo, p_cm, p_so, p_cq, p_co, p_fi, p_fo, x_cm, x_so, x_cq, x_co, x_fi, x_fo,
     h_cm, h_so, h_cq, h_co, h_fi, h_fo, f_cm, f_so, f_cq, f_co, f_fi, f_fo, y_cm, y_so, y_cq, y_co, y_fi, y_fo,
     loc_sem, hid_s, hid_r, mem_s, mem_r, vec_s, vec_r, in_s, in_r, z_s, z_r, x_s, x_r, c_s, c_r, a_s, a_r,
     gc_s, gc_r, gx_s, gx_r, gz_s, gz_r, gy_s, gy_r, gp_s, gp_r, gi_s, gi_r, go_s, go_r, gm_s, gm_r, da_s, da_r,
     hop_s, w_s, w_r, gq_s, gq_r, ga_s, ga_r, yh_s, yh_r, yf_s, yf_r, yp_s, yp_r, s1_s, s1_r, s2_s, s2_r) = refs
    me_dp = lax.axis_index("dp")
    me_sq = lax.axis_index("seq")
    me_hi = me_dp // 2
    me_lo = me_dp % 2
    half = me_sq % 2
    pair = me_sq + 1 - 2 * half
    far = (me_sq + 2) % sq
    cross = (pair + 2) % sq
    shards = (cross_memory_ref, self_out_ref, cross_query_ref, cross_out_ref, ffn_in_ref, ffn_out_ref, ffn_out_ref)
    wholes = (w_cm, w_so, w_cq, w_co, w_fi, w_fo, w_fo)

    def remote(src, dst, send, recv, device):
        return pltpu.make_async_remote_copy(src_ref=src, dst_ref=dst, send_sem=send, recv_sem=recv, device_id=device, device_id_type=MESH)

    def other_dp(step):
        return (me_dp + 1 + step) % dp

    barrier = pltpu.get_barrier_semaphore()
    many(dp - 1, lambda k: pl.semaphore_signal(barrier, inc=1, device_id=(other_dp(k), me_sq), device_id_type=MESH))
    for peer in (pair, far, cross):
        pl.semaphore_signal(barrier, inc=1, device_id=(me_dp, peer), device_id_type=MESH)
    pl.semaphore_wait(barrier, dp - 1 + 3)

    def slab_copy(src, dst_all, slab, send, recv, peer):
        return remote(src, dst_all.at[slab], send, recv.at[slab], (me_dp, peer))

    def mem_slab(slab):
        return mem_all.at[pl.ds(pl.multiple_of(slab * mem_rows, mem_rows), mem_rows)]

    def mem_copy(src, slab, send, peer):
        return remote(src, mem_slab(slab), send, mem_r.at[slab], (me_dp, peer))

    own_hidden = pltpu.make_async_copy(hidden_ref, hid_all.at[me_sq], loc_sem.at[0])
    own_memory = pltpu.make_async_copy(memory_ref, mem_slab(me_sq), loc_sem.at[1])
    hid_far = slab_copy(hidden_ref, hid_all, me_sq, hid_s.at[1], hid_r, far)
    hid_pair = slab_copy(hidden_ref, hid_all, me_sq, hid_s.at[0], hid_r, pair)
    mem_far = mem_copy(memory_ref, me_sq, mem_s.at[1], far)
    mem_pair_copy = mem_copy(memory_ref, me_sq, mem_s.at[0], pair)
    hid_next = slab_copy(hid_all.at[far], hid_all, far, hid_s.at[2], hid_r, pair)
    mem_next = mem_copy(mem_slab(far), far, mem_s.at[2], pair)

    def vec_copy(peer, slot):
        return remote(vec_ref, vec_all.at[slot], vec_s.at[peer], vec_r.at[slot], (peer, me_sq))

    def in_copy(part, peer, slot):
        return remote(
            self_in_ref.at[:, pl.ds(pl.multiple_of(part * width + me_sq * LANES, LANES), LANES)],
            w_in.at[pl.ds(pl.multiple_of(slot * strip, strip), strip), pl.ds(part * LANES, LANES)],
            in_s.at[part, peer], in_r.at[part, slot], (peer, me_sq))

    own_vec = pltpu.make_async_copy(vec_ref, vec_all.at[me_dp], loc_sem.at[2])
    own_in = [pltpu.make_async_copy(
        self_in_ref.at[:, pl.ds(pl.multiple_of(part * width + me_sq * LANES, LANES), LANES)],
        w_in.at[pl.ds(pl.multiple_of(me_dp * strip, strip), strip), pl.ds(part * LANES, LANES)],
        loc_sem.at[3 + part]) for part in range(3)]

    hid_far.start()
    hid_pair.start()
    many(dp - 1, lambda k: vec_copy(other_dp(k), me_dp).start())
    many(dp - 1, lambda k: [in_copy(part, other_dp(k), me_dp).start() for part in range(3)])
    own_hidden.start()
    own_memory.start()
    own_vec.start()
    for copy in own_in:
        copy.start()

    def half_columns(index, side):
        size = shards[index].shape[1] // 2
        return pl.ds(pl.multiple_of(side * size, LANES), size)

    def columns(index, side=None):
        side = half if side is None else side
        if index < 4:
            return half_columns(index, side)
        size = shards[index].shape[1] // 4
        part = me_sq // 2 if index == 4 else index - 5
        return pl.ds(pl.multiple_of((side * 2 + part) * size, LANES), size)

    def sent_columns(index, side):
        return half_columns(index, side) if index <= 4 else columns(index, side)

    def block_rows(index, slot):
        size = shards[index].shape[0]
        return pl.ds(pl.multiple_of(slot * size, size), size)

    def z_copy(index, peer, slot):
        return remote(shards[index].at[:, columns(index)], wholes[index].at[block_rows(index, slot * 2 + me_lo), columns(index)],
                      z_s.at[index, peer], z_r.at[index, slot], (peer * 2 + me_lo, me_sq))

    def x_copy(index, slot, low, own):
        there = wholes[index].at[block_rows(index, slot * 2 + low), columns(index)]
        src = shards[index].at[:, columns(index)] if own else there
        return remote(src, there, x_s.at[index, slot], x_r.at[index, slot], (me_hi * 2 + 1 - me_lo, me_sq))

    def c_copy(index):
        there = wholes[index].at[:, sent_columns(index, half)]
        return remote(there, there, c_s.at[index], c_r.at[index], (me_dp, pair))

    def c_wait(index):
        there = wholes[index].at[:, sent_columns(index, 1 - half)]
        remote(there, there, c_s.at[index], c_r.at[index], (me_dp, pair)).wait_recv()

    def w_copy(index, block):
        there = wholes[index].at[block_rows(index, block), columns(index)]
        return remote(there, there, w_s.at[index - 4, block], w_r.at[index - 4, block], (me_dp, far))

    def w_wait(index, block):
        size = shards[index].shape[1] // 4
        there = wholes[index].at[block_rows(index, block), pl.ds(pl.multiple_of((half * 2 + far // 2) * size, LANES), size)]
        remote(there, there, w_s.at[index - 4, block], w_r.at[index - 4, block], (me_dp, far)).wait_recv()

    def own_copy(index):
        return pltpu.make_async_copy(shards[index].at[:, columns(index)], wholes[index].at[block_rows(index, me_dp), columns(index)], loc_sem.at[6 + index])

    def other_hi(step):
        return (me_hi + 1 + step) % high

    def own_stage(index):
        x_copy(index, me_hi, me_lo, True).start()
        own_copy(index).start()

    line = high == 4

    def unless_outer(block, step):
        if line:
            pl.when((block - me_hi) * (block - me_hi) != 9)(step)
        else:
            step()

    def hop_copy(index):
        block = 3 * (2 - me_hi) % 4
        there = wholes[index].at[block_rows(index, block * 2 + me_lo), columns(index)]
        return remote(there, there, hop_s.at[index], z_r.at[index, block], ((3 - block) * 2 + me_lo, me_sq))

    def first_stage(index):
        many(high - 1, lambda k: unless_outer(other_hi(k), lambda: z_copy(index, other_hi(k), me_hi).start()))

    def arrive_high(index, block):
        z_copy(index, block, block).wait_recv()
        x_copy(index, block, me_lo, False).start()
        if index == 4:
            w_copy(index, block * 2 + me_lo).start()

    def second_stage(index):
        if index == 4:
            own_copy(index).wait()
            w_copy(index, me_dp).start()
        many(high - 1, lambda k: unless_outer(other_hi(k), lambda: arrive_high(index, other_hi(k))))
        if line:
            pl.when((me_hi == 1) | (me_hi == 2))(lambda: hop_copy(index).start())

    def late_stage(index):
        if line:
            pl.when((me_hi == 0) | (me_hi == 3))(lambda: arrive_high(index, 3 - me_hi))

    def third_stage(index):
        def arrive(k):
            x_copy(index, k, 1 - me_lo, False).wait_recv()
            if index == 4:
                w_copy(index, k * 2 + 1 - me_lo).start()
        many(high, arrive)
        if index != 4:
            own_copy(index).wait()
            c_copy(index).start()

    def fourth_stage(index):
        many(dp, lambda k: w_wait(index, k))
        c_copy(index).start()

    def finish_weight(index):
        many(high - 1, lambda k: unless_outer(other_hi(k), lambda: z_copy(index, other_hi(k), me_hi).wait_send()))
        if line:
            pl.when((me_hi == 1) | (me_hi == 2))(lambda: hop_copy(index).wait_send())
        many(high, lambda k: x_copy(index, k, me_lo, False).wait_send())
        if index == 4:
            many(dp, lambda k: w_copy(index, k).wait_send())
        c_copy(index).wait_send()

    for index in (0, 1, 2, 4, 5, 6, 3):
        own_stage(index)

    own_vec.wait()
    many(dp - 1, lambda k: vec_copy(other_dp(k), other_dp(k)).wait_recv())
    vec_full[...] = jnp.zeros_like(vec_full)
    bias_full[...] = jnp.zeros_like(bias_full)
    lane_k = lax.broadcasted_iota(i32, (LANES, width), 0)
    lane_j = lax.broadcasted_iota(i32, (LANES, width), 1)
    big = inner // dp
    piece = min(big, LANES)
    big_k = lax.broadcasted_iota(i32, (LANES, inner), 0)
    big_j = lax.broadcasted_iota(i32, (LANES, inner), 1)

    def place(slot):
        hot = ((lane_j - slot * strip == lane_k) & (lane_k < strip)).astype(f32).astype(bf16)
        vec_full[...] = vec_full[...] + nn(vec_all[slot], hot)[:8]
        for part in range(big // piece):
            wide = ((big_j - slot * big - part * piece == big_k) & (big_k < piece)).astype(f32).astype(bf16)
            bias_full[...] = bias_full[...] + nn(vec_all[slot], wide)[8 + part:9 + part]
    lax.fori_loop(0, dp, lambda slot, carry: (place(slot), carry)[1], 0)
    gain_one, shift_one = vec_full[0:1], vec_full[1:2]
    gain_two, shift_two = vec_full[2:3], vec_full[3:4]

    def norm_slab(slab):
        def step(place_rows):
            unit, _ = unit_rows(hid_all[slab, place_rows].astype(f32))
            start = pl.multiple_of(slab * rows + place_rows.start, place_rows.size)
            normed_all[pl.ds(start, place_rows.size)] = (unit * gain_one + shift_one).astype(bf16)
        tiles(rows, 256, step)

    def project_slab(slab):
        def step(place_rows):
            here = pl.ds(pl.multiple_of(slab * rows + place_rows.start, place_rows.size), place_rows.size)
            packed = nn(normed_all[here], w_in[...]).astype(bf16)
            q_all[here] = packed[:, :LANES]
            k_all[here] = packed[:, LANES:2 * LANES]
            v_all[here] = packed[:, 2 * LANES:]
        tiles(rows, 256, step)

    own_hidden.wait()
    norm_slab(me_sq)
    hid_pair_in = slab_copy(hid_all.at[pair], hid_all, pair, hid_s.at[0], hid_r, pair)
    hid_pair_in.wait_recv()
    norm_slab(pair)
    for copy in own_in:
        copy.wait()
    many(dp - 1, lambda k: [in_copy(part, other_dp(k), other_dp(k)).wait_recv() for part in range(3)])
    for index in (0, 1, 2):
        first_stage(index)
    project_slab(me_sq)
    project_slab(pair)
    slab_copy(hid_all.at[far], hid_all, far, hid_s.at[1], hid_r, far).wait_recv()
    hid_next.start()
    mem_far.start()
    mem_pair_copy.start()
    norm_slab(far)
    project_slab(far)
    slab_copy(hid_all.at[cross], hid_all, cross, hid_s.at[2], hid_r, pair).wait_recv()
    norm_slab(cross)
    project_slab(cross)

    limit = len_ref[0]
    mem_limit = mlen_ref[0]
    scale = HD ** (-0.5) * log2_e

    def softmax_block(scores, values):
        largest = jnp.max(scores, axis=1, keepdims=True)
        powers = jnp.exp2(scores - largest)
        total = jnp.sum(powers, axis=1, keepdims=True)
        return nn(powers.astype(bf16), values) / total, largest + jnp.log2(total)

    def att_copy(block, owner):
        return remote(o_heads.at[pl.ds(pl.multiple_of(block * rows, rows), rows)],
                      att_tok.at[:, pl.ds(pl.multiple_of(owner * LANES, LANES), LANES)],
                      a_s.at[block], a_r.at[owner], (me_dp, block))

    def self_block(block):
        here = pl.ds(block * rows, rows)
        query = q_all[here]
        head_queries = [pick(query, head_mask(head)) for head in range(2)]

        def key_part(index, carry, diagonal):
            there = pl.ds(pl.multiple_of(index * rows, rows), rows)
            place = index * rows + lax.broadcasted_iota(i32, (1, rows), 1)
            bias = jnp.where(place < limit, 0.0, masked_score)
            held = []
            for head in range(2):
                largest, total, out = carry[3 * head:3 * head + 3]
                scores = nt(head_queries[head], k_all[there]) * scale + bias
                if diagonal:
                    scores = jnp.where(lax.broadcasted_iota(i32, (rows, rows), 1) <= lax.broadcasted_iota(i32, (rows, rows), 0), scores, masked_score)
                higher = jnp.maximum(largest, jnp.max(scores, axis=1, keepdims=True))
                powers = jnp.exp2(scores - higher)
                shrink = jnp.exp2(largest - higher)
                total = total * shrink + jnp.sum(powers, axis=1, keepdims=True)
                held += [higher, total, out * shrink + nn(powers.astype(bf16), v_all[there])]
            return tuple(held)

        carry = (jnp.full((rows, 1), -3e38, f32), jnp.zeros((rows, 1), f32), jnp.zeros((rows, LANES), f32)) * 2
        if block:
            carry = lax.fori_loop(0, block, lambda index, held: key_part(index, held, False), carry)
        carry = key_part(block, carry, True)
        outs = [carry[3 * head + 2] / carry[3 * head + 1] for head in range(2)]
        spreads = [carry[3 * head] + jnp.log2(carry[3 * head + 1]) for head in range(2)]
        o_heads[here] = jnp.where(head_mask(0), outs[0], outs[1]).astype(bf16)
        turned = jnp.transpose(jnp.where(head_mask(0), spreads[0], spreads[1]))
        self_lse[0:1, here] = turned[0:1]
        self_lse[1:2, here] = turned[HD:HD + 1]

        @pl.when(me_sq != block)
        def _():
            att_copy(block, me_sq).start()

    def forward_memory():
        mem_copy(mem_slab(far), far, mem_s.at[1], far).wait_recv()
        mem_next.start()

    def each(stage, *indices):
        for index in indices:
            stage(index)

    comm_steps = {3: lambda: (each(second_stage, 0, 1, 2), first_stage(5)),
                  2: lambda: (forward_memory(), each(late_stage, 0, 1, 2), second_stage(4), first_stage(6)),
                  1: lambda: (late_stage(4), first_stage(3)), 0: lambda: (third_stage(0), second_stage(5))}
    first_stage(4)
    for block in range(sq - 1, -1, -1):
        self_block(block)
        comm_steps[block]()
    each(third_stage, 1, 2)
    late_stage(5)
    att_tok[:, pl.ds(pl.multiple_of(me_sq * LANES, LANES), LANES)] = o_heads[pl.ds(pl.multiple_of(me_sq * rows, rows), rows)]

    own_memory.wait()
    mem_copy(mem_slab(pair), pair, mem_s.at[0], pair).wait_recv()
    mem_copy(mem_slab(cross), cross, mem_s.at[2], pair).wait_recv()
    c_wait(0)

    def project_memory(slab, carry):
        place = pl.ds(pl.multiple_of(slab * mem_rows, mem_rows), mem_rows)
        mem_pair[place] = nn(mem_all[place], w_cm[...]).astype(bf16)
        return carry
    lax.fori_loop(0, sq, project_memory, 0)

    for peer in (pair, far, cross):
        att_copy(peer, peer).wait_recv()
    c_wait(1)
    c_wait(2)

    def step_two(here):
        value = hidden_ref[here].astype(f32) + nn(att_tok[here], w_so[...])
        after_self[here] = value
        unit, _ = unit_rows(value)
        normed = (unit * gain_two + shift_two).astype(bf16)
        normed_two[here] = normed
        cross_q[here] = nn(normed, w_cq[...]).astype(bf16)
    tiles(rows, 256, step_two)

    mem_bias = jnp.where(lax.broadcasted_iota(i32, (1, all_mem), 1) < mem_limit, 0.0, masked_score)

    def cross_pair(number, held):
        lanes = pl.ds(pl.multiple_of(number * LANES, LANES), LANES)
        value_lanes = pl.ds(pl.multiple_of(width + number * LANES, LANES), LANES)
        query = cross_q[:, lanes]
        outs, spreads = [], []
        for head in range(2):
            scores = nt(pick(query, head_mask(head)), mem_pair[:, lanes]) * scale + mem_bias
            out, spread = softmax_block(scores, mem_pair[:, value_lanes])
            outs.append(out)
            spreads.append(spread)
        mixed[:, lanes] = jnp.where(head_mask(0), outs[0], outs[1]).astype(bf16)
        turned = jnp.transpose(jnp.where(head_mask(0), spreads[0], spreads[1]))
        cross_lse[pl.ds(2 * number, 1)] = turned[0:1]
        cross_lse[pl.ds(2 * number + 1, 1)] = turned[HD:HD + 1]
        return held

    pairs = width // LANES
    each(second_stage, 6, 3)
    third_stage(4)
    lax.fori_loop(0, 1, cross_pair, 0)
    each(late_stage, 6, 3)
    third_stage(5)
    lax.fori_loop(1, 2, cross_pair, 0)
    fourth_stage(4)
    lax.fori_loop(2, 3, cross_pair, 0)
    each(third_stage, 6, 3)
    lax.fori_loop(3, pairs, cross_pair, 0)
    c_wait(3)

    def step_three(here):
        after_cross[here] = after_self[here] + nn(mixed[here], w_co[...])
    tiles(rows, 256, step_three)

    c_wait(4)
    c_wait(5)
    c_wait(6)
    gain_three, shift_three, outer_bias, exit_row = vec_full[4:5], vec_full[5:6], vec_full[6:7], vec_full[7:8]
    parts = ((g_cm, p_cm, x_cm, h_cm, f_cm, y_cm, out_cm), (g_so, p_so, x_so, h_so, f_so, y_so, out_so),
             (g_cq, p_cq, x_cq, h_cq, f_cq, y_cq, out_cq), (g_co, p_co, x_co, h_co, f_co, y_co, out_co),
             (g_fi, p_fi, x_fi, h_fi, f_fi, y_fi, out_fi), (g_fo, p_fo, x_fo, h_fo, f_fo, y_fo, out_fo))
    chunk = 512

    def norm_back(grad, unit, inverse, gain):
        scaled = grad * gain
        first = jnp.mean(scaled, axis=-1, keepdims=True)
        second = jnp.mean(scaled * unit, axis=-1, keepdims=True)
        return inverse * (scaled - first - unit * second)

    def add_sum(index, value):
        sums[index:index + 1] = sums[index:index + 1] + jnp.sum(value, axis=0, keepdims=True)

    def gc_copy(index):
        size = shards[index].shape[1] // 2
        other = pl.ds(pl.multiple_of((1 - half) * size, LANES), size)
        return remote(parts[index][0].at[:, :, :, other], parts[index][1], gc_s.at[index], gc_r.at[index], (me_dp, pair))

    def gq_copy():
        return remote(parts[5][1].at[:, :, :, part_columns(5, far // 2)], quarter_got, gq_s.at[0], gq_r.at[0], (me_dp, far))

    def ga_copy(owner, peer):
        size = shards[5].shape[1] // 4
        there = out_fo.at[:, pl.ds(pl.multiple_of((owner % 2 * 2 + owner // 2) * size, LANES), size)]
        return remote(there, there, ga_s.at[peer], ga_r.at[owner], (me_dp, peer))

    def gx_copy(index):
        src = parts[index][1].at[:, 1 - me_lo, :, part_columns(index, me_sq // 2)] if index == 5 else parts[index][1].at[:, 1 - me_lo]
        return remote(src, parts[index][2], gx_s.at[index], gx_r.at[index], (me_hi * 2 + 1 - me_lo, me_sq))

    def gz_copy(index, peer, slot):
        return remote(parts[index][2].at[peer], parts[index][3].at[slot], gz_s.at[index, peer], gz_r.at[index, slot], (peer * 2 + me_lo, me_sq))

    def gy_copy(index):
        return remote(parts[index][4], parts[index][5], gy_s.at[index], gy_r.at[index], (me_dp, far))

    def gp_copy(index, side):
        size = shards[index].shape[1] // 2
        there = parts[index][6].at[:, pl.ds(pl.multiple_of(side * size, LANES), size)]
        return remote(there, there, gp_s.at[index], gp_r.at[index], (me_dp, pair))

    def reduce_pair(index):
        gc_copy(index).start()

    def reduce_low(index):
        gc_copy(index).wait_recv()
        whole_ref, part_ref = parts[index][0], parts[index][1]

        def add(place, carry):
            for low in range(2):
                part_ref[place, low] = (part_ref[place, low].astype(f32) + whole_ref[place, low, :, half_columns(index, half)].astype(f32)).astype(bf16)
            return carry
        lax.fori_loop(0, high, add, 0)
        if index == 5:
            gq_copy().start()
        else:
            gx_copy(index).start()

    def part_columns(index, side):
        size = shards[index].shape[1] // 4
        return pl.ds(pl.multiple_of(side * size, LANES), size)

    def reduce_across(index):
        gq_copy().wait_recv()
        part_ref = parts[index][1]

        def add(place, carry):
            for low in range(2):
                mine = part_columns(index, me_sq // 2)
                part_ref[place, low, :, mine] = (part_ref[place, low, :, mine].astype(f32) + quarter_got[place, low].astype(f32)).astype(bf16)
            return carry
        lax.fori_loop(0, high, add, 0)
        gx_copy(index).start()

    def reduce_high(index):
        gx_copy(index).wait_recv()
        part_ref, low_ref = parts[index][1], parts[index][2]

        def add(place, carry):
            mine = part_ref[place, me_lo, :, part_columns(index, me_sq // 2)] if index == 5 else part_ref[place, me_lo]
            low_ref[place] = (low_ref[place].astype(f32) + mine.astype(f32)).astype(bf16)
            return carry
        lax.fori_loop(0, high, add, 0)
        many(high - 1, lambda k: gz_copy(index, other_hi(k), me_hi).start())

    def reduce_far(index):
        low_ref, high_ref, far_ref = parts[index][2], parts[index][3], parts[index][4]
        high_ref[me_hi] = low_ref[me_hi]
        many(high - 1, lambda k: gz_copy(index, other_hi(k), other_hi(k)).wait_recv())
        def add(place, held):
            return held + high_ref[place].astype(f32)
        total = lax.fori_loop(1, high, add, high_ref[0].astype(f32))
        far_ref[...] = total if index == 5 else total.astype(bf16)
        if index == 5:
            size = shards[index].shape[1] // 4
            parts[index][6][:, pl.ds(pl.multiple_of((half * 2 + me_sq // 2) * size, LANES), size)] = far_ref[...]
            for peer in (far, cross, pair):
                ga_copy(me_sq, peer).start()
        else:
            gy_copy(index).start()

    def reduce_last(index):
        far_ref, got_ref, out_ref = parts[index][4], parts[index][5], parts[index][6]
        gy_copy(index).wait_recv()
        out_ref[:, half_columns(index, half)] = far_ref[...].astype(f32) + got_ref[...].astype(f32)
        gp_copy(index, half).start()

    def reduce_end(index):
        if index == 5:
            for peer in (far, cross, pair):
                ga_copy(peer, peer).wait_recv()
        else:
            gp_copy(index, 1 - half).wait_recv()

    def reduce_drain(index):
        gc_copy(index).wait_send()
        gx_copy(index).wait_send()
        many(high - 1, lambda k: gz_copy(index, other_hi(k), me_hi).wait_send())
        if index == 5:
            gq_copy().wait_send()
            for peer in (far, cross, pair):
                ga_copy(me_sq, peer).wait_send()
        else:
            gy_copy(index).wait_send()
            gp_copy(index, half).wait_send()

    def weight_grad(index, left, rights):
        out_ref = parts[index][0]
        size = shards[index].shape[0]
        pieces = chunk // size

        def step(tile, carry):
            features = left(tile)
            for number, right in enumerate(rights):
                value = tn(features, right())
                cols = pl.ds(number * value.shape[1], value.shape[1])
                for piece in range(pieces):
                    place = tile * pieces + piece
                    out_ref[place // 2, place % 2, :, cols] = value[piece * size:(piece + 1) * size].astype(bf16)
            return carry
        lax.fori_loop(0, size * dp // chunk, step, 0)

    def feature_tile(ref):
        return lambda tile: ref[:, pl.ds(pl.multiple_of(tile * chunk, chunk), chunk)]

    hid_next.wait_send()
    for index in range(7):
        finish_weight(index)
    grad_res = grad_hidden_ref
    grad_packed, sum_in, turned_q = w_fo, after_cross, slope
    packed_cols = pl.ds(0, 3 * LANES)
    turned_rows = pl.ds(0, LANES)
    sums[...] = jnp.zeros_like(sums)
    halting_ref[...] = jnp.zeros_like(halting_ref)

    def ffn_step(here):
        size = here.size
        unit, inverse = unit_rows(after_cross[here])
        normed = (unit * gain_three + shift_three).astype(bf16)
        normed_three[here] = normed
        out = after_cross[here] + outer_bias
        for part in range(inner // chunk):
            cols = pl.ds(part * chunk, chunk)
            pre = nn(normed, w_fi[:, cols]) + bias_full[:, cols]
            square = pre * pre
            bent = jnp.tanh(gelu_scale * (pre + gelu_cubic * square * pre))
            act = (0.5 * pre * (1.0 + bent)).astype(bf16)
            active[part, here] = act
            slope[:, cols] = 0.5 * (1.0 + bent) + 0.5 * pre * (1.0 - bent * bent) * gelu_scale * (1.0 + 3.0 * gelu_cubic * square)
            out = out + nn(act, w_fo[cols])
        result_ref[here] = out.astype(bf16)
        halt = 1.0 / (1.0 + jnp.exp(-jnp.sum(out * exit_row, axis=-1, keepdims=True)))
        place = here.start + lax.broadcasted_iota(i32, (size, rows), 0)
        same = place == lax.broadcasted_iota(i32, (size, rows), 1)
        halting_ref[...] = halting_ref[...] + jnp.sum(jnp.where(same, halt, 0.0), axis=0, keepdims=True)
        halt_grad = jnp.sum(jnp.where(same, halt_grad_ref[...], 0.0), axis=1, keepdims=True)
        live = (me_sq * rows + here.start + lax.broadcasted_iota(i32, (size, 1), 0) < limit).astype(f32)
        grad_logit = halt_grad * live * halt * (1.0 - halt)
        add_sum(7, grad_logit * out)
        grad_out = grad_ref[here].astype(f32) * live + grad_logit * exit_row
        grad_branch = grad_out.astype(bf16)
        branch[here] = grad_branch
        add_sum(6, grad_branch.astype(f32))
        grad_normed = jnp.zeros((size, width), f32)
        for part in range(inner // chunk):
            cols = pl.ds(part * chunk, chunk)
            grad_part = (nt(grad_branch, w_fo[cols]) * slope[:, cols]).astype(bf16)
            grad_inner[part, here] = grad_part
            add_sum(8 + part, grad_part.astype(f32))
            grad_normed = grad_normed + nt(grad_part, w_fi[:, cols])
        add_sum(4, grad_normed * unit)
        add_sum(5, grad_normed)
        grad_cross = grad_out + norm_back(grad_normed, unit, inverse, gain_three)
        grad_res[here] = grad_cross
        grad_cross_branch = grad_cross.astype(bf16)
        cross_branch[here] = grad_cross_branch
        grad_mixed[here] = nt(grad_cross_branch, w_co[...]).astype(bf16)
    tiles(rows, 256, ffn_step)
    weight_grad(5, lambda tile: active[tile], [lambda: branch[...]])
    reduce_pair(5)
    weight_grad(4, feature_tile(normed_three), [functools.partial(lambda part: grad_inner[part], part) for part in range(inner // chunk)])
    reduce_pair(4)
    weight_grad(3, feature_tile(mixed), [lambda: cross_branch[...]])
    reduce_pair(3)

    select = (lax.broadcasted_iota(i32, (8, width), 1) // HD == lax.broadcasted_iota(i32, (8, width), 0)).astype(f32)
    cross_delta[...] = nt(select, grad_mixed[...].astype(f32) * mixed[...].astype(f32), lax.Precision.HIGHEST)
    score_scale = HD ** (-0.5)

    def attend_back(keys, values, query, grad, spread_rows, delta_rows, bias, mask):
        grad_keys, grad_values, grad_query = None, None, None
        for head in range(2):
            only = head_mask(head)
            head_keys = pick(keys, only)
            scores = nt(head_keys, query) * scale + bias
            if mask is not None:
                scores = jnp.where(mask, scores, masked_score)
            powers = jnp.exp2(scores - spread_rows[head])
            grad_powers = nt(pick(values, only), grad)
            grad_scores = (powers * (grad_powers - delta_rows[head])).astype(bf16)
            value_part = nn(powers.astype(bf16), pick(grad, only))
            key_part = nn(grad_scores, pick(query, only))
            query_part = nn(jnp.transpose(head_keys), grad_scores)
            grad_values = value_part if head == 0 else grad_values + value_part
            grad_keys = key_part if head == 0 else grad_keys + key_part
            grad_query = query_part if head == 0 else grad_query + query_part
        return grad_keys, grad_values, grad_query

    key_block = 512
    key_blocks = all_mem // key_block
    grad_pair = active
    grad_cq = branch
    grad_att = normed_three
    part_hid = hid_all
    cross_comm = {0: lambda: (reduce_low(5), reduce_low(4)), 1: lambda: reduce_low(3), 2: lambda: None, 3: lambda: None}
    def cross_back(number, held):
        lanes = pl.ds(pl.multiple_of(number * LANES, LANES), LANES)
        value_lanes = pl.ds(pl.multiple_of(width + number * LANES, LANES), LANES)

        def block_step(block, total):
            here = pl.ds(pl.multiple_of(block * key_block, key_block), key_block)
            key_place = block * key_block + lax.broadcasted_iota(i32, (key_block, 1), 0)
            grad_keys, grad_values, grad_query = attend_back(
                mem_pair[here, lanes], mem_pair[here, value_lanes], cross_q[:, lanes], grad_mixed[:, lanes],
                [cross_lse[pl.ds(2 * number + head, 1)] for head in range(2)],
                [cross_delta[pl.ds(2 * number + head, 1)] for head in range(2)],
                jnp.where(key_place < mem_limit, 0.0, masked_score), None)
            grad_pair[block, :, lanes] = (grad_keys * score_scale).astype(bf16)
            grad_pair[key_blocks + block, :, lanes] = grad_values.astype(bf16)
            return total + grad_query

        total = lax.fori_loop(0, key_blocks, block_step, jnp.zeros((LANES, rows), f32))
        grad_cq[:, lanes] = (jnp.transpose(total) * score_scale).astype(bf16)
        return held

    for number in range(pairs):
        lax.fori_loop(number, number + 1, cross_back, 0)
        cross_comm[number]()

    def step_two_back(here):
        grad_normed = nt(grad_cq[here], w_cq[...])
        unit, inverse = unit_rows(after_self[here])
        add_sum(2, grad_normed * unit)
        add_sum(3, grad_normed)
        grad_self = grad_res[here] + norm_back(grad_normed, unit, inverse, gain_two)
        grad_res[here] = grad_self
        grad_self_branch = grad_self.astype(bf16)
        cross_branch[here] = grad_self_branch
        grad_att[here] = nt(grad_self_branch, w_so[...]).astype(bf16)

    tiles(rows, 256, step_two_back)

    def da_copy(peer, owner):
        return remote(grad_att.at[:, pl.ds(pl.multiple_of(peer * LANES, LANES), LANES)],
                      grad_heads.at[pl.ds(pl.multiple_of(owner * rows, rows), rows)], da_s.at[peer], da_r.at[owner], (me_dp, peer))

    for peer in (far, cross, pair):
        da_copy(peer, me_sq).start()
    grad_heads[pl.ds(pl.multiple_of(me_sq * rows, rows), rows)] = grad_att[:, pl.ds(pl.multiple_of(me_sq * LANES, LANES), LANES)]

    def gm_copy(kind):
        source, target = ((cross, pair), (pair, pair), (far, far))[kind]
        return remote(part_mem.at[source], part_mem_got.at[kind], gm_s.at[kind], gm_r.at[kind], (me_dp, target))

    def memory_pair():
        gm_copy(0).start()
        gm_copy(1).start()

    def memory_far():
        gm_copy(0).wait_recv()
        part_mem[far] = (part_mem[far].astype(f32) + part_mem_got[0].astype(f32)).astype(bf16)
        gm_copy(2).start()

    def memory_end():
        gm_copy(1).wait_recv()
        gm_copy(2).wait_recv()
        grad_memory_ref[...] = (part_mem[me_sq].astype(f32) + part_mem_got[1].astype(f32)) + part_mem_got[2].astype(f32)

    def memory_part(slab, carry):
        per_block = key_block // mem_rows
        place = pl.ds(pl.multiple_of(slab % per_block * mem_rows, mem_rows), mem_rows)
        part_mem[slab] = (nt(grad_pair[slab // per_block, place], w_cm[:, :width])
                          + nt(grad_pair[key_blocks + slab // per_block, place], w_cm[:, width:])).astype(bf16)
        return carry

    reduce_across(5)
    reduce_high(4)
    weight_grad(0, feature_tile(mem_all), [functools.partial(lambda part: grad_pair[part * key_blocks:(part + 1) * key_blocks].reshape(all_mem, width), part) for part in range(2)])
    reduce_pair(0)
    reduce_high(3)
    weight_grad(1, feature_tile(att_tok), [lambda: cross_branch[...]])
    reduce_pair(1)
    weight_grad(2, feature_tile(normed_two), [lambda: grad_cq[...]])
    reduce_pair(2)
    lax.fori_loop(0, sq, memory_part, 0)
    memory_pair()

    def s1_copy(peer, owner):
        return remote(sums, sums_seq.at[owner], s1_s.at[peer], s1_r.at[owner], (me_dp, peer))

    for peer in (pair, far, cross):
        da_copy(peer, peer).wait_recv()
    select_two = (lax.broadcasted_iota(i32, (8, LANES), 1) // HD == lax.broadcasted_iota(i32, (8, LANES), 0)).astype(f32)
    deltas = nt(select_two, grad_heads[...].astype(f32) * o_heads[...].astype(f32), lax.Precision.HIGHEST)
    self_lse[2:4] = deltas[0:2]
    turned_q[turned_rows] = jnp.zeros((LANES, rows * sq), f32)
    half_rows = rows // 2

    def away(block):
        return me_sq // 2 != block // 2

    def away_rows(block):
        return pl.ds(block % 2 * half_rows, half_rows)

    def keep_rows(block):
        @pl.when(away(block))
        def _():
            grad_inner[0, away_rows(block)] = hid_all[block, pl.ds(pl.multiple_of(half * half_rows, half_rows), half_rows)]

    for block in range(sq):
        keep_rows(block)

    def yh_copy(block):
        there = half_got.at[block % 2]
        return remote(part_hid.at[block, pl.ds(pl.multiple_of((1 - half) * half_rows, half_rows), half_rows)], there,
                      yh_s.at[block], yh_r.at[block], (me_dp, pair))

    def yf_copy(block, side):
        return remote(part_hid.at[block, pl.ds(pl.multiple_of(half * half_rows, half_rows), half_rows)], far_got.at[pl.ds(pl.multiple_of(side * half_rows, half_rows), half_rows)],
                      yf_s.at[block], yf_r.at[side], (me_dp, block))

    def yp_copy(block):
        return remote(part_hid.at[block], pair_got, yp_s.at[0], yp_r.at[0], (me_dp, pair))

    def send_part(block):
        @pl.when(away(block))
        def _():
            yh_copy(block).start()

        @pl.when(pair == block)
        def _():
            yp_copy(block).start()

    def forward_part(block):
        @pl.when(away(block))
        def _():
            yh_copy(block).wait_recv()
            place = pl.ds(pl.multiple_of(half * half_rows, half_rows), half_rows)
            both = part_hid[block, place].astype(f32) + half_got[block % 2].astype(f32)
            part_hid[block, place] = both.astype(bf16)
            yf_copy(block, half).start()
            unit, _ = unit_rows(grad_inner[0, away_rows(block)].astype(f32))
            add_sum(0, both * unit)
            add_sum(1, both)

    schedule = {
        (0, 0): lambda: (reduce_high(5), memory_far()), (0, 1): lambda: reduce_low(0), (0, 2): lambda: (reduce_low(1), reduce_low(2)),
        (0, 3): lambda: (reduce_far(4), reduce_far(3)), (0, sq): lambda: (reduce_high(0), reduce_far(5)),
        (1, 1): lambda: forward_part(0), (1, 2): lambda: (reduce_high(1), reduce_high(2), reduce_last(4)),
        (1, sq): lambda: (reduce_far(0), reduce_last(3)), (2, 2): lambda: forward_part(1), (2, sq): lambda: (reduce_far(1), reduce_far(2)),
        (3, 3): lambda: forward_part(2), (3, sq): lambda: reduce_last(0)}

    def comm_point(block, index):
        if (block, index) in schedule:
            schedule[block, index]()

    def gi_copy(peer, slot):
        return remote(grad_in.at[peer], grad_in_got.at[slot], gi_s.at[peer], gi_r.at[slot], (peer, me_sq))

    def input_sums():
        for place in range(dp):
            grad_in[place] = sum_in[place * strip:(place + 1) * strip, packed_cols].astype(bf16)
        many(dp - 1, lambda k: gi_copy(other_dp(k), me_dp).start())

    def key_step(block):
        here = pl.ds(block * rows, rows)
        keys, values = k_all[here], v_all[here]
        bias = jnp.where(block * rows + lax.broadcasted_iota(i32, (rows, 1), 0) < limit, 0.0, masked_score)

        def query_step(index, carry, diagonal):
            def part(there, first, count, mask):
                grad_keys, grad_values, grad_query = attend_back(
                    keys[first:first + count], values[first:first + count], q_all[there], grad_heads[there],
                    [self_lse[head:head + 1, there] for head in range(2)],
                    [self_lse[2 + head:3 + head, there] for head in range(2)], bias[first:first + count], mask)
                turned_q[turned_rows, there] = turned_q[turned_rows, there] + grad_query
                return grad_keys, grad_values

            if not diagonal:
                grad_keys, grad_values = part(pl.ds(pl.multiple_of(index * rows, rows), rows), 0, rows, None)
                return carry[0] + grad_keys, carry[1] + grad_values
            both = []
            for first in (0, half_rows):
                size = rows - first
                mask = lax.broadcasted_iota(i32, (half_rows, size), 0) <= lax.broadcasted_iota(i32, (half_rows, size), 1)
                both.append(part(pl.ds(index * rows + first, size), first, half_rows, mask))
            return tuple(jnp.concatenate([both[0][item], both[1][item]], axis=0) for item in range(2))

        zero = jnp.zeros((rows, LANES), f32)
        carry = query_step(block, (zero, zero), True)
        comm_point(block, block)
        for index in range(block + 1, sq):
            carry = lax.fori_loop(index, index + 1, lambda place, held: query_step(place, held, False), carry)
            comm_point(block, index)
        grad_packed[here, pl.ds(LANES, LANES)] = (carry[0] * score_scale).astype(bf16)
        grad_packed[here, pl.ds(2 * LANES, LANES)] = carry[1].astype(bf16)
        grad_packed[here, pl.ds(0, LANES)] = (jnp.transpose(turned_q[turned_rows, here]) * score_scale).astype(bf16)

        def input_part(tile, held):
            cols = pl.ds(pl.multiple_of(tile * 256, 256), 256)
            value = tn(normed_all[here, cols], grad_packed[here, packed_cols])
            if block == 0:
                sum_in[cols, packed_cols] = value
            else:
                sum_in[cols, packed_cols] = sum_in[cols, packed_cols] + value
            return held
        lax.fori_loop(0, width // 256, input_part, 0)
        if block == sq - 1:
            input_sums()

        def hidden_part(place):
            rows_here = pl.ds(pl.multiple_of(block * rows + place.start, place.size), place.size)
            part_hid[block, place] = nt(grad_packed[rows_here, packed_cols], w_in[...]).astype(bf16)
        tiles(rows, 256, hidden_part)
        send_part(block)

    for block in range(sq):
        key_step(block)
        comm_point(block, sq)
    grad_in_got[me_dp] = grad_in[me_dp]
    forward_part(sq - 1)
    yp_copy(me_sq).wait_recv()

    def own_sums(here):
        grad_normed = part_hid[me_sq, here].astype(f32) + pair_got[here].astype(f32)
        unit, _ = unit_rows(hidden_ref[here].astype(f32))
        add_sum(0, grad_normed * unit)
        add_sum(1, grad_normed)
    tiles(rows, 256, own_sums)
    for peer in (far, cross, pair):
        s1_copy(peer, me_sq).start()

    memory_end()
    reduce_last(1)
    reduce_last(2)

    for peer in (far, cross, pair):
        s1_copy(peer, peer).wait_recv()
    sums_seq[me_sq] = sums[...]
    last_sums[...] = (sums_seq[0] + sums_seq[1]) + (sums_seq[2] + sums_seq[3])

    lanes_two = max(LANES, big)

    def v_blocks(peer):
        return (last_sums.at[pl.ds(0, 8), pl.ds(pl.multiple_of(peer * strip // LANES * LANES, LANES), LANES)],
                last_sums.at[pl.ds(8, 8), pl.ds(pl.multiple_of(peer * big % width // lanes_two * lanes_two, LANES), lanes_two)])

    def v_copy(peer, slot):
        one, two = v_blocks(peer)
        return (remote(one, vec_got.at[slot], s2_s.at[0, peer], s2_r.at[0, slot], (peer, me_sq)),
                remote(two, bias_got.at[slot], s2_s.at[1, peer], s2_r.at[1, slot], (peer, me_sq)))
    many(dp - 1, lambda k: [copy.start() for copy in v_copy(other_dp(k), me_dp)])
    one, two = v_blocks(me_dp)
    vec_got[me_dp] = one[...]
    bias_got[me_dp] = two[...]
    many(dp - 1, lambda k: gi_copy(other_dp(k), other_dp(k)).wait_recv())
    total_in = grad_in_got[0].astype(f32)
    for place in range(1, dp):
        total_in = total_in + grad_in_got[place].astype(f32)

    def go_copy(owner, peer):
        return remote(last_in.at[owner], last_in.at[owner], go_s.at[0, peer], go_r.at[0, owner], (me_dp, peer))
    last_in[me_sq] = total_in.astype(bf16)
    for peer in (far, cross, pair):
        go_copy(me_sq, peer).start()
    yf_copy(me_sq, 0).wait_recv()
    yf_copy(me_sq, 1).wait_recv()

    def last_step(here):
        grad_normed = part_hid[me_sq, here].astype(f32) + pair_got[here].astype(f32) + far_got[here].astype(f32)
        unit, inverse = unit_rows(hidden_ref[here].astype(f32))
        grad_hidden_ref[here] = grad_res[here] + norm_back(grad_normed, unit, inverse, gain_one)
    tiles(rows, 256, last_step)
    many(dp - 1, lambda k: [copy.wait_recv() for copy in v_copy(other_dp(k), other_dp(k))])
    out_vec[...] = vec_got[0]
    out_bias[...] = bias_got[0]

    def add_vec(place, carry):
        out_vec[...] = out_vec[...] + vec_got[place]
        out_bias[...] = out_bias[...] + bias_got[place]
        return carry
    lax.fori_loop(1, dp, add_vec, 0)
    for index in range(6):
        reduce_end(index)
    for peer in (far, cross, pair):
        go_copy(peer, peer).wait_recv()
    for owner in range(sq):
        for part in range(3):
            out_si[:, part * width + owner * LANES:part * width + (owner + 1) * LANES] = last_in[owner, :, part * LANES:(part + 1) * LANES].astype(f32)
    for index in range(6):
        reduce_drain(index)
    for peer in (far, cross, pair):
        da_copy(peer, me_sq).wait_send()
        s1_copy(peer, me_sq).wait_send()
        go_copy(me_sq, peer).wait_send()
    many(dp - 1, lambda k: gi_copy(other_dp(k), me_dp).wait_send())
    many(dp - 1, lambda k: [copy.wait_send() for copy in v_copy(other_dp(k), me_dp)])
    for kind in range(3):
        gm_copy(kind).wait_send()
    yp_copy(pair).wait_send()
    for block in range(sq):
        @pl.when(away(block))
        def _():
            yh_copy(block).wait_send()
            yf_copy(block, half).wait_send()
    for copy in (hid_far, hid_pair, mem_far, mem_pair_copy, mem_next):
        copy.wait_send()
    many(dp - 1, lambda k: vec_copy(other_dp(k), me_dp).wait_send())
    many(dp - 1, lambda k: [in_copy(part, other_dp(k), me_dp).wait_send() for part in range(3)])
    for peer in (pair, far, cross):
        att_copy(peer, me_sq).wait_send()


def whole_specs(names):
    return [pl.BlockSpec(memory_space=name) for name in names]


def run_layer(sizes, args):
    dp, sq, rows, mem_rows, width, inner = sizes
    seq_rows, all_mem = rows * sq, mem_rows * sq
    high, strip, big = dp // 2, width // dp, inner // dp
    V, A, S = pltpu.VMEM, pl.ANY, pltpu.SMEM
    dma = pltpu.SemaphoreType.DMA
    shard_shapes = [(strip, 2 * width), (strip, width), (strip, width), (strip, width), (strip, inner), (big, width)]
    outs = [((rows, width), bf16), ((1, rows), f32), ((rows, width), f32), ((mem_rows, width), f32),
            ((strip, 3 * width), f32)] + [(shape, f32) for shape in shard_shapes] + [((8, LANES), f32), ((8, max(LANES, big)), f32)]
    scratch = [((width, 2 * width), bf16), ((width, width), bf16), ((width, width), bf16), ((width, width), bf16),
               ((width, inner), bf16), ((inner, width), bf16), ((8, width), f32), ((1, inner), f32),
               ((rows, width), f32), ((rows, width), f32), ((rows, width), bf16), ((rows, width), bf16),
               ((rows, width), bf16), ((all_mem, 2 * width), bf16), ((8, rows), f32), ((rows, width), bf16),
               ((seq_rows, LANES), bf16), ((seq_rows, LANES), bf16), ((seq_rows, LANES), bf16), ((8, seq_rows), f32),
               ((width, 3 * LANES), bf16), ((sq, rows, width), bf16), ((all_mem, width), bf16),
               ((dp, 16, LANES), bf16), ((seq_rows, width), bf16), ((seq_rows, LANES), bf16),
               ((rows, width), bf16), ((inner // 512, rows, 512), bf16), ((inner // 512, rows, 512), bf16), ((256, inner), f32),
               ((rows, width), bf16), ((rows, width), bf16), ((rows, width), bf16), ((8, rows), f32),
               ((seq_rows, LANES), bf16),
               ((dp, strip, 3 * LANES), bf16), ((dp, strip, 3 * LANES), bf16),
               ((sq, mem_rows, width), bf16), ((3, mem_rows, width), bf16),
               ((2, rows // 2, width), bf16), ((rows, width), bf16), ((rows, width), bf16),
               ((16, width), f32), ((sq, 16, width), f32), ((16, width), f32), ((dp, 8, LANES), f32), ((dp, 8, max(LANES, big)), f32),
               ((high, 2, big, width // 4), bf16), ((sq, strip, 3 * LANES), bf16)]
    scratch += [((high, 2, size, columns), bf16) for size, columns in shard_shapes]
    scratch += [((high, 2, size, columns // 2), bf16) for size, columns in shard_shapes]
    ways = [2] * 5 + [4]
    scratch += [((high, size, columns // way), bf16) for (size, columns), way in zip(shard_shapes, ways)] * 2
    scratch += [((size, columns // 2), bf16) for size, columns in shard_shapes[:5]] + [((big, width // 4), f32)]
    scratch += [((size, columns // 2), bf16) for size, columns in shard_shapes[:5]] + [((8, LANES), f32)]
    semaphores = [dma((13,)), dma((3,)), dma((sq,)), dma((3,)), dma((sq,)), dma((dp,)), dma((dp,)), dma((3, dp)), dma((3, dp)),
                  dma((7, high)), dma((7, high)), dma((7, high)), dma((7, high)), dma((7,)), dma((7,)), dma((sq,)), dma((sq,)),
                  dma((6,)), dma((6,)), dma((6,)), dma((6,)), dma((6, high)), dma((6, high)), dma((6,)), dma((6,)), dma((6,)), dma((6,)),
                  dma((dp,)), dma((dp,)), dma((3, sq)), dma((3, sq)), dma((sq,)), dma((sq,)), dma((sq,)), dma((sq,)),
                  dma((7,)), dma((1, dp)), dma((1, dp)), dma((1,)), dma((1,)), dma((sq,)), dma((sq,)),
                  dma((sq,)), dma((sq,)), dma((sq,)), dma((2,)), dma((1,)), dma((1,)),
                  dma((sq,)), dma((sq,)), dma((2, dp)), dma((2, dp))]
    return pl.pallas_call(
        functools.partial(layer_kernel, sizes),
        out_shape=[jax.ShapeDtypeStruct(*out) for out in outs],
        in_specs=whole_specs([S, S, V, V, V, V, V, A, A, A, A, A, A, A]),
        out_specs=whole_specs([V] * len(outs)),
        scratch_shapes=[pltpu.VMEM(*item) for item in scratch] + semaphores,
        compiler_params=pltpu.CompilerParams(collective_id=0, has_side_effects=True, vmem_limit_bytes=62 << 20),
        name="layer",
    )(*args)


def finish_kernel(count, strip, big, width, *refs):
    sources, (vec_ref, bias_ref) = refs[:count], refs[count:count + 2]
    targets, vectors, bias_out = refs[count + 2:2 * count + 2], refs[2 * count + 2:2 * count + 10], refs[2 * count + 10]
    held, (sem_in, sem_out) = refs[2 * count + 11:-2], refs[-2:]
    loads = [pltpu.make_async_copy(sources[index], held[index], sem_in.at[index]) for index in range(count)]
    copies = [pltpu.make_async_copy(held[index], targets[index], sem_out.at[index]) for index in range(count)]
    for load in loads:
        load.start()
    for load, copy in zip(loads, copies):
        load.wait()
        copy.start()
    place = lax.axis_index("dp")
    turned = pltpu.roll(vec_ref[...], (LANES - place * strip % LANES) % LANES, 1)
    for row in range(8):
        vectors[row][...] = turned[row, :strip]
    span = bias_ref.shape[1]
    chosen = lax.broadcasted_iota(i32, (8, span), 0) == place * big // width
    line = jnp.sum(jnp.where(chosen, bias_ref[...], 0.0), axis=0, keepdims=True)
    lines = pltpu.roll(jnp.broadcast_to(line, (8, span)), (span - place * big % span) % span, 1)
    bias_out[...] = lines[0, :big]
    for copy in copies:
        copy.wait()


def run_finish(strip, big, width, arrays, vec, bias):
    count = len(arrays)
    V, A = pltpu.VMEM, pl.ANY
    shapes = [jax.ShapeDtypeStruct(array.shape, array.dtype) for array in arrays]
    shapes += [jax.ShapeDtypeStruct((strip,), f32)] * 8 + [jax.ShapeDtypeStruct((big,), f32)]
    return pl.pallas_call(
        functools.partial(finish_kernel, count, strip, big, width),
        out_shape=shapes,
        in_specs=whole_specs([A] * count + [V, V]),
        out_specs=whole_specs([A] * count + [V] * 9),
        scratch_shapes=[pltpu.VMEM(array.shape, array.dtype) for array in arrays] + [pltpu.SemaphoreType.DMA((count,))] * 2,
        name="finish",
    )(*arrays, vec, bias)


def shards(hidden_in, memory, lengths, memory_lengths, self_in, self_out, cross_query, cross_memory, cross_out,
           ffn_in, ffn_bias, ffn_out, out_bias, gain_self, shift_self, gain_cross, shift_cross, gain_ffn, shift_ffn,
           exit_weight, grad_result, grad_halting):
    dp = lax.axis_size("dp")
    sq = lax.axis_size("seq")
    rows, width = hidden_in.shape
    mem_rows = memory.shape[0]
    inner = ffn_in.shape[1]
    sizes = (dp, sq, rows, mem_rows, width, inner)
    strip = width // dp
    big = inner // dp
    piece = min(big, LANES)
    vectors = jnp.stack([gain_self, shift_self, gain_cross, shift_cross, gain_ffn, shift_ffn, out_bias, exit_weight])
    packed_vec = jnp.concatenate([
        jnp.pad(vectors, ((0, 0), (0, LANES - strip))),
        jnp.pad(ffn_bias.reshape(big // piece, piece), ((0, 8 - big // piece), (0, LANES - piece)))])
    outs = run_layer(
        sizes, (lengths, memory_lengths, hidden_in, memory, packed_vec, grad_result, grad_halting.reshape(1, rows), self_in,
                cross_memory, self_out, cross_query, cross_out, ffn_in, ffn_out))
    finished = run_finish(strip, big, width, outs[:11], outs[11], outs[12])
    (result, halting, grad_hidden, grad_memory, out_si, out_cm, out_so, out_cq, out_co, out_fi, out_fo) = finished[:11]
    small, grad_bias = finished[11:19], finished[19]
    return (result, halting.reshape(rows), grad_hidden, grad_memory, out_si, out_so, out_cq, out_cm, out_co, out_fi,
            grad_bias, out_fo, small[6], small[0], small[1], small[2], small[3], small[4], small[5], small[7])


def solution(mesh):
    both = P(("dp", "seq"), None)
    matrix = P("dp", None)
    vector = P("dp")
    return jax.shard_map(
        shards,
        mesh=mesh,
        in_specs=(both, both, vector, vector, matrix, matrix, matrix, matrix, matrix, matrix, vector, matrix)
        + (vector,) * 8 + (both, P(("dp", "seq"))),
        out_specs=(both, P(("dp", "seq")), both, both) + (matrix,) * 6 + (vector, matrix) + (vector,) * 8,
        check_vma=False,
    )
```

```python
import functools
import jax
import jax.numpy as jnp
from jax import lax
from jax.experimental import pallas as pl
from jax.experimental.pallas import tpu as pltpu
from jax.sharding import PartitionSpec as P

bf16 = jnp.bfloat16
f32 = jnp.float32
i32 = jnp.int32
MESH = pl.DeviceIdType.MESH
HD = 64
LANES = 128
epsilon = 1e-05
masked_score = -1e30
gelu_scale = 0.7978845608028654
gelu_cubic = 0.044715
log2_e = 1.4426950408889634


def nn(left, right):
    return jnp.dot(left, right, preferred_element_type=f32)


def nt(left, right, precision=None):
    return lax.dot_general(
        left, right, (((1,), (1,)), ((), ())), preferred_element_type=f32, precision=precision
    )


def tn(left, right):
    return lax.dot_general(
        left, right, (((0,), (0,)), ((), ())), preferred_element_type=f32
    )


def many(count, step):
    if count <= 8:
        for index in range(count):
            step(index)
    else:
        lax.fori_loop(0, count, lambda index, carry: (step(index), carry)[1], 0)


def tiles(rows, size, step):
    lax.fori_loop(0, rows // size, lambda index, carry: (step(pl.ds(pl.multiple_of(index * size, size), size)), carry)[1], 0)


def unit_rows(value):
    average = jnp.mean(value, axis=-1, keepdims=True)
    centred = value - average
    variance = jnp.mean(centred * centred, axis=-1, keepdims=True)
    inverse = lax.rsqrt(variance + epsilon)
    return centred * inverse, inverse


def head_mask(head):
    lane = lax.broadcasted_iota(i32, (1, LANES), 1)
    return (lane < HD) == (head == 0)


def pick(value, mask):
    return jnp.where(mask, value, jnp.zeros_like(value))


def layer_kernel(sizes, *refs):
    dp, sq, rows, mem_rows, width, inner = sizes
    high = dp // 2
    strip = width // dp
    seq_rows = rows * sq
    all_mem = mem_rows * sq
    (len_ref, mlen_ref, hidden_ref, memory_ref, vec_ref, grad_ref, halt_grad_ref, self_in_ref, cross_memory_ref, self_out_ref,
     cross_query_ref, cross_out_ref, ffn_in_ref, ffn_out_ref,
     result_ref, halting_ref, grad_hidden_ref, grad_memory_ref, out_si, out_cm, out_so, out_cq, out_co, out_fi, out_fo, out_vec, out_bias,
     w_cm, w_so, w_cq, w_co, w_fi, w_fo, vec_full, bias_full, after_self, after_cross, normed_two, cross_q,
     mixed, mem_pair, cross_lse, att_tok, q_all, k_all, v_all, self_lse,
     w_in, hid_all, mem_all, vec_all, normed_all, o_heads,
     normed_three, active, grad_inner, slope, branch, cross_branch, grad_mixed, cross_delta,
     grad_heads, grad_in, grad_in_got, part_mem, part_mem_got,
     half_got, pair_got, far_got, sums, sums_seq, last_sums, vec_got, bias_got, quarter_got, last_in,
     g_cm, g_so, g_cq, g_co, g_fi, g_fo, p_cm, p_so, p_cq, p_co, p_fi, p_fo, x_cm, x_so, x_cq, x_co, x_fi, x_fo,
     h_cm, h_so, h_cq, h_co, h_fi, h_fo, f_cm, f_so, f_cq, f_co, f_fi, f_fo, y_cm, y_so, y_cq, y_co, y_fi, y_fo,
     loc_sem, hid_s, hid_r, mem_s, mem_r, vec_s, vec_r, in_s, in_r, z_s, z_r, x_s, x_r, c_s, c_r, a_s, a_r,
     gc_s, gc_r, gx_s, gx_r, gz_s, gz_r, gy_s, gy_r, gp_s, gp_r, gi_s, gi_r, go_s, go_r, gm_s, gm_r, da_s, da_r,
     hop_s, w_s, w_r, gq_s, gq_r, ga_s, ga_r, yh_s, yh_r, yf_s, yf_r, yp_s, yp_r, s1_s, s1_r, s2_s, s2_r) = refs
    me_dp = lax.axis_index("dp")
    me_sq = lax.axis_index("seq")
    me_hi = me_dp // 2
    me_lo = me_dp % 2
    half = me_sq % 2
    pair = me_sq + 1 - 2 * half
    far = (me_sq + 2) % sq
    cross = (pair + 2) % sq
    shards = (cross_memory_ref, self_out_ref, cross_query_ref, cross_out_ref, ffn_in_ref, ffn_out_ref, ffn_out_ref)
    wholes = (w_cm, w_so, w_cq, w_co, w_fi, w_fo, w_fo)

    def remote(src, dst, send, recv, device):
        return pltpu.make_async_remote_copy(src_ref=src, dst_ref=dst, send_sem=send, recv_sem=recv, device_id=device, device_id_type=MESH)

    def other_dp(step):
        return (me_dp + 1 + step) % dp

    barrier = pltpu.get_barrier_semaphore()
    many(dp - 1, lambda k: pl.semaphore_signal(barrier, inc=1, device_id=(other_dp(k), me_sq), device_id_type=MESH))
    for peer in (pair, far, cross):
        pl.semaphore_signal(barrier, inc=1, device_id=(me_dp, peer), device_id_type=MESH)
    pl.semaphore_wait(barrier, dp - 1 + 3)

    def slab_copy(src, dst_all, slab, send, recv, peer):
        return remote(src, dst_all.at[slab], send, recv.at[slab], (me_dp, peer))

    def mem_slab(slab):
        return mem_all.at[pl.ds(pl.multiple_of(slab * mem_rows, mem_rows), mem_rows)]

    def mem_copy(src, slab, send, peer):
        return remote(src, mem_slab(slab), send, mem_r.at[slab], (me_dp, peer))

    own_hidden = pltpu.make_async_copy(hidden_ref, hid_all.at[me_sq], loc_sem.at[0])
    own_memory = pltpu.make_async_copy(memory_ref, mem_slab(me_sq), loc_sem.at[1])
    hid_far = slab_copy(hidden_ref, hid_all, me_sq, hid_s.at[1], hid_r, far)
    hid_pair = slab_copy(hidden_ref, hid_all, me_sq, hid_s.at[0], hid_r, pair)
    mem_far = mem_copy(memory_ref, me_sq, mem_s.at[1], far)
    mem_pair_copy = mem_copy(memory_ref, me_sq, mem_s.at[0], pair)
    hid_next = slab_copy(hid_all.at[far], hid_all, far, hid_s.at[2], hid_r, pair)
    mem_next = mem_copy(mem_slab(far), far, mem_s.at[2], pair)

    def vec_copy(peer, slot):
        return remote(vec_ref, vec_all.at[slot], vec_s.at[peer], vec_r.at[slot], (peer, me_sq))

    def in_copy(part, peer, slot):
        return remote(
            self_in_ref.at[:, pl.ds(pl.multiple_of(part * width + me_sq * LANES, LANES), LANES)],
            w_in.at[pl.ds(pl.multiple_of(slot * strip, strip), strip), pl.ds(part * LANES, LANES)],
            in_s.at[part, peer], in_r.at[part, slot], (peer, me_sq))

    own_vec = pltpu.make_async_copy(vec_ref, vec_all.at[me_dp], loc_sem.at[2])
    own_in = [pltpu.make_async_copy(
        self_in_ref.at[:, pl.ds(pl.multiple_of(part * width + me_sq * LANES, LANES), LANES)],
        w_in.at[pl.ds(pl.multiple_of(me_dp * strip, strip), strip), pl.ds(part * LANES, LANES)],
        loc_sem.at[3 + part]) for part in range(3)]

    hid_far.start()
    hid_pair.start()
    many(dp - 1, lambda k: vec_copy(other_dp(k), me_dp).start())
    many(dp - 1, lambda k: [in_copy(part, other_dp(k), me_dp).start() for part in range(3)])
    own_hidden.start()
    own_memory.start()
    own_vec.start()
    for copy in own_in:
        copy.start()

    def half_columns(index, side):
        size = shards[index].shape[1] // 2
        return pl.ds(pl.multiple_of(side * size, LANES), size)

    def columns(index, side=None):
        side = half if side is None else side
        if index < 4:
            return half_columns(index, side)
        size = shards[index].shape[1] // 4
        part = me_sq // 2 if index == 4 else index - 5
        return pl.ds(pl.multiple_of((side * 2 + part) * size, LANES), size)

    def sent_columns(index, side):
        return half_columns(index, side) if index <= 4 else columns(index, side)

    def block_rows(index, slot):
        size = shards[index].shape[0]
        return pl.ds(pl.multiple_of(slot * size, size), size)

    def z_copy(index, peer, slot):
        return remote(shards[index].at[:, columns(index)], wholes[index].at[block_rows(index, slot * 2 + me_lo), columns(index)],
                      z_s.at[index, peer], z_r.at[index, slot], (peer * 2 + me_lo, me_sq))

    def x_copy(index, slot, low, own):
        there = wholes[index].at[block_rows(index, slot * 2 + low), columns(index)]
        src = shards[index].at[:, columns(index)] if own else there
        return remote(src, there, x_s.at[index, slot], x_r.at[index, slot], (me_hi * 2 + 1 - me_lo, me_sq))

    def c_copy(index):
        there = wholes[index].at[:, sent_columns(index, half)]
        return remote(there, there, c_s.at[index], c_r.at[index], (me_dp, pair))

    def c_wait(index):
        there = wholes[index].at[:, sent_columns(index, 1 - half)]
        remote(there, there, c_s.at[index], c_r.at[index], (me_dp, pair)).wait_recv()

    def w_copy(index, block):
        there = wholes[index].at[block_rows(index, block), columns(index)]
        return remote(there, there, w_s.at[index - 4, block], w_r.at[index - 4, block], (me_dp, far))

    def w_wait(index, block):
        size = shards[index].shape[1] // 4
        there = wholes[index].at[block_rows(index, block), pl.ds(pl.multiple_of((half * 2 + far // 2) * size, LANES), size)]
        remote(there, there, w_s.at[index - 4, block], w_r.at[index - 4, block], (me_dp, far)).wait_recv()

    def own_copy(index):
        return pltpu.make_async_copy(shards[index].at[:, columns(index)], wholes[index].at[block_rows(index, me_dp), columns(index)], loc_sem.at[6 + index])

    def other_hi(step):
        return (me_hi + 1 + step) % high

    def own_stage(index):
        x_copy(index, me_hi, me_lo, True).start()
        own_copy(index).start()

    line = high == 4

    def unless_outer(block, step):
        if line:
            pl.when((block - me_hi) * (block - me_hi) != 9)(step)
        else:
            step()

    def hop_copy(index):
        block = 3 * (2 - me_hi) % 4
        there = wholes[index].at[block_rows(index, block * 2 + me_lo), columns(index)]
        return remote(there, there, hop_s.at[index], z_r.at[index, block], ((3 - block) * 2 + me_lo, me_sq))

    def first_stage(index):
        many(high - 1, lambda k: unless_outer(other_hi(k), lambda: z_copy(index, other_hi(k), me_hi).start()))

    def arrive_high(index, block):
        z_copy(index, block, block).wait_recv()
        x_copy(index, block, me_lo, False).start()
        if index == 4:
            w_copy(index, block * 2 + me_lo).start()

    def second_stage(index):
        if index == 4:
            own_copy(index).wait()
            w_copy(index, me_dp).start()
        many(high - 1, lambda k: unless_outer(other_hi(k), lambda: arrive_high(index, other_hi(k))))
        if line:
            pl.when((me_hi == 1) | (me_hi == 2))(lambda: hop_copy(index).start())

    def late_stage(index):
        if line:
            pl.when((me_hi == 0) | (me_hi == 3))(lambda: arrive_high(index, 3 - me_hi))

    def third_stage(index):
        def arrive(k):
            x_copy(index, k, 1 - me_lo, False).wait_recv()
            if index == 4:
                w_copy(index, k * 2 + 1 - me_lo).start()
        many(high, arrive)
        if index != 4:
            own_copy(index).wait()
            c_copy(index).start()

    def fourth_stage(index):
        many(dp, lambda k: w_wait(index, k))
        c_copy(index).start()

    def finish_weight(index):
        many(high - 1, lambda k: unless_outer(other_hi(k), lambda: z_copy(index, other_hi(k), me_hi).wait_send()))
        if line:
            pl.when((me_hi == 1) | (me_hi == 2))(lambda: hop_copy(index).wait_send())
        many(high, lambda k: x_copy(index, k, me_lo, False).wait_send())
        if index == 4:
            many(dp, lambda k: w_copy(index, k).wait_send())
        c_copy(index).wait_send()

    for index in (0, 1, 2, 4, 5, 6, 3):
        own_stage(index)

    own_vec.wait()
    many(dp - 1, lambda k: vec_copy(other_dp(k), other_dp(k)).wait_recv())
    vec_full[...] = jnp.zeros_like(vec_full)
    bias_full[...] = jnp.zeros_like(bias_full)
    lane_k = lax.broadcasted_iota(i32, (LANES, width), 0)
    lane_j = lax.broadcasted_iota(i32, (LANES, width), 1)
    big = inner // dp
    piece = min(big, LANES)
    big_k = lax.broadcasted_iota(i32, (LANES, inner), 0)
    big_j = lax.broadcasted_iota(i32, (LANES, inner), 1)

    def place(slot):
        hot = ((lane_j - slot * strip == lane_k) & (lane_k < strip)).astype(f32).astype(bf16)
        vec_full[...] = vec_full[...] + nn(vec_all[slot], hot)[:8]
        for part in range(big // piece):
            wide = ((big_j - slot * big - part * piece == big_k) & (big_k < piece)).astype(f32).astype(bf16)
            bias_full[...] = bias_full[...] + nn(vec_all[slot], wide)[8 + part:9 + part]
    lax.fori_loop(0, dp, lambda slot, carry: (place(slot), carry)[1], 0)
    gain_one, shift_one = vec_full[0:1], vec_full[1:2]
    gain_two, shift_two = vec_full[2:3], vec_full[3:4]

    def norm_slab(slab):
        def step(place_rows):
            unit, _ = unit_rows(hid_all[slab, place_rows].astype(f32))
            start = pl.multiple_of(slab * rows + place_rows.start, place_rows.size)
            normed_all[pl.ds(start, place_rows.size)] = (unit * gain_one + shift_one).astype(bf16)
        tiles(rows, 256, step)

    def project_slab(slab):
        def step(place_rows):
            here = pl.ds(pl.multiple_of(slab * rows + place_rows.start, place_rows.size), place_rows.size)
            packed = nn(normed_all[here], w_in[...]).astype(bf16)
            q_all[here] = packed[:, :LANES]
            k_all[here] = packed[:, LANES:2 * LANES]
            v_all[here] = packed[:, 2 * LANES:]
        tiles(rows, 256, step)

    own_hidden.wait()
    norm_slab(me_sq)
    hid_pair_in = slab_copy(hid_all.at[pair], hid_all, pair, hid_s.at[0], hid_r, pair)
    hid_pair_in.wait_recv()
    norm_slab(pair)
    for copy in own_in:
        copy.wait()
    many(dp - 1, lambda k: [in_copy(part, other_dp(k), other_dp(k)).wait_recv() for part in range(3)])
    for index in (0, 1, 2):
        first_stage(index)
    project_slab(me_sq)
    project_slab(pair)
    slab_copy(hid_all.at[far], hid_all, far, hid_s.at[1], hid_r, far).wait_recv()
    hid_next.start()
    mem_far.start()
    mem_pair_copy.start()
    norm_slab(far)
    project_slab(far)
    slab_copy(hid_all.at[cross], hid_all, cross, hid_s.at[2], hid_r, pair).wait_recv()
    norm_slab(cross)
    project_slab(cross)

    limit = len_ref[0]
    mem_limit = mlen_ref[0]
    scale = HD ** (-0.5) * log2_e

    def softmax_block(scores, values):
        largest = jnp.max(scores, axis=1, keepdims=True)
        powers = jnp.exp2(scores - largest)
        total = jnp.sum(powers, axis=1, keepdims=True)
        return nn(powers.astype(bf16), values) / total, largest + jnp.log2(total)

    def att_copy(block, owner):
        return remote(o_heads.at[pl.ds(pl.multiple_of(block * rows, rows), rows)],
                      att_tok.at[:, pl.ds(pl.multiple_of(owner * LANES, LANES), LANES)],
                      a_s.at[block], a_r.at[owner], (me_dp, block))

    def self_block(block):
        here = pl.ds(block * rows, rows)
        query = q_all[here]
        head_queries = [pick(query, head_mask(head)) for head in range(2)]

        def key_part(index, carry, diagonal):
            there = pl.ds(pl.multiple_of(index * rows, rows), rows)
            place = index * rows + lax.broadcasted_iota(i32, (1, rows), 1)
            bias = jnp.where(place < limit, 0.0, masked_score)
            held = []
            for head in range(2):
                largest, total, out = carry[3 * head:3 * head + 3]
                scores = nt(head_queries[head], k_all[there]) * scale + bias
                if diagonal:
                    scores = jnp.where(lax.broadcasted_iota(i32, (rows, rows), 1) <= lax.broadcasted_iota(i32, (rows, rows), 0), scores, masked_score)
                higher = jnp.maximum(largest, jnp.max(scores, axis=1, keepdims=True))
                powers = jnp.exp2(scores - higher)
                shrink = jnp.exp2(largest - higher)
                total = total * shrink + jnp.sum(powers, axis=1, keepdims=True)
                held += [higher, total, out * shrink + nn(powers.astype(bf16), v_all[there])]
            return tuple(held)

        carry = (jnp.full((rows, 1), -3e38, f32), jnp.zeros((rows, 1), f32), jnp.zeros((rows, LANES), f32)) * 2
        if block:
            carry = lax.fori_loop(0, block, lambda index, held: key_part(index, held, False), carry)
        carry = key_part(block, carry, True)
        outs = [carry[3 * head + 2] / carry[3 * head + 1] for head in range(2)]
        spreads = [carry[3 * head] + jnp.log2(carry[3 * head + 1]) for head in range(2)]
        o_heads[here] = jnp.where(head_mask(0), outs[0], outs[1]).astype(bf16)
        turned = jnp.transpose(jnp.where(head_mask(0), spreads[0], spreads[1]))
        self_lse[0:1, here] = turned[0:1]
        self_lse[1:2, here] = turned[HD:HD + 1]

        @pl.when(me_sq != block)
        def _():
            att_copy(block, me_sq).start()

    def forward_memory():
        mem_copy(mem_slab(far), far, mem_s.at[1], far).wait_recv()
        mem_next.start()

    def each(stage, *indices):
        for index in indices:
            stage(index)

    comm_steps = {3: lambda: (each(second_stage, 0, 1, 2), first_stage(5)),
                  2: lambda: (forward_memory(), each(late_stage, 0, 1, 2), second_stage(4), first_stage(6)),
                  1: lambda: (late_stage(4), first_stage(3)), 0: lambda: (third_stage(0), second_stage(5))}
    first_stage(4)
    for block in range(sq - 1, -1, -1):
        self_block(block)
        comm_steps[block]()
    each(third_stage, 1, 2)
    late_stage(5)
    att_tok[:, pl.ds(pl.multiple_of(me_sq * LANES, LANES), LANES)] = o_heads[pl.ds(pl.multiple_of(me_sq * rows, rows), rows)]

    own_memory.wait()
    mem_copy(mem_slab(pair), pair, mem_s.at[0], pair).wait_recv()
    mem_copy(mem_slab(cross), cross, mem_s.at[2], pair).wait_recv()
    c_wait(0)

    def project_memory(slab, carry):
        place = pl.ds(pl.multiple_of(slab * mem_rows, mem_rows), mem_rows)
        mem_pair[place] = nn(mem_all[place], w_cm[...]).astype(bf16)
        return carry
    lax.fori_loop(0, sq, project_memory, 0)

    for peer in (pair, far, cross):
        att_copy(peer, peer).wait_recv()
    c_wait(1)
    c_wait(2)

    def step_two(here):
        value = hidden_ref[here].astype(f32) + nn(att_tok[here], w_so[...])
        after_self[here] = value
        unit, _ = unit_rows(value)
        normed = (unit * gain_two + shift_two).astype(bf16)
        normed_two[here] = normed
        cross_q[here] = nn(normed, w_cq[...]).astype(bf16)
    tiles(rows, 256, step_two)

    mem_bias = jnp.where(lax.broadcasted_iota(i32, (1, all_mem), 1) < mem_limit, 0.0, masked_score)

    def cross_pair(number, held):
        lanes = pl.ds(pl.multiple_of(number * LANES, LANES), LANES)
        value_lanes = pl.ds(pl.multiple_of(width + number * LANES, LANES), LANES)
        query = cross_q[:, lanes]
        outs, spreads = [], []
        for head in range(2):
            scores = nt(pick(query, head_mask(head)), mem_pair[:, lanes]) * scale + mem_bias
            out, spread = softmax_block(scores, mem_pair[:, value_lanes])
            outs.append(out)
            spreads.append(spread)
        mixed[:, lanes] = jnp.where(head_mask(0), outs[0], outs[1]).astype(bf16)
        turned = jnp.transpose(jnp.where(head_mask(0), spreads[0], spreads[1]))
        cross_lse[pl.ds(2 * number, 1)] = turned[0:1]
        cross_lse[pl.ds(2 * number + 1, 1)] = turned[HD:HD + 1]
        return held

    pairs = width // LANES
    each(second_stage, 6, 3)
    third_stage(4)
    lax.fori_loop(0, 1, cross_pair, 0)
    each(late_stage, 6, 3)
    third_stage(5)
    lax.fori_loop(1, 2, cross_pair, 0)
    fourth_stage(4)
    lax.fori_loop(2, 3, cross_pair, 0)
    each(third_stage, 6, 3)
    lax.fori_loop(3, pairs, cross_pair, 0)
    c_wait(3)

    def step_three(here):
        after_cross[here] = after_self[here] + nn(mixed[here], w_co[...])
    tiles(rows, 256, step_three)

    c_wait(4)
    c_wait(5)
    c_wait(6)
    gain_three, shift_three, outer_bias, exit_row = vec_full[4:5], vec_full[5:6], vec_full[6:7], vec_full[7:8]
    parts = ((g_cm, p_cm, x_cm, h_cm, f_cm, y_cm, out_cm), (g_so, p_so, x_so, h_so, f_so, y_so, out_so),
             (g_cq, p_cq, x_cq, h_cq, f_cq, y_cq, out_cq), (g_co, p_co, x_co, h_co, f_co, y_co, out_co),
             (g_fi, p_fi, x_fi, h_fi, f_fi, y_fi, out_fi), (g_fo, p_fo, x_fo, h_fo, f_fo, y_fo, out_fo))
    chunk = 512

    def norm_back(grad, unit, inverse, gain):
        scaled = grad * gain
        first = jnp.mean(scaled, axis=-1, keepdims=True)
        second = jnp.mean(scaled * unit, axis=-1, keepdims=True)
        return inverse * (scaled - first - unit * second)

    def add_sum(index, value):
        sums[index:index + 1] = sums[index:index + 1] + jnp.sum(value, axis=0, keepdims=True)

    def gc_copy(index):
        size = shards[index].shape[1] // 2
        other = pl.ds(pl.multiple_of((1 - half) * size, LANES), size)
        return remote(parts[index][0].at[:, :, :, other], parts[index][1], gc_s.at[index], gc_r.at[index], (me_dp, pair))

    def gq_copy():
        return remote(parts[5][1].at[:, :, :, part_columns(5, far // 2)], quarter_got, gq_s.at[0], gq_r.at[0], (me_dp, far))

    def ga_copy(owner, peer):
        size = shards[5].shape[1] // 4
        there = out_fo.at[:, pl.ds(pl.multiple_of((owner % 2 * 2 + owner // 2) * size, LANES), size)]
        return remote(there, there, ga_s.at[peer], ga_r.at[owner], (me_dp, peer))

    def gx_copy(index):
        src = parts[index][1].at[:, 1 - me_lo, :, part_columns(index, me_sq // 2)] if index == 5 else parts[index][1].at[:, 1 - me_lo]
        return remote(src, parts[index][2], gx_s.at[index], gx_r.at[index], (me_hi * 2 + 1 - me_lo, me_sq))

    def gz_copy(index, peer, slot):
        return remote(parts[index][2].at[peer], parts[index][3].at[slot], gz_s.at[index, peer], gz_r.at[index, slot], (peer * 2 + me_lo, me_sq))

    def gy_copy(index):
        return remote(parts[index][4], parts[index][5], gy_s.at[index], gy_r.at[index], (me_dp, far))

    def gp_copy(index, side):
        size = shards[index].shape[1] // 2
        there = parts[index][6].at[:, pl.ds(pl.multiple_of(side * size, LANES), size)]
        return remote(there, there, gp_s.at[index], gp_r.at[index], (me_dp, pair))

    def reduce_pair(index):
        gc_copy(index).start()

    def reduce_low(index):
        gc_copy(index).wait_recv()
        whole_ref, part_ref = parts[index][0], parts[index][1]

        def add(place, carry):
            for low in range(2):
                part_ref[place, low] = (part_ref[place, low].astype(f32) + whole_ref[place, low, :, half_columns(index, half)].astype(f32)).astype(bf16)
            return carry
        lax.fori_loop(0, high, add, 0)
        if index == 5:
            gq_copy().start()
        else:
            gx_copy(index).start()

    def part_columns(index, side):
        size = shards[index].shape[1] // 4
        return pl.ds(pl.multiple_of(side * size, LANES), size)

    def reduce_across(index):
        gq_copy().wait_recv()
        part_ref = parts[index][1]

        def add(place, carry):
            for low in range(2):
                mine = part_columns(index, me_sq // 2)
                part_ref[place, low, :, mine] = (part_ref[place, low, :, mine].astype(f32) + quarter_got[place, low].astype(f32)).astype(bf16)
            return carry
        lax.fori_loop(0, high, add, 0)
        gx_copy(index).start()

    def reduce_high(index):
        gx_copy(index).wait_recv()
        part_ref, low_ref = parts[index][1], parts[index][2]

        def add(place, carry):
            mine = part_ref[place, me_lo, :, part_columns(index, me_sq // 2)] if index == 5 else part_ref[place, me_lo]
            low_ref[place] = (low_ref[place].astype(f32) + mine.astype(f32)).astype(bf16)
            return carry
        lax.fori_loop(0, high, add, 0)
        many(high - 1, lambda k: gz_copy(index, other_hi(k), me_hi).start())

    def reduce_far(index):
        low_ref, high_ref, far_ref = parts[index][2], parts[index][3], parts[index][4]
        high_ref[me_hi] = low_ref[me_hi]
        many(high - 1, lambda k: gz_copy(index, other_hi(k), other_hi(k)).wait_recv())
        def add(place, held):
            return held + high_ref[place].astype(f32)
        total = lax.fori_loop(1, high, add, high_ref[0].astype(f32))
        far_ref[...] = total if index == 5 else total.astype(bf16)
        if index == 5:
            size = shards[index].shape[1] // 4
            parts[index][6][:, pl.ds(pl.multiple_of((half * 2 + me_sq // 2) * size, LANES), size)] = far_ref[...]
            for peer in (far, cross, pair):
                ga_copy(me_sq, peer).start()
        else:
            gy_copy(index).start()

    def reduce_last(index):
        far_ref, got_ref, out_ref = parts[index][4], parts[index][5], parts[index][6]
        gy_copy(index).wait_recv()
        out_ref[:, half_columns(index, half)] = far_ref[...].astype(f32) + got_ref[...].astype(f32)
        gp_copy(index, half).start()

    def reduce_end(index):
        if index == 5:
            for peer in (far, cross, pair):
                ga_copy(peer, peer).wait_recv()
        else:
            gp_copy(index, 1 - half).wait_recv()

    def reduce_drain(index):
        gc_copy(index).wait_send()
        gx_copy(index).wait_send()
        many(high - 1, lambda k: gz_copy(index, other_hi(k), me_hi).wait_send())
        if index == 5:
            gq_copy().wait_send()
            for peer in (far, cross, pair):
                ga_copy(me_sq, peer).wait_send()
        else:
            gy_copy(index).wait_send()
            gp_copy(index, half).wait_send()

    def weight_grad(index, left, rights):
        out_ref = parts[index][0]
        size = shards[index].shape[0]
        pieces = chunk // size

        def step(tile, carry):
            features = left(tile)
            for number, right in enumerate(rights):
                value = tn(features, right())
                cols = pl.ds(number * value.shape[1], value.shape[1])
                for piece in range(pieces):
                    place = tile * pieces + piece
                    out_ref[place // 2, place % 2, :, cols] = value[piece * size:(piece + 1) * size].astype(bf16)
            return carry
        lax.fori_loop(0, size * dp // chunk, step, 0)

    def feature_tile(ref):
        return lambda tile: ref[:, pl.ds(pl.multiple_of(tile * chunk, chunk), chunk)]

    hid_next.wait_send()
    for index in range(7):
        finish_weight(index)
    grad_res = grad_hidden_ref
    grad_packed, sum_in, turned_q = w_fo, after_cross, slope
    packed_cols = pl.ds(0, 3 * LANES)
    turned_rows = pl.ds(0, LANES)
    sums[...] = jnp.zeros_like(sums)
    halting_ref[...] = jnp.zeros_like(halting_ref)

    def ffn_step(here):
        size = here.size
        unit, inverse = unit_rows(after_cross[here])
        normed = (unit * gain_three + shift_three).astype(bf16)
        normed_three[here] = normed
        out = after_cross[here] + outer_bias
        for part in range(inner // chunk):
            cols = pl.ds(part * chunk, chunk)
            pre = nn(normed, w_fi[:, cols]) + bias_full[:, cols]
            square = pre * pre
            bent = jnp.tanh(gelu_scale * (pre + gelu_cubic * square * pre))
            act = (0.5 * pre * (1.0 + bent)).astype(bf16)
            active[part, here] = act
            slope[:, cols] = 0.5 * (1.0 + bent) + 0.5 * pre * (1.0 - bent * bent) * gelu_scale * (1.0 + 3.0 * gelu_cubic * square)
            out = out + nn(act, w_fo[cols])
        result_ref[here] = out.astype(bf16)
        halt = 1.0 / (1.0 + jnp.exp(-jnp.sum(out * exit_row, axis=-1, keepdims=True)))
        place = here.start + lax.broadcasted_iota(i32, (size, rows), 0)
        same = place == lax.broadcasted_iota(i32, (size, rows), 1)
        halting_ref[...] = halting_ref[...] + jnp.sum(jnp.where(same, halt, 0.0), axis=0, keepdims=True)
        halt_grad = jnp.sum(jnp.where(same, halt_grad_ref[...], 0.0), axis=1, keepdims=True)
        live = (me_sq * rows + here.start + lax.broadcasted_iota(i32, (size, 1), 0) < limit).astype(f32)
        grad_logit = halt_grad * live * halt * (1.0 - halt)
        add_sum(7, grad_logit * out)
        grad_out = grad_ref[here].astype(f32) * live + grad_logit * exit_row
        grad_branch = grad_out.astype(bf16)
        branch[here] = grad_branch
        add_sum(6, grad_branch.astype(f32))
        grad_normed = jnp.zeros((size, width), f32)
        for part in range(inner // chunk):
            cols = pl.ds(part * chunk, chunk)
            grad_part = (nt(grad_branch, w_fo[cols]) * slope[:, cols]).astype(bf16)
            grad_inner[part, here] = grad_part
            add_sum(8 + part, grad_part.astype(f32))
            grad_normed = grad_normed + nt(grad_part, w_fi[:, cols])
        add_sum(4, grad_normed * unit)
        add_sum(5, grad_normed)
        grad_cross = grad_out + norm_back(grad_normed, unit, inverse, gain_three)
        grad_res[here] = grad_cross
        grad_cross_branch = grad_cross.astype(bf16)
        cross_branch[here] = grad_cross_branch
        grad_mixed[here] = nt(grad_cross_branch, w_co[...]).astype(bf16)
    tiles(rows, 256, ffn_step)
    weight_grad(5, lambda tile: active[tile], [lambda: branch[...]])
    reduce_pair(5)
    weight_grad(4, feature_tile(normed_three), [functools.partial(lambda part: grad_inner[part], part) for part in range(inner // chunk)])
    reduce_pair(4)
    weight_grad(3, feature_tile(mixed), [lambda: cross_branch[...]])
    reduce_pair(3)

    select = (lax.broadcasted_iota(i32, (8, width), 1) // HD == lax.broadcasted_iota(i32, (8, width), 0)).astype(f32)
    cross_delta[...] = nt(select, grad_mixed[...].astype(f32) * mixed[...].astype(f32), lax.Precision.HIGHEST)
    score_scale = HD ** (-0.5)

    def attend_back(keys, values, query, grad, spread_rows, delta_rows, bias, mask):
        grad_keys, grad_values, grad_query = None, None, None
        for head in range(2):
            only = head_mask(head)
            head_keys = pick(keys, only)
            scores = nt(head_keys, query) * scale + bias
            if mask is not None:
                scores = jnp.where(mask, scores, masked_score)
            powers = jnp.exp2(scores - spread_rows[head])
            grad_powers = nt(pick(values, only), grad)
            grad_scores = (powers * (grad_powers - delta_rows[head])).astype(bf16)
            value_part = nn(powers.astype(bf16), pick(grad, only))
            key_part = nn(grad_scores, pick(query, only))
            query_part = nn(jnp.transpose(head_keys), grad_scores)
            grad_values = value_part if head == 0 else grad_values + value_part
            grad_keys = key_part if head == 0 else grad_keys + key_part
            grad_query = query_part if head == 0 else grad_query + query_part
        return grad_keys, grad_values, grad_query

    key_block = 512
    key_blocks = all_mem // key_block
    grad_pair = active
    grad_cq = branch
    grad_att = normed_three
    part_hid = hid_all
    cross_comm = {0: lambda: (reduce_low(5), reduce_low(4)), 1: lambda: reduce_low(3), 2: lambda: None, 3: lambda: None}
    def cross_back(number, held):
        lanes = pl.ds(pl.multiple_of(number * LANES, LANES), LANES)
        value_lanes = pl.ds(pl.multiple_of(width + number * LANES, LANES), LANES)

        def block_step(block, total):
            here = pl.ds(pl.multiple_of(block * key_block, key_block), key_block)
            key_place = block * key_block + lax.broadcasted_iota(i32, (key_block, 1), 0)
            grad_keys, grad_values, grad_query = attend_back(
                mem_pair[here, lanes], mem_pair[here, value_lanes], cross_q[:, lanes], grad_mixed[:, lanes],
                [cross_lse[pl.ds(2 * number + head, 1)] for head in range(2)],
                [cross_delta[pl.ds(2 * number + head, 1)] for head in range(2)],
                jnp.where(key_place < mem_limit, 0.0, masked_score), None)
            grad_pair[block, :, lanes] = (grad_keys * score_scale).astype(bf16)
            grad_pair[key_blocks + block, :, lanes] = grad_values.astype(bf16)
            return total + grad_query

        total = lax.fori_loop(0, key_blocks, block_step, jnp.zeros((LANES, rows), f32))
        grad_cq[:, lanes] = (jnp.transpose(total) * score_scale).astype(bf16)
        return held

    for number in range(pairs):
        lax.fori_loop(number, number + 1, cross_back, 0)
        cross_comm[number]()

    def step_two_back(here):
        grad_normed = nt(grad_cq[here], w_cq[...])
        unit, inverse = unit_rows(after_self[here])
        add_sum(2, grad_normed * unit)
        add_sum(3, grad_normed)
        grad_self = grad_res[here] + norm_back(grad_normed, unit, inverse, gain_two)
        grad_res[here] = grad_self
        grad_self_branch = grad_self.astype(bf16)
        cross_branch[here] = grad_self_branch
        grad_att[here] = nt(grad_self_branch, w_so[...]).astype(bf16)

    tiles(rows, 256, step_two_back)

    def da_copy(peer, owner):
        return remote(grad_att.at[:, pl.ds(pl.multiple_of(peer * LANES, LANES), LANES)],
                      grad_heads.at[pl.ds(pl.multiple_of(owner * rows, rows), rows)], da_s.at[peer], da_r.at[owner], (me_dp, peer))

    for peer in (far, cross, pair):
        da_copy(peer, me_sq).start()
    grad_heads[pl.ds(pl.multiple_of(me_sq * rows, rows), rows)] = grad_att[:, pl.ds(pl.multiple_of(me_sq * LANES, LANES), LANES)]

    def gm_copy(kind):
        source, target = ((cross, pair), (pair, pair), (far, far))[kind]
        return remote(part_mem.at[source], part_mem_got.at[kind], gm_s.at[kind], gm_r.at[kind], (me_dp, target))

    def memory_pair():
        gm_copy(0).start()
        gm_copy(1).start()

    def memory_far():
        gm_copy(0).wait_recv()
        part_mem[far] = (part_mem[far].astype(f32) + part_mem_got[0].astype(f32)).astype(bf16)
        gm_copy(2).start()

    def memory_end():
        gm_copy(1).wait_recv()
        gm_copy(2).wait_recv()
        grad_memory_ref[...] = (part_mem[me_sq].astype(f32) + part_mem_got[1].astype(f32)) + part_mem_got[2].astype(f32)

    def memory_part(slab, carry):
        per_block = key_block // mem_rows
        place = pl.ds(pl.multiple_of(slab % per_block * mem_rows, mem_rows), mem_rows)
        part_mem[slab] = (nt(grad_pair[slab // per_block, place], w_cm[:, :width])
                          + nt(grad_pair[key_blocks + slab // per_block, place], w_cm[:, width:])).astype(bf16)
        return carry

    reduce_across(5)
    reduce_high(4)
    weight_grad(0, feature_tile(mem_all), [functools.partial(lambda part: grad_pair[part * key_blocks:(part + 1) * key_blocks].reshape(all_mem, width), part) for part in range(2)])
    reduce_pair(0)
    reduce_high(3)
    weight_grad(1, feature_tile(att_tok), [lambda: cross_branch[...]])
    reduce_pair(1)
    weight_grad(2, feature_tile(normed_two), [lambda: grad_cq[...]])
    reduce_pair(2)
    lax.fori_loop(0, sq, memory_part, 0)
    memory_pair()

    def s1_copy(peer, owner):
        return remote(sums, sums_seq.at[owner], s1_s.at[peer], s1_r.at[owner], (me_dp, peer))

    for peer in (pair, far, cross):
        da_copy(peer, peer).wait_recv()
    select_two = (lax.broadcasted_iota(i32, (8, LANES), 1) // HD == lax.broadcasted_iota(i32, (8, LANES), 0)).astype(f32)
    deltas = nt(select_two, grad_heads[...].astype(f32) * o_heads[...].astype(f32), lax.Precision.HIGHEST)
    self_lse[2:4] = deltas[0:2]
    turned_q[turned_rows] = jnp.zeros((LANES, rows * sq), f32)
    half_rows = rows // 2

    def away(block):
        return me_sq // 2 != block // 2

    def away_rows(block):
        return pl.ds(block % 2 * half_rows, half_rows)

    def keep_rows(block):
        @pl.when(away(block))
        def _():
            grad_inner[0, away_rows(block)] = hid_all[block, pl.ds(pl.multiple_of(half * half_rows, half_rows), half_rows)]

    for block in range(sq):
        keep_rows(block)

    def yh_copy(block):
        there = half_got.at[block % 2]
        return remote(part_hid.at[block, pl.ds(pl.multiple_of((1 - half) * half_rows, half_rows), half_rows)], there,
                      yh_s.at[block], yh_r.at[block], (me_dp, pair))

    def yf_copy(block, side):
        return remote(part_hid.at[block, pl.ds(pl.multiple_of(half * half_rows, half_rows), half_rows)], far_got.at[pl.ds(pl.multiple_of(side * half_rows, half_rows), half_rows)],
                      yf_s.at[block], yf_r.at[side], (me_dp, block))

    def yp_copy(block):
        return remote(part_hid.at[block], pair_got, yp_s.at[0], yp_r.at[0], (me_dp, pair))

    def send_part(block):
        @pl.when(away(block))
        def _():
            yh_copy(block).start()

        @pl.when(pair == block)
        def _():
            yp_copy(block).start()

    def forward_part(block):
        @pl.when(away(block))
        def _():
            yh_copy(block).wait_recv()
            place = pl.ds(pl.multiple_of(half * half_rows, half_rows), half_rows)
            both = part_hid[block, place].astype(f32) + half_got[block % 2].astype(f32)
            part_hid[block, place] = both.astype(bf16)
            yf_copy(block, half).start()
            unit, _ = unit_rows(grad_inner[0, away_rows(block)].astype(f32))
            add_sum(0, both * unit)
            add_sum(1, both)

    schedule = {
        (0, 0): lambda: (reduce_high(5), memory_far()), (0, 1): lambda: reduce_low(0), (0, 2): lambda: (reduce_low(1), reduce_low(2)),
        (0, 3): lambda: (reduce_far(4), reduce_far(3)), (0, sq): lambda: (reduce_high(0), reduce_far(5)),
        (1, 1): lambda: forward_part(0), (1, 2): lambda: (reduce_high(1), reduce_high(2), reduce_last(4)),
        (1, sq): lambda: (reduce_far(0), reduce_last(3)), (2, 2): lambda: forward_part(1), (2, sq): lambda: (reduce_far(1), reduce_far(2)),
        (3, 3): lambda: forward_part(2), (3, sq): lambda: reduce_last(0)}

    def comm_point(block, index):
        if (block, index) in schedule:
            schedule[block, index]()

    def gi_copy(peer, slot):
        return remote(grad_in.at[peer], grad_in_got.at[slot], gi_s.at[peer], gi_r.at[slot], (peer, me_sq))

    def input_sums():
        for place in range(dp):
            grad_in[place] = sum_in[place * strip:(place + 1) * strip, packed_cols].astype(bf16)
        many(dp - 1, lambda k: gi_copy(other_dp(k), me_dp).start())

    def key_step(block):
        here = pl.ds(block * rows, rows)
        keys, values = k_all[here], v_all[here]
        bias = jnp.where(block * rows + lax.broadcasted_iota(i32, (rows, 1), 0) < limit, 0.0, masked_score)

        def query_step(index, carry, diagonal):
            def part(there, first, count, mask):
                grad_keys, grad_values, grad_query = attend_back(
                    keys[first:first + count], values[first:first + count], q_all[there], grad_heads[there],
                    [self_lse[head:head + 1, there] for head in range(2)],
                    [self_lse[2 + head:3 + head, there] for head in range(2)], bias[first:first + count], mask)
                turned_q[turned_rows, there] = turned_q[turned_rows, there] + grad_query
                return grad_keys, grad_values

            if not diagonal:
                grad_keys, grad_values = part(pl.ds(pl.multiple_of(index * rows, rows), rows), 0, rows, None)
                return carry[0] + grad_keys, carry[1] + grad_values
            both = []
            for first in (0, half_rows):
                size = rows - first
                mask = lax.broadcasted_iota(i32, (half_rows, size), 0) <= lax.broadcasted_iota(i32, (half_rows, size), 1)
                both.append(part(pl.ds(index * rows + first, size), first, half_rows, mask))
            return tuple(jnp.concatenate([both[0][item], both[1][item]], axis=0) for item in range(2))

        zero = jnp.zeros((rows, LANES), f32)
        carry = query_step(block, (zero, zero), True)
        comm_point(block, block)
        for index in range(block + 1, sq):
            carry = lax.fori_loop(index, index + 1, lambda place, held: query_step(place, held, False), carry)
            comm_point(block, index)
        grad_packed[here, pl.ds(LANES, LANES)] = (carry[0] * score_scale).astype(bf16)
        grad_packed[here, pl.ds(2 * LANES, LANES)] = carry[1].astype(bf16)
        grad_packed[here, pl.ds(0, LANES)] = (jnp.transpose(turned_q[turned_rows, here]) * score_scale).astype(bf16)

        def input_part(tile, held):
            cols = pl.ds(pl.multiple_of(tile * 256, 256), 256)
            value = tn(normed_all[here, cols], grad_packed[here, packed_cols])
            if block == 0:
                sum_in[cols, packed_cols] = value
            else:
                sum_in[cols, packed_cols] = sum_in[cols, packed_cols] + value
            return held
        lax.fori_loop(0, width // 256, input_part, 0)
        if block == sq - 1:
            input_sums()

        def hidden_part(place):
            rows_here = pl.ds(pl.multiple_of(block * rows + place.start, place.size), place.size)
            part_hid[block, place] = nt(grad_packed[rows_here, packed_cols], w_in[...]).astype(bf16)
        tiles(rows, 256, hidden_part)
        send_part(block)

    for block in range(sq):
        key_step(block)
        comm_point(block, sq)
    grad_in_got[me_dp] = grad_in[me_dp]
    forward_part(sq - 1)
    yp_copy(me_sq).wait_recv()

    def own_sums(here):
        grad_normed = part_hid[me_sq, here].astype(f32) + pair_got[here].astype(f32)
        unit, _ = unit_rows(hidden_ref[here].astype(f32))
        add_sum(0, grad_normed * unit)
        add_sum(1, grad_normed)
    tiles(rows, 256, own_sums)
    for peer in (far, cross, pair):
        s1_copy(peer, me_sq).start()

    memory_end()
    reduce_last(1)
    reduce_last(2)

    for peer in (far, cross, pair):
        s1_copy(peer, peer).wait_recv()
    sums_seq[me_sq] = sums[...]
    last_sums[...] = (sums_seq[0] + sums_seq[1]) + (sums_seq[2] + sums_seq[3])

    lanes_two = max(LANES, big)

    def v_blocks(peer):
        return (last_sums.at[pl.ds(0, 8), pl.ds(pl.multiple_of(peer * strip // LANES * LANES, LANES), LANES)],
                last_sums.at[pl.ds(8, 8), pl.ds(pl.multiple_of(peer * big % width // lanes_two * lanes_two, LANES), lanes_two)])

    def v_copy(peer, slot):
        one, two = v_blocks(peer)
        return (remote(one, vec_got.at[slot], s2_s.at[0, peer], s2_r.at[0, slot], (peer, me_sq)),
                remote(two, bias_got.at[slot], s2_s.at[1, peer], s2_r.at[1, slot], (peer, me_sq)))
    many(dp - 1, lambda k: [copy.start() for copy in v_copy(other_dp(k), me_dp)])
    one, two = v_blocks(me_dp)
    vec_got[me_dp] = one[...]
    bias_got[me_dp] = two[...]
    many(dp - 1, lambda k: gi_copy(other_dp(k), other_dp(k)).wait_recv())
    total_in = grad_in_got[0].astype(f32)
    for place in range(1, dp):
        total_in = total_in + grad_in_got[place].astype(f32)

    def go_copy(owner, peer):
        return remote(last_in.at[owner], last_in.at[owner], go_s.at[0, peer], go_r.at[0, owner], (me_dp, peer))
    last_in[me_sq] = total_in.astype(bf16)
    for peer in (far, cross, pair):
        go_copy(me_sq, peer).start()
    yf_copy(me_sq, 0).wait_recv()
    yf_copy(me_sq, 1).wait_recv()

    def last_step(here):
        grad_normed = part_hid[me_sq, here].astype(f32) + pair_got[here].astype(f32) + far_got[here].astype(f32)
        unit, inverse = unit_rows(hidden_ref[here].astype(f32))
        grad_hidden_ref[here] = grad_res[here] + norm_back(grad_normed, unit, inverse, gain_one)
    tiles(rows, 256, last_step)
    many(dp - 1, lambda k: [copy.wait_recv() for copy in v_copy(other_dp(k), other_dp(k))])
    out_vec[...] = vec_got[0]
    out_bias[...] = bias_got[0]

    def add_vec(place, carry):
        out_vec[...] = out_vec[...] + vec_got[place]
        out_bias[...] = out_bias[...] + bias_got[place]
        return carry
    lax.fori_loop(1, dp, add_vec, 0)
    for index in range(6):
        reduce_end(index)
    for peer in (far, cross, pair):
        go_copy(peer, peer).wait_recv()
    for owner in range(sq):
        for part in range(3):
            out_si[:, part * width + owner * LANES:part * width + (owner + 1) * LANES] = last_in[owner, :, part * LANES:(part + 1) * LANES].astype(f32)
    for index in range(6):
        reduce_drain(index)
    for peer in (far, cross, pair):
        da_copy(peer, me_sq).wait_send()
        s1_copy(peer, me_sq).wait_send()
        go_copy(me_sq, peer).wait_send()
    many(dp - 1, lambda k: gi_copy(other_dp(k), me_dp).wait_send())
    many(dp - 1, lambda k: [copy.wait_send() for copy in v_copy(other_dp(k), me_dp)])
    for kind in range(3):
        gm_copy(kind).wait_send()
    yp_copy(pair).wait_send()
    for block in range(sq):
        @pl.when(away(block))
        def _():
            yh_copy(block).wait_send()
            yf_copy(block, half).wait_send()
    for copy in (hid_far, hid_pair, mem_far, mem_pair_copy, mem_next):
        copy.wait_send()
    many(dp - 1, lambda k: vec_copy(other_dp(k), me_dp).wait_send())
    many(dp - 1, lambda k: [in_copy(part, other_dp(k), me_dp).wait_send() for part in range(3)])
    for peer in (pair, far, cross):
        att_copy(peer, me_sq).wait_send()


def whole_specs(names):
    return [pl.BlockSpec(memory_space=name) for name in names]


def run_layer(sizes, args):
    dp, sq, rows, mem_rows, width, inner = sizes
    seq_rows, all_mem = rows * sq, mem_rows * sq
    high, strip, big = dp // 2, width // dp, inner // dp
    V, A, S = pltpu.VMEM, pl.ANY, pltpu.SMEM
    dma = pltpu.SemaphoreType.DMA
    shard_shapes = [(strip, 2 * width), (strip, width), (strip, width), (strip, width), (strip, inner), (big, width)]
    outs = [((rows, width), bf16), ((1, rows), f32), ((rows, width), f32), ((mem_rows, width), f32),
            ((strip, 3 * width), f32)] + [(shape, f32) for shape in shard_shapes] + [((8, LANES), f32), ((8, max(LANES, big)), f32)]
    scratch = [((width, 2 * width), bf16), ((width, width), bf16), ((width, width), bf16), ((width, width), bf16),
               ((width, inner), bf16), ((inner, width), bf16), ((8, width), f32), ((1, inner), f32),
               ((rows, width), f32), ((rows, width), f32), ((rows, width), bf16), ((rows, width), bf16),
               ((rows, width), bf16), ((all_mem, 2 * width), bf16), ((8, rows), f32), ((rows, width), bf16),
               ((seq_rows, LANES), bf16), ((seq_rows, LANES), bf16), ((seq_rows, LANES), bf16), ((8, seq_rows), f32),
               ((width, 3 * LANES), bf16), ((sq, rows, width), bf16), ((all_mem, width), bf16),
               ((dp, 16, LANES), bf16), ((seq_rows, width), bf16), ((seq_rows, LANES), bf16),
               ((rows, width), bf16), ((inner // 512, rows, 512), bf16), ((inner // 512, rows, 512), bf16), ((256, inner), f32),
               ((rows, width), bf16), ((rows, width), bf16), ((rows, width), bf16), ((8, rows), f32),
               ((seq_rows, LANES), bf16),
               ((dp, strip, 3 * LANES), bf16), ((dp, strip, 3 * LANES), bf16),
               ((sq, mem_rows, width), bf16), ((3, mem_rows, width), bf16),
               ((2, rows // 2, width), bf16), ((rows, width), bf16), ((rows, width), bf16),
               ((16, width), f32), ((sq, 16, width), f32), ((16, width), f32), ((dp, 8, LANES), f32), ((dp, 8, max(LANES, big)), f32),
               ((high, 2, big, width // 4), bf16), ((sq, strip, 3 * LANES), bf16)]
    scratch += [((high, 2, size, columns), bf16) for size, columns in shard_shapes]
    scratch += [((high, 2, size, columns // 2), bf16) for size, columns in shard_shapes]
    ways = [2] * 5 + [4]
    scratch += [((high, size, columns // way), bf16) for (size, columns), way in zip(shard_shapes, ways)] * 2
    scratch += [((size, columns // 2), bf16) for size, columns in shard_shapes[:5]] + [((big, width // 4), f32)]
    scratch += [((size, columns // 2), bf16) for size, columns in shard_shapes[:5]] + [((8, LANES), f32)]
    semaphores = [dma((13,)), dma((3,)), dma((sq,)), dma((3,)), dma((sq,)), dma((dp,)), dma((dp,)), dma((3, dp)), dma((3, dp)),
                  dma((7, high)), dma((7, high)), dma((7, high)), dma((7, high)), dma((7,)), dma((7,)), dma((sq,)), dma((sq,)),
                  dma((6,)), dma((6,)), dma((6,)), dma((6,)), dma((6, high)), dma((6, high)), dma((6,)), dma((6,)), dma((6,)), dma((6,)),
                  dma((dp,)), dma((dp,)), dma((3, sq)), dma((3, sq)), dma((sq,)), dma((sq,)), dma((sq,)), dma((sq,)),
                  dma((7,)), dma((1, dp)), dma((1, dp)), dma((1,)), dma((1,)), dma((sq,)), dma((sq,)),
                  dma((sq,)), dma((sq,)), dma((sq,)), dma((2,)), dma((1,)), dma((1,)),
                  dma((sq,)), dma((sq,)), dma((2, dp)), dma((2, dp))]
    return pl.pallas_call(
        functools.partial(layer_kernel, sizes),
        out_shape=[jax.ShapeDtypeStruct(*out) for out in outs],
        in_specs=whole_specs([S, S, V, V, V, V, V, A, A, A, A, A, A, A]),
        out_specs=whole_specs([V] * len(outs)),
        scratch_shapes=[pltpu.VMEM(*item) for item in scratch] + semaphores,
        compiler_params=pltpu.CompilerParams(collective_id=0, has_side_effects=True, vmem_limit_bytes=62 << 20),
        name="layer",
    )(*args)


def finish_kernel(count, strip, big, width, *refs):
    sources, (vec_ref, bias_ref) = refs[:count], refs[count:count + 2]
    targets, vectors, bias_out = refs[count + 2:2 * count + 2], refs[2 * count + 2:2 * count + 10], refs[2 * count + 10]
    held, (sem_in, sem_out) = refs[2 * count + 11:-2], refs[-2:]
    loads, copies = [], []
    for index in range(count):
        size = sources[index].shape[0]
        pieces = 4 if size >= 64 else 1
        for piece in range(pieces):
            part = pl.ds(piece * (size // pieces), size // pieces)
            loads.append(pltpu.make_async_copy(sources[index].at[part], held[index].at[part], sem_in.at[index, piece]))
            copies.append(pltpu.make_async_copy(held[index].at[part], targets[index].at[part], sem_out.at[index, piece]))
    for load in loads:
        load.start()
    for load, copy in zip(loads, copies):
        load.wait()
        copy.start()
    place = lax.axis_index("dp")
    turned = pltpu.roll(vec_ref[...], (LANES - place * strip % LANES) % LANES, 1)
    for row in range(8):
        vectors[row][...] = turned[row, :strip]
    span = bias_ref.shape[1]
    chosen = lax.broadcasted_iota(i32, (8, span), 0) == place * big // width
    line = jnp.sum(jnp.where(chosen, bias_ref[...], 0.0), axis=0, keepdims=True)
    lines = pltpu.roll(jnp.broadcast_to(line, (8, span)), (span - place * big % span) % span, 1)
    bias_out[...] = lines[0, :big]
    for copy in copies:
        copy.wait()


def run_finish(strip, big, width, arrays, vec, bias):
    count = len(arrays)
    V, A = pltpu.VMEM, pl.ANY
    shapes = [jax.ShapeDtypeStruct(array.shape, array.dtype) for array in arrays]
    shapes += [jax.ShapeDtypeStruct((strip,), f32)] * 8 + [jax.ShapeDtypeStruct((big,), f32)]
    return pl.pallas_call(
        functools.partial(finish_kernel, count, strip, big, width),
        out_shape=shapes,
        in_specs=whole_specs([A] * count + [V, V]),
        out_specs=whole_specs([A] * count + [V] * 9),
        scratch_shapes=[pltpu.VMEM(array.shape, array.dtype) for array in arrays] + [pltpu.SemaphoreType.DMA((count, 4))] * 2,
        name="finish",
    )(*arrays, vec, bias)


def shards(hidden_in, memory, lengths, memory_lengths, self_in, self_out, cross_query, cross_memory, cross_out,
           ffn_in, ffn_bias, ffn_out, out_bias, gain_self, shift_self, gain_cross, shift_cross, gain_ffn, shift_ffn,
           exit_weight, grad_result, grad_halting):
    dp = lax.axis_size("dp")
    sq = lax.axis_size("seq")
    rows, width = hidden_in.shape
    mem_rows = memory.shape[0]
    inner = ffn_in.shape[1]
    sizes = (dp, sq, rows, mem_rows, width, inner)
    strip = width // dp
    big = inner // dp
    piece = min(big, LANES)
    vectors = jnp.stack([gain_self, shift_self, gain_cross, shift_cross, gain_ffn, shift_ffn, out_bias, exit_weight])
    packed_vec = jnp.concatenate([
        jnp.pad(vectors, ((0, 0), (0, LANES - strip))),
        jnp.pad(ffn_bias.reshape(big // piece, piece), ((0, 8 - big // piece), (0, LANES - piece)))])
    outs = run_layer(
        sizes, (lengths, memory_lengths, hidden_in, memory, packed_vec, grad_result, grad_halting.reshape(1, rows), self_in,
                cross_memory, self_out, cross_query, cross_out, ffn_in, ffn_out))
    finished = run_finish(strip, big, width, outs[:11], outs[11], outs[12])
    (result, halting, grad_hidden, grad_memory, out_si, out_cm, out_so, out_cq, out_co, out_fi, out_fo) = finished[:11]
    small, grad_bias = finished[11:19], finished[19]
    return (result, halting.reshape(rows), grad_hidden, grad_memory, out_si, out_so, out_cq, out_cm, out_co, out_fi,
            grad_bias, out_fo, small[6], small[0], small[1], small[2], small[3], small[4], small[5], small[7])


def solution(mesh):
    both = P(("dp", "seq"), None)
    matrix = P("dp", None)
    vector = P("dp")
    return jax.shard_map(
        shards,
        mesh=mesh,
        in_specs=(both, both, vector, vector, matrix, matrix, matrix, matrix, matrix, matrix, vector, matrix)
        + (vector,) * 8 + (both, P(("dp", "seq"))),
        out_specs=(both, P(("dp", "seq")), both, both) + (matrix,) * 6 + (vector, matrix) + (vector,) * 8,
        check_vma=False,
    )
```
